512 devices in a mesh: dp: 64 (over z, x_hi, core), mp: 8 (over x_lo, y).
Axes of the slice: x: 4 (x_hi: 2, x_lo: 2; x = x_hi * 2 + x_lo), y: 4, z: 16, core: 2. Of those that a mesh axis runs over, the one named last changes fastest.
Arguments:
- queries: bfloat16 [65536, 256], P('dp'), may hold values from -1400 to 1400, as said below
- item_table: bfloat16 [32768, 512], P('dp'), may hold values from -6 to 6
- cand_row: int32 [4096], P('dp'), may hold values from 0 to 511
- cand_owner: int32 [4096, 1], P('dp'), may hold values from 0 to 63; in each aligned block of 64 rows (0 to 63, 64 to 127, ...) at most 2 rows name the same one
- cand_count: int32 [4096], P('dp'), may hold values from 1 to 100
- positive: int32 [65536], P('dp'), may hold values from 0 to 4095
- w_in: bfloat16 [512, 1024], P(None, 'mp'), may hold values from -0.25 to 0.25
- b_in: float32 [1024], P('mp'), may hold values from -3 to 3
- w_out: bfloat16 [1024, 256], P('mp'), may hold values from -0.1875 to 0.1875
Outputs:
- loss: float32 [65536], P('dp')
- query_grad: float32 [65536, 256], P(('dp', 'mp'))
- grad_w_in: float32 [512, 1024], P(None, 'mp')
- grad_b_in: float32 [1024], P('mp')
- grad_w_out: float32 [1024, 256], P('mp')
- grad_table: float32 [32768, 512], P('dp')
The draws below stay inside these ranges and needn't reach their ends.
Inputs may be any that keep to these rules, and one draw needn't show every extreme that they name: `cand_owner`: no owner is named by more than 2 of the candidates of one index of dp; in some index of dp one owner is named by exactly 2. `queries`: query vectors are finite.
All inputs are finite; a program needn't handle non-finite values.
Results may differ from the reference program's by a relative error of at most 0.01.
Values may be sent and summed in bfloat16 or wider, within the bound.
A program may use at most 64 MiB of HBM per device.

```python
import math
import jax
import jax.numpy as jnp
import numpy as np
from jax import lax

EMB = 512
HID = 1024
OUT = 256
ROWS_DEV = 512
NCAND = 4096
QUERIES = 65536
ROWS = 32768
CAND_DP = 64
CAP = 2
N_DP = 64


def draw_queries(key, part):
    first = jax.random.fold_in(key, 0)
    return jax.random.normal(first, (QUERIES, OUT), jnp.float32).astype(jnp.bfloat16)


def plant(result, key, low, top_value):
    shape = result.shape
    spot = [jax.random.randint(jax.random.fold_in(key, axis), (), 0, shape[axis]) for axis in range(len(shape))]
    result = result.at[tuple(spot)].set(low)
    longest = shape.index(max(shape))
    spot[longest] = (spot[longest] + 1) % shape[longest]
    return result.at[tuple(spot)].set(top_value)


def steps_of(own_key, shape, cuts, least, top_value):
    gain = 1.0
    for dim, parts in cuts:
        heights = jax.random.uniform(jax.random.fold_in(jax.random.fold_in(own_key, 6), dim), (parts,), jnp.float32, least / len(cuts), top_value / len(cuts))
        gain = gain * jnp.repeat(jnp.exp(heights), shape[dim] // parts).reshape((-1,) + (1,) * (len(shape) - 1 - dim))
    return gain


def shared_out(key, own, number, rows, number_of, top, limit, slope):
    sequence = jax.random.permutation(key, number_of)
    heavy_load, common = load_shares(number_of, rows * top, limit, slope, True), load_shares(number_of, rows * top, limit, slope, False)
    places = jnp.arange(number_of)

    def named(lengths, turn):
        used = int((lengths > 0).sum())
        fixed = max(1, used // 4)
        passed = fixed + (places - fixed + turn * (used - fixed)) % max(1, number_of - fixed)
        return jnp.zeros((number_of,), jnp.int32).at[sequence[jnp.where(places < fixed, places, passed)]].set(jnp.asarray(lengths, jnp.int32))

    lengths = jnp.where(number % 4 == 0, named(heavy_load, number // 4), named(common, number - number // 4 - 1))
    mixed = jax.random.permutation(jax.random.fold_in(own, 3), number_of)
    donor, sink = mixed[0:number_of // 2 * 2:2], mixed[1:number_of // 2 * 2:2]
    margin = jnp.minimum(lengths[donor] - 1, limit - lengths[sink]) // 2
    margin = jnp.where((donor == sequence[0]) | (sink == sequence[0]) | (lengths[sink] == 0), 0, jnp.maximum(margin, 0))
    passed = jax.random.randint(jax.random.fold_in(own, 4), (number_of // 2,), 0, 1 << 20) % (margin + 1)
    lengths = lengths.at[donor].add(-passed).at[sink].add(passed)
    labels = jnp.searchsorted(jnp.cumsum(lengths), jnp.arange(rows * top), side="right").astype(jnp.int32)
    listing = labels.reshape(top, rows).T
    listing = listing[jax.random.permutation(jax.random.fold_in(own, 1), rows)]
    turn = jax.random.randint(jax.random.fold_in(own, 2), (rows, 1), 0, top)
    return jnp.take_along_axis(listing, (jnp.arange(top)[None, :] + turn) % top, axis=1)


def load_shares(count, total, limit, lean, full):
    portions = [(1 << 20) // math.isqrt(standing ** lean) + 1 for standing in range(1, count + 1)]
    largest = limit if full else min(limit, max(-(-total // count), total * portions[0] // sum(portions)))
    least = 1 if total - largest >= count - 1 else 0
    counts, rest = [largest] + [least] * (count - 1), total - largest - least * (count - 1)
    while rest > 0:
        free = [i for i in range(1, count) if counts[i] < largest] or [i for i in range(1, count) if counts[i] < limit]
        pool, left = sum([portions[i] for i in free]), rest
        for i in free:
            more = min(limit - counts[i], max(1, left * portions[i] // pool), rest)
            counts[i] = counts[i] + more
            rest = rest - more
    return np.array(counts)


def centred(key, dims, spread, most, cuts=(), held_as=jnp.bfloat16):
    drawn = spread * jax.random.normal(key, dims, jnp.float32)
    if cuts:
        drawn = drawn * steps_of(key, dims, cuts, -0.22, 0.18)
    return jnp.clip(drawn, -most, most).astype(held_as)


def setup_inputs(seed: int = 0) -> dict:
    streams_of = jax.random.split(jax.random.key(seed), 10)
    queries = draw_queries(jax.random.fold_in(streams_of[9], 71), 0)
    item_table = centred(streams_of[1], (ROWS, EMB), 1.0, 6.0, ((0, 64),))
    cand_row = plant(jax.random.randint(streams_of[2], (NCAND,), 0, ROWS_DEV), jax.random.fold_in(streams_of[2], 1), 0, ROWS_DEV - 1).astype(jnp.int32)
    cand_owner_keys = jax.random.split(jax.random.fold_in(streams_of[3], 1), NCAND // CAND_DP)
    cand_owner_turns = jax.random.permutation(jax.random.fold_in(streams_of[3], 3), NCAND // CAND_DP)
    cand_owner = jax.vmap(lambda own, number: shared_out(jax.random.fold_in(streams_of[3], 2), own, number, CAND_DP, N_DP, 1, CAP, 1))(cand_owner_keys, cand_owner_turns).reshape((NCAND, 1))
    cand_count = plant(jax.random.randint(streams_of[4], (NCAND,), 1, 101), jax.random.fold_in(streams_of[4], 1), 1, 100).astype(jnp.int32)
    positive = plant(jax.random.randint(streams_of[5], (QUERIES,), 0, NCAND), jax.random.fold_in(streams_of[5], 1), 0, NCAND - 1).astype(jnp.int32)
    w_in = centred(streams_of[6], (EMB, HID), EMB ** -0.5, 0.25, ((1, 8),))
    b_in = centred(streams_of[7], (HID,), 0.5, 3.0, ((0, 8),), jnp.float32)
    w_out = centred(streams_of[8], (HID, OUT), HID ** -0.5, 0.1875, ((0, 8),))
    return {"queries": queries, "item_table": item_table, "cand_row": cand_row, "cand_owner": cand_owner, "cand_count": cand_count, "positive": positive, "w_in": w_in, "b_in": b_in, "w_out": w_out}


def reference(queries, item_table, cand_row, cand_owner, cand_count, positive, w_in, b_in, w_out):
    ids = (cand_owner[:, 0] * ROWS_DEV + cand_row).astype(jnp.int32)
    emb = jnp.take(item_table, ids, axis=0)
    pre = jnp.dot(emb, w_in, preferred_element_type=jnp.float32) + b_in
    hidden = jnp.maximum(pre, 0.0).astype(jnp.bfloat16)
    items = jnp.dot(hidden, w_out, preferred_element_type=jnp.float32).astype(jnp.bfloat16)
    logq = jnp.log(cand_count.astype(jnp.float32))
    scale = 1.0 / math.sqrt(OUT)
    block = math.gcd(QUERIES, 4096)
    nblocks = QUERIES // block
    columns = jnp.arange(NCAND).astype(jnp.int32)

    def step(carry, pieces):
        qblock, pblock = pieces
        scores = jnp.dot(qblock, items.T, preferred_element_type=jnp.float32) * scale - logq[None, :]
        top = lax.optimization_barrier(jnp.max(scores, axis=1, keepdims=True))
        lse = top[:, 0] + jnp.log(lax.optimization_barrier(jnp.sum(jnp.exp(scores - top), axis=1)))
        onehot = pblock[:, None] == columns[None, :]
        pos = lax.optimization_barrier(jnp.sum(jnp.where(onehot, scores, 0.0), axis=1))
        probgrad = (jnp.exp(scores - lse[:, None]) - onehot.astype(jnp.float32)).astype(jnp.bfloat16)
        qgrad = jnp.dot(probgrad, items, preferred_element_type=jnp.float32) * scale
        carry = carry + jnp.dot(probgrad.T, qblock, preferred_element_type=jnp.float32) * scale
        return (carry, (lse - pos, qgrad))
    start = jnp.zeros((NCAND, OUT), jnp.float32)
    total, outs = lax.scan(step, start, (queries.reshape(nblocks, block, OUT), positive.reshape(nblocks, block)))
    loss = outs[0].reshape(QUERIES)
    query_grad = outs[1].reshape(QUERIES, OUT)
    item_grad = total.astype(jnp.bfloat16)
    grad_w_out = jnp.dot(hidden.T, item_grad, preferred_element_type=jnp.float32)
    back = jnp.dot(item_grad, w_out.T, preferred_element_type=jnp.float32)
    pre_grad = jnp.where(pre > 0.0, back, 0.0).astype(jnp.bfloat16)
    grad_w_in = jnp.dot(emb.T, pre_grad, preferred_element_type=jnp.float32)
    grad_b_in = lax.optimization_barrier(jnp.sum(pre_grad.astype(jnp.float32), axis=0))
    emb_grad = jnp.dot(pre_grad, w_in.T, preferred_element_type=jnp.float32).astype(jnp.bfloat16)
    grad_table = jnp.zeros((ROWS, EMB), jnp.float32).at[ids].add(emb_grad.astype(jnp.float32))
    return (loss, query_grad, grad_w_in, grad_b_in, grad_w_out, grad_table)
```

```python
import functools
import math

import jax
import jax.numpy as jnp
from jax import lax
from jax.experimental import pallas as pl
from jax.experimental.pallas import tpu as pltpu
from jax.sharding import PartitionSpec as P

MESH = pl.DeviceIdType.MESH
F32 = jnp.float32
BF16 = jnp.bfloat16
GRP = 4
QT = 256


def dot(a, b, ca, cb):
    return lax.dot_general(a, b, (((ca,), (cb,)), ((), ())), preferred_element_type=F32)


def drain(ref, sem):
    pltpu.make_async_copy(ref, ref, sem).wait()


def step_kernel(n_dp, n_mp, names, *refs):
    r = dict(zip(names, refs))
    nz = n_dp // GRP
    dp, mp = lax.axis_index("dp"), lax.axis_index("mp")
    z, g = lax.div(dp, GRP), lax.rem(dp, GRP)
    core, x_hi = lax.rem(g, 2), lax.div(g, 2)
    gc = x_hi * 2 + (1 - core)
    gx = lax.rem(g + 2, GRP)
    to_core, to_x = (z * GRP + gc, mp), (z * GRP + gx, mp)
    cl = r["own_col"].shape[0]
    slots = 2 * n_dp
    sm = slots // n_mp
    srcs = n_dp // n_mp
    nc = srcs * cl
    ns = n_dp * sm
    emb_w = r["table"].shape[1]
    out_w = r["q"].shape[1]
    nq = r["q"].shape[0]
    scale = 1.0 / math.sqrt(out_w)
    qb = nq // n_mp

    def near(i):
        odd = lax.rem(i, 2)
        return odd * lax.div(i + 1, 2) + (1 - odd) * lax.rem(nz - lax.div(i, 2), nz)

    def zplus(k):
        return lax.rem(z + k, nz)

    def zminus(k):
        return lax.rem(z + nz - k, nz)

    def send(src, dst, ssem, rsem, dev):
        pltpu.make_async_remote_copy(
            src_ref=src, dst_ref=dst, send_sem=ssem, recv_sem=rsem, device_id=dev, device_id_type=MESH
        ).start()

    def loop(lo, hi, body):
        def step(i, c):
            body(i)
            return c

        lax.fori_loop(lo, hi, step, 0)

    barrier = pltpu.get_barrier_semaphore()

    def greet(dev):
        pl.semaphore_signal(barrier, inc=1, device_id=dev, device_id_type=MESH)

    loop(0, nz - 1, lambda i: greet((zplus(near(nz - 1 - i)) * GRP + g, mp)))
    for j in range(1, GRP):
        greet((z * GRP + lax.rem(g + j, GRP), mp))
    for j in range(1, n_mp):
        greet((dp, lax.rem(mp + j, n_mp)))

    cand = r["cand"]
    lane = lax.broadcasted_iota(jnp.int32, (n_dp, 128), 1)
    sub = lax.broadcasted_iota(jnp.int32, (n_dp, 128), 0)
    owner = cand[0:1, :]
    earlier = (r["own_col"][...] == owner) & (
        lax.broadcasted_iota(jnp.int32, (cl, 128), 0) < lax.broadcasted_iota(jnp.int32, (cl, 128), 1)
    )
    rank = jnp.sum(jnp.where(earlier, 1.0, 0.0), axis=0, keepdims=True)
    owner_of = (sub & (nz - 1)) * GRP + lax.shift_right_logical(sub, int(math.log2(nz)))
    mine = owner_of == owner
    row1 = cand[1:2, :].astype(F32) + 1.0
    first = jnp.sum(jnp.where(mine & (rank < 0.5), row1, 0.0), axis=1, keepdims=True)
    second = jnp.sum(jnp.where(mine & (rank > 0.5), row1, 0.0), axis=1, keepdims=True)
    asked = jnp.where(lane == 2 * dp, first, jnp.where(lane == 2 * dp + 1, second, 0.0))
    for j in range(GRP):
        r["r1s"][j] = asked[j * nz : (j + 1) * nz]
    r["r1r"][pl.ds(g, 1)] = r["r1s"][pl.ds(g, 1)]
    code = (
        ((owner & (GRP - 1)) * nz + lax.shift_right_logical(owner, 2)) * sm + lax.rem(dp, srcs) * 2
    ).astype(F32) + rank
    info = jnp.where(lax.broadcasted_iota(jnp.int32, (1, 128), 1) < 64, code, cand[2:3, :].astype(F32))
    r["i1"][...] = info
    r["infoz"][pl.ds(z, 1), pl.ds(g, 1)] = info[None, None]

    pl.semaphore_wait(barrier, nz - 1 + GRP - 1 + n_mp - 1)

    for j in range(1, GRP):
        gd = lax.rem(g + j, GRP)
        send(r["r1s"].at[gd], r["r1r"].at[g], r["ss"].at[0], r["rs"].at[0], (z * GRP + gd, mp))
    for j in range(1, GRP):
        gd = lax.rem(g + j, GRP)
        send(r["i1"], r["infoz"].at[z, g], r["ss"].at[1], r["rs"].at[1], (z * GRP + gd, mp))
    drain(r["r1r"].at[pl.ds(0, GRP - 1)], r["rs"].at[0])
    asked4 = r["r1r"][0] + r["r1r"][1] + r["r1r"][2] + r["r1r"][3]
    for i in range(nz):
        r["s2"][i] = asked4[i : i + 1, :]
    r["rq"][pl.ds(z, 1)] = r["s2"][pl.ds(z, 1)]

    def ask(i):
        zd = zplus(near(nz - 1 - i))
        send(r["s2"].at[zd], r["rq"].at[z], r["ss"].at[2], r["rs"].at[2], (zd * GRP + g, mp))

    loop(0, nz - 1, ask)
    drain(r["infoz"].at[0, pl.ds(0, GRP - 1)], r["rs"].at[1])

    def tell(i):
        zd = zplus(near(nz - 1 - i))
        send(r["infoz"].at[z], r["infoz"].at[z], r["ss"].at[3], r["rs"].at[3], (zd * GRP + g, mp))

    loop(0, nz - 1, tell)
    drain(r["rq"].at[pl.ds(0, nz - 1)], r["rs"].at[2])

    asked_row = r["rq"][0]
    for i in range(1, nz):
        asked_row = asked_row + r["rq"][i]
    rows_dev = r["table"].shape[0]
    hits = lax.broadcasted_iota(jnp.int32, (rows_dev, 128), 0).astype(F32) + 1.0 == asked_row
    r["ht"][...] = jnp.where(hits, 1.0, 0.0).astype(BF16)
    emb = dot(r["ht"][...], r["table"][...], 0, 0)[:slots].astype(BF16)
    r["emb"][...] = emb
    pre = dot(emb, r["w_in"][...], 1, 0) + r["b_in"][...]
    r["pre"][...] = pre
    hidden = jnp.maximum(pre, 0.0).astype(BF16)
    r["hid"][...] = hidden
    item_p = dot(hidden, r["w_out"][...], 1, 0)
    for j in range(n_mp):
        r["bs"][j] = item_p[j * sm : (j + 1) * sm]
    r["br"][pl.ds(mp, 1)] = r["bs"][pl.ds(mp, 1)]
    for j in range(1, n_mp):
        md = lax.rem(mp + j, n_mp)
        send(r["bs"].at[md], r["br"].at[mp], r["ss"].at[4], r["rs"].at[4], (dp, md))
    drain(r["br"].at[pl.ds(0, n_mp - 1)], r["rs"].at[4])
    item_own = r["br"][0]
    for j in range(1, n_mp):
        item_own = item_own + r["br"][j]
    r["ag"][pl.ds(g * nz + z, 1)] = item_own.astype(BF16)[None]

    def ag_start(buf, ss, rz):
        own = g * nz + z

        def go(i):
            k = near(nz - 1 - i)
            send(buf.at[own], buf.at[own], r["ss"].at[ss], rz.at[k], (zplus(k) * GRP + g, mp))

        loop(0, nz - 1, go)

    def ag_finish(buf, ss, rs, rz, rx):
        own = g * nz + z

        def pass_on(k, b):
            send(buf.at[b], buf.at[b], r["ss"].at[ss + 1], rx.at[k], to_x)
            send(buf.at[b], buf.at[b], r["ss"].at[ss + 2], r["rs"].at[rs], to_core)

        pass_on(0, own)

        def relay(i):
            k = near(i)
            b = g * nz + zminus(k)
            drain(buf.at[b], rz.at[k])
            pass_on(k, b)

        loop(1, nz, relay)

        def relay_x(i):
            k = near(i)
            b = gx * nz + zminus(k)
            drain(buf.at[b], rx.at[k])
            send(buf.at[b], buf.at[b], r["ss"].at[ss + 3], r["rs"].at[rs + 1], to_core)

        loop(0, nz, relay_x)
        drain(buf.at[pl.ds(0, nz)], r["rs"].at[rs])
        drain(buf.at[pl.ds(0, nz)], r["rs"].at[rs + 1])

    def ag_sent(buf, ss):
        drain(buf.at[pl.ds(0, nz - 1)], r["ss"].at[ss])
        for j in range(1, 4):
            drain(buf.at[pl.ds(0, nz)], r["ss"].at[ss + j])

    ag_start(r["ag"], 5, r["rz"].at[0])

    drain(r["infoz"].at[pl.ds(0, nz - 1)], r["rs"].at[3])
    r["t8"][...] = jnp.zeros_like(r["t8"])
    for s in range(srcs):
        src = mp * srcs + s
        r["t8"][s : s + 1, :] = r["infoz"][lax.div(src, GRP), lax.rem(src, GRP)]
    lines = r["t8"][...]
    cols = lines.T
    at = lax.broadcasted_iota(jnp.int32, (cl, ns), 1).astype(F32)
    for s in range(srcs):
        here = slice(s * cl, (s + 1) * cl)
        r["pick"][here, :] = jnp.where(cols[0:cl, s : s + 1] == at, 1.0, 0.0).astype(BF16)
        r["logq"][here, :] = jnp.log(cols[64 : 64 + cl, s : s + 1])
    ag_finish(r["ag"], 5, 5, r["rz"].at[0], r["rx"].at[0])

    items = dot(r["pick"][...], r["ag"][...].reshape(ns, out_w), 1, 0)
    r["items"][...] = items.astype(BF16)
    r["items_t"][...] = items.T.astype(BF16)

    ids = lax.broadcasted_iota(jnp.int32, (nc, QT), 0) + mp * nc

    def score(t):
        where = pl.ds(pl.multiple_of(t * QT, QT), QT)
        sc = dot(r["items"][...], r["q"][where, :], 1, 1) * scale - r["logq"][...]
        top = jnp.max(sc, axis=0, keepdims=True)
        ex = jnp.exp(sc - top)
        r["ex"][t] = ex
        r["st"][0, :, where] = top
        r["st"][1, :, where] = jnp.sum(ex, axis=0, keepdims=True)
        r["st"][2, :, where] = jnp.sum(jnp.where(ids == r["pos"][:, where], sc, 0.0), axis=0, keepdims=True)

    loop(0, nq // QT, score)
    r["sr"][pl.ds(mp, 1)] = r["st"][...][None]
    for j in range(1, n_mp):
        md = lax.rem(mp + j, n_mp)
        send(r["st"], r["sr"].at[mp], r["ss"].at[9], r["rs"].at[7], (dp, md))
    drain(r["sr"].at[pl.ds(0, n_mp - 1)], r["rs"].at[7])
    top = r["sr"][0, 0]
    for j in range(1, n_mp):
        top = jnp.maximum(top, r["sr"][j, 0])
    total = jnp.zeros_like(top)
    at_pos = jnp.zeros_like(top)
    for j in range(n_mp):
        total = total + r["sr"][j, 1] * jnp.exp(r["sr"][j, 0] - top)
        at_pos = at_pos + r["sr"][j, 2]
    lse = top + jnp.log(total)
    r["loss"][...] = lse - at_pos
    r["fac"][...] = jnp.exp(r["st"][0] - lse)

    r["ig"][...] = jnp.zeros_like(r["ig"])

    def prob(t):
        where = pl.ds(pl.multiple_of(t * QT, QT), QT)
        pg = r["ex"][t] * r["fac"][:, where] - jnp.where(ids == r["pos"][:, where], 1.0, 0.0)
        pg = pg.astype(BF16)
        r["pg"][t] = pg
        r["ig"][...] += dot(pg, r["q"][where, :], 1, 0)

    loop(0, nq // QT, prob)

    def rs_start(buf, got, ss, rc):
        def go(j):
            xd = lax.rem(x_hi + j, 2)
            gd = xd * 2 + 1 - core
            send(buf.at[pl.ds(gd * nz, nz)], got.at[xd], r["ss"].at[ss], rc.at[xd], to_core)

        go(1)
        go(0)

    def rs_middle(buf, got, out, gotx, ss, rc, rx):
        drain(got.at[1 - x_hi], rc.at[1 - x_hi])

        def go(i):
            k = near(nz - 1 - i)
            zz = zplus(k)
            out[pl.ds(zz, 1)] = buf[pl.ds(gx * nz + zz, 1)] + got[1 - x_hi, pl.ds(zz, 1)]
            send(out.at[zz], gotx.at[zz], r["ss"].at[ss + 1], rx.at[k], to_x)

        loop(0, nz, go)
        drain(got.at[x_hi], rc.at[x_hi])

    def rs_finish(buf, got, gotx, outz, gotz, ss, rs, rx):
        def block(zz):
            return buf[pl.ds(g * nz + zz, 1)] + got[x_hi, pl.ds(zz, 1)] + gotx[pl.ds(zz, 1)]

        def go(i):
            k = near(nz - 1 - i)
            zz = zplus(k)
            drain(gotx.at[zz], rx.at[k])
            outz[pl.ds(zz, 1)] = block(zz)
            send(outz.at[zz], gotz.at[z], r["ss"].at[ss + 2], r["rs"].at[rs], (zz * GRP + g, mp))

        loop(0, nz - 1, go)
        drain(gotx.at[z], rx.at[0])
        gotz[pl.ds(z, 1)] = block(z)

    def rs_result(gotz, rs):
        drain(gotz.at[pl.ds(0, nz - 1)], r["rs"].at[rs])
        total = gotz[0]
        for i in range(1, nz):
            total = total + gotz[i]
        return total

    def rs_sent(buf, out, outz, ss):
        drain(buf.at[pl.ds(0, 2 * nz)], r["ss"].at[ss])
        drain(out, r["ss"].at[ss + 1])
        drain(outz.at[pl.ds(0, nz - 1)], r["ss"].at[ss + 2])

    ig = r["ig"][...] * scale
    hi = ig.astype(BF16)
    lo = (ig - hi.astype(F32)).astype(BF16)
    part = ns // GRP
    for j in range(GRP):
        pick = r["pick"][:, j * part : (j + 1) * part]
        r["es"][j * nz : (j + 1) * nz] = (dot(pick, hi, 0, 0) + dot(pick, lo, 0, 0)).reshape(nz, sm, out_w)
    rs_start(r["es"], r["er"], 10, r["rc"].at[0])

    def query(t):
        qg = dot(r["items_t"][...], r["pg"][t], 1, 0) * scale
        for j in range(QT // qb):
            r["hs"][t * (QT // qb) + j] = qg[:, j * qb : (j + 1) * qb]

    loop(0, nq // QT, query)
    rs_middle(r["es"], r["er"], r["ey"], r["ex2"], 10, r["rc"].at[0], r["rx"].at[1])
    rs_finish(r["es"], r["er"], r["ex2"], r["ez"], r["ezr"], 10, 8, r["rx"].at[1])

    r["hr"][pl.ds(mp, 1)] = r["hs"][pl.ds(mp, 1)]
    for j in range(1, n_mp):
        md = lax.rem(mp + j, n_mp)
        send(r["hs"].at[md], r["hr"].at[mp], r["ss"].at[13], r["rs"].at[9], (dp, md))

    r["igm"][pl.ds(mp, 1)] = rs_result(r["ezr"], 8).astype(BF16)[None]
    for j in range(1, n_mp):
        md = lax.rem(mp + j, n_mp)
        send(r["igm"].at[mp], r["igm"].at[mp], r["ss"].at[14], r["rs"].at[10], (dp, md))
    drain(r["igm"].at[pl.ds(0, n_mp - 1)], r["rs"].at[10])

    item_grad = r["igm"][...].reshape(slots, out_w)
    back = dot(item_grad, r["w_out"][...], 1, 1)
    pre_grad = jnp.where(r["pre"][...] > 0.0, back, 0.0)
    pre_bf = pre_grad.astype(BF16)
    gwi = dot(r["emb"][...], pre_bf, 0, 0)
    gwo = dot(r["hid"][...], item_grad, 0, 0)
    gb = jnp.sum(pre_bf.astype(F32), axis=0, keepdims=True)
    hid_w = gb.shape[1]
    nb = emb_w // n_dp
    r["ga"][:, 0:nb, :] = gwi.reshape(n_dp, nb, hid_w)
    r["ga"][:, nb : nb + 8, :] = jnp.zeros((n_dp, 8, hid_w), F32)
    half = hid_w // 8
    r["ga"][0:half, nb : nb + 8, :] = gwo[:, 0:128].reshape(half, 8, 128)
    r["ga"][half : 2 * half, nb : nb + 8, :] = gwo[:, 128:256].reshape(half, 8, 128)
    r["ga"][2 * half, nb : nb + 1, :] = gb
    rs_start(r["ga"], r["gr"], 15, r["rc"].at[1])
    emb_p = dot(pre_bf, r["w_in"][...], 1, 1)
    for j in range(n_mp):
        r["ks"][j] = emb_p[j * sm : (j + 1) * sm]
    r["kr"][pl.ds(mp, 1)] = r["ks"][pl.ds(mp, 1)]
    rs_middle(r["ga"], r["gr"], r["gy"], r["gx2"], 15, r["rc"].at[1], r["rx"].at[2])
    for j in range(1, n_mp):
        md = lax.rem(mp + j, n_mp)
        send(r["ks"].at[md], r["kr"].at[mp], r["ss"].at[18], r["rs"].at[12], (dp, md))
    rs_finish(r["ga"], r["gr"], r["gx2"], r["gz"], r["gzr"], 15, 11, r["rx"].at[2])

    drain(r["kr"].at[pl.ds(0, n_mp - 1)], r["rs"].at[12])
    emb_own = r["kr"][0]
    for j in range(1, n_mp):
        emb_own = emb_own + r["kr"][j]
    r["eg"][pl.ds(mp, 1)] = emb_own.astype(BF16)[None]
    for j in range(1, n_mp):
        md = lax.rem(mp + j, n_mp)
        send(r["eg"].at[mp], r["eg"].at[mp], r["ss"].at[19], r["rs"].at[13], (dp, md))

    r["gf"][pl.ds(g * nz + z, 1)] = rs_result(r["gzr"], 11)[None]
    ag_start(r["gf"], 20, r["rz"].at[1])

    drain(r["eg"].at[pl.ds(0, n_mp - 1)], r["rs"].at[13])
    r["g_table"][...] = dot(r["ht"][:, 0:slots], r["eg"][...].reshape(slots, emb_w), 1, 0)

    drain(r["hr"].at[pl.ds(0, n_mp - 1)], r["rs"].at[9])
    q_sum = r["hr"][0]
    for j in range(1, n_mp):
        q_sum = q_sum + r["hr"][j]
    r["g_q"][...] = q_sum.T

    ag_finish(r["gf"], 20, 14, r["rz"].at[1], r["rx"].at[3])
    r["g_wi"][...] = r["gf"][:, 0:nb, :].reshape(emb_w, hid_w)
    r["g_wo"][:, 0:128] = r["gf"][0:half, nb : nb + 8, :].reshape(hid_w, 128)
    r["g_wo"][:, 128:256] = r["gf"][half : 2 * half, nb : nb + 8, :].reshape(hid_w, 128)
    r["g_b"][...] = r["gf"][2 * half, nb : nb + 1, :]

    drain(r["r1s"].at[pl.ds(0, GRP - 1)], r["ss"].at[0])
    drain(r["infoz"].at[0, pl.ds(0, GRP - 1)], r["ss"].at[1])
    drain(r["s2"].at[pl.ds(0, nz - 1)], r["ss"].at[2])
    drain(r["infoz"].at[pl.ds(0, nz - 1)], r["ss"].at[3])
    drain(r["bs"].at[pl.ds(0, n_mp - 1)], r["ss"].at[4])
    ag_sent(r["ag"], 5)
    drain(r["sr"].at[pl.ds(0, n_mp - 1)], r["ss"].at[9])
    rs_sent(r["es"], r["ey"], r["ez"], 10)
    drain(r["hs"].at[pl.ds(0, n_mp - 1)], r["ss"].at[13])
    drain(r["igm"].at[pl.ds(0, n_mp - 1)], r["ss"].at[14])
    rs_sent(r["ga"], r["gy"], r["gz"], 15)
    drain(r["ks"].at[pl.ds(0, n_mp - 1)], r["ss"].at[18])
    drain(r["eg"].at[pl.ds(0, n_mp - 1)], r["ss"].at[19])
    ag_sent(r["gf"], 20)


def per_device(queries, item_table, cand_row, cand_owner, cand_count, positive, w_in, b_in, w_out):
    n_dp, n_mp = lax.axis_size("dp"), lax.axis_size("mp")
    nz = n_dp // GRP
    cl = cand_row.shape[0]
    nq, out_w = queries.shape
    rows_dev, emb_w = item_table.shape
    hid_w = w_in.shape[1]
    slots = 2 * n_dp
    sm = slots // n_mp
    nc = n_dp // n_mp * cl
    ns = n_dp * sm
    qb = nq // n_mp
    nt = nq // QT
    gr = emb_w // n_dp + 8
    cand = jnp.stack(
        [
            jnp.pad(cand_owner[:, 0], (0, 128 - cl), constant_values=-1),
            jnp.pad(cand_row, (0, 128 - cl)),
            jnp.pad(cand_count, (64, 64 - cl), constant_values=1),
        ]
    )
    ins = dict(
        q=queries, table=item_table, cand=cand, own_col=cand_owner, pos=positive[None, :],
        w_in=w_in, b_in=b_in[None, :], w_out=w_out,
    )
    outs = dict(
        loss=((1, nq), F32), g_q=((qb, out_w), F32), g_wi=((emb_w, hid_w), F32),
        g_b=((1, hid_w), F32), g_wo=((hid_w, out_w), F32), g_table=((rows_dev, emb_w), F32),
    )
    vmem = dict(
        r1s=((GRP, nz, 128), F32), r1r=((GRP, nz, 128), F32), i1=((1, 128), F32),
        infoz=((nz, GRP, 1, 128), F32), s2=((nz, 1, 128), F32), rq=((nz, 1, 128), F32),
        ht=((rows_dev, 128), BF16), emb=((slots, emb_w), BF16), pre=((slots, hid_w), F32),
        hid=((slots, hid_w), BF16), bs=((n_mp, sm, out_w), F32), br=((n_mp, sm, out_w), F32),
        ag=((n_dp, sm, out_w), BF16), t8=((8, 128), F32), pick=((nc, ns), BF16), logq=((nc, 1), F32),
        items=((nc, out_w), BF16), items_t=((out_w, nc), BF16), ex=((nt, nc, QT), F32),
        st=((3, 1, nq), F32), sr=((n_mp, 3, 1, nq), F32), fac=((1, nq), F32),
        pg=((nt, nc, QT), BF16), ig=((nc, out_w), F32),
        es=((n_dp, sm, out_w), F32), er=((2, nz, sm, out_w), F32), ey=((nz, sm, out_w), F32),
        ex2=((nz, sm, out_w), F32), ez=((nz, sm, out_w), F32), ezr=((nz, sm, out_w), F32),
        hs=((n_mp, out_w, qb), F32), hr=((n_mp, out_w, qb), F32), igm=((n_mp, sm, out_w), BF16),
        ga=((n_dp, gr, hid_w), F32), gr=((2, nz, gr, hid_w), F32), gy=((nz, gr, hid_w), F32),
        gx2=((nz, gr, hid_w), F32), gz=((nz, gr, hid_w), F32), gzr=((nz, gr, hid_w), F32),
        gf=((n_dp, gr, hid_w), F32),
        ks=((n_mp, sm, emb_w), F32), kr=((n_mp, sm, emb_w), F32), eg=((n_mp, sm, emb_w), BF16),
    )
    sems = dict(ss=(24,), rs=(16,), rz=(2, nz), rx=(4, nz), rc=(2, 2))
    names = (*ins, *outs, *vmem, *sems)
    whole = pl.BlockSpec(memory_space=pltpu.VMEM)
    loss, g_q, g_wi, g_b, g_wo, g_table = pl.pallas_call(
        functools.partial(step_kernel, n_dp, n_mp, names),
        out_shape=[jax.ShapeDtypeStruct(*s) for s in outs.values()],
        in_specs=[whole] * len(ins),
        out_specs=[whole] * len(outs),
        scratch_shapes=[pltpu.VMEM(*s) for s in vmem.values()]
        + [pltpu.SemaphoreType.DMA(s) for s in sems.values()],
        compiler_params=pltpu.CompilerParams(
            collective_id=0, has_side_effects=True, vmem_limit_bytes=56 * 1024 * 1024
        ),
    )(*ins.values())
    return loss.reshape(nq), g_q, g_wi, g_b.reshape(hid_w), g_wo, g_table


def solution(mesh):
    placed = (
        P("dp", None),
        P("dp", None),
        P("dp"),
        P("dp", None),
        P("dp"),
        P("dp"),
        P(None, "mp"),
        P("mp"),
        P("mp", None),
    )
    return jax.shard_map(
        per_device,
        mesh=mesh,
        in_specs=placed,
        out_specs=(
            P("dp"),
            P(("dp", "mp"), None),
            P(None, "mp"),
            P("mp"),
            P("mp", None),
            P("dp", None),
        ),
        check_vma=False,
    )
```

```python
import functools
import math

import jax
import jax.numpy as jnp
from jax import lax
from jax.experimental import pallas as pl
from jax.experimental.pallas import tpu as pltpu
from jax.sharding import PartitionSpec as P

MESH = pl.DeviceIdType.MESH
F32 = jnp.float32
BF16 = jnp.bfloat16
GRP = 4
QT = 256
VMEM_BYTES = 64_000_000
OUTS = ("o_loss", "o_q", "o_gf", "o_ht", "o_eg")
NY = 4


def dot(a, b, ca, cb):
    return lax.dot_general(a, b, (((ca,), (cb,)), ((), ())), preferred_element_type=F32)


def drain(ref, sem):
    pltpu.make_async_copy(ref, ref, sem).wait()


def step_kernel(n_dp, n_mp, names, *refs):
    r = dict(zip(names, refs))
    nz = n_dp // GRP
    dp, mp = lax.axis_index("dp"), lax.axis_index("mp")
    z, g = lax.div(dp, GRP), lax.rem(dp, GRP)
    core, x_hi = lax.rem(g, 2), lax.div(g, 2)
    gc = x_hi * 2 + (1 - core)
    gx = lax.rem(g + 2, GRP)
    to_core, to_x = (z * GRP + gc, mp), (z * GRP + gx, mp)
    cl = r["own"].shape[1]
    slots = 2 * n_dp
    sm = slots // n_mp
    srcs = n_dp // n_mp
    nc = srcs * cl
    ns = n_dp * sm
    emb_w = r["table"].shape[1]
    out_w = r["q"].shape[1]
    nq = r["q"].shape[0]
    scale = 1.0 / math.sqrt(out_w)
    qb = nq // n_mp

    def near(i):
        odd = lax.rem(i, 2)
        return odd * lax.div(i + 1, 2) + (1 - odd) * lax.rem(nz - lax.div(i, 2), nz)

    def zplus(k):
        return lax.rem(z + k, nz)

    def zminus(k):
        return lax.rem(z + nz - k, nz)

    def send(src, dst, ssem, rsem, dev):
        pltpu.make_async_remote_copy(
            src_ref=src, dst_ref=dst, send_sem=ssem, recv_sem=rsem, device_id=dev, device_id_type=MESH
        ).start()

    def loop(lo, hi, body):
        def step(i, c):
            body(i)
            return c

        lax.fori_loop(lo, hi, step, 0)

    x_lo, y = lax.div(mp, NY), lax.rem(mp, NY)
    loads = {}
    for i, name in enumerate(("table", "w_in", "w_out", "q")):
        loads[name] = pltpu.make_async_copy(r[name + "_in"], r[name], r["ls"].at[i])

    barrier = pltpu.get_barrier_semaphore()

    def greet(dev):
        pl.semaphore_signal(barrier, inc=1, device_id=dev, device_id_type=MESH)

    loop(0, nz - 1, lambda i: greet((zplus(near(nz - 1 - i)) * GRP + g, mp)))
    for j in range(1, GRP):
        greet((z * GRP + lax.rem(g + j, GRP), mp))
    for j in range(1, n_mp):
        greet((dp, lax.rem(mp + j, n_mp)))

    for name in loads:
        loads[name].start()

    r["t8"][...] = jnp.full_like(r["t8"], -1.0)
    r["t8"][0:1, 0:cl] = r["own"][...].astype(F32)
    r["t8"][1:2, 0:cl] = r["row"][...].astype(F32)
    cand = r["t8"][...]
    own_col = cand.T[0:cl, 0:1]
    lane = lax.broadcasted_iota(jnp.int32, (n_dp, 128), 1)
    sub = lax.broadcasted_iota(jnp.int32, (n_dp, 128), 0)
    earlier = (own_col == cand[0:1, :]) & (
        lax.broadcasted_iota(jnp.int32, (cl, 128), 0) < lax.broadcasted_iota(jnp.int32, (cl, 128), 1)
    )
    rank = jnp.sum(jnp.where(earlier, 1.0, 0.0), axis=0, keepdims=True)
    owner = cand[0:1, :].astype(jnp.int32)
    owner_of = (sub & (nz - 1)) * GRP + lax.shift_right_logical(sub, int(math.log2(nz)))
    mine = owner_of == owner
    row1 = cand[1:2, :] + 1.0
    first = jnp.sum(jnp.where(mine & (rank < 0.5), row1, 0.0), axis=1, keepdims=True)
    second = jnp.sum(jnp.where(mine & (rank > 0.5), row1, 0.0), axis=1, keepdims=True)
    asked = jnp.where(lane == 2 * dp, first, jnp.where(lane == 2 * dp + 1, second, 0.0))
    for j in range(GRP):
        r["r1s"][j] = asked[j * nz : (j + 1) * nz]
    r["r1r"][pl.ds(g, 1)] = r["r1s"][pl.ds(g, 1)]
    code = (
        ((owner & (GRP - 1)) * nz + lax.shift_right_logical(owner, 2)) * sm + lax.rem(dp, srcs) * 2
    ).astype(F32) + rank
    r["i1"][0:1, :] = code
    r["i1"][0:1, 64 : 64 + cl] = r["cnt"][...].astype(F32)
    r["infoz"][pl.ds(z, 1), pl.ds(g, 1)] = r["i1"][...][None, None]

    pl.semaphore_wait(barrier, nz - 1 + GRP - 1 + n_mp - 1)

    for j in range(1, GRP):
        gd = lax.rem(g + j, GRP)
        send(r["r1s"].at[gd], r["r1r"].at[g], r["ss"].at[0], r["rs"].at[0], (z * GRP + gd, mp))
    for j in range(1, GRP):
        gd = lax.rem(g + j, GRP)
        send(r["i1"], r["infoz"].at[z, g], r["ss"].at[1], r["rs"].at[1], (z * GRP + gd, mp))
    drain(r["r1r"].at[pl.ds(0, GRP - 1)], r["rs"].at[0])
    asked4 = r["r1r"][0] + r["r1r"][1] + r["r1r"][2] + r["r1r"][3]
    for i in range(nz):
        r["s2"][i] = asked4[i : i + 1, :]
    r["rq"][pl.ds(z, 1)] = r["s2"][pl.ds(z, 1)]

    def ask(i):
        zd = zplus(near(nz - 1 - i))
        send(r["s2"].at[zd], r["rq"].at[z], r["ss"].at[2], r["rs"].at[2], (zd * GRP + g, mp))

    loop(0, nz - 1, ask)
    drain(r["infoz"].at[0, pl.ds(0, GRP - 1)], r["rs"].at[1])

    def tell(i):
        zd = zplus(near(nz - 1 - i))
        send(r["infoz"].at[z], r["infoz"].at[z], r["ss"].at[3], r["rs"].at[3], (zd * GRP + g, mp))

    loop(0, nz - 1, tell)
    drain(r["rq"].at[pl.ds(0, nz - 1)], r["rs"].at[2])

    asked_row = r["rq"][0]
    for i in range(1, nz):
        asked_row = asked_row + r["rq"][i]
    for name in ("table", "w_in", "w_out"):
        loads[name].wait()
    rows_dev = r["table"].shape[0]
    hits = lax.broadcasted_iota(jnp.int32, (rows_dev, 128), 0).astype(F32) + 1.0 == asked_row
    r["ht"][...] = jnp.where(hits, 1.0, 0.0).astype(BF16)
    emb = dot(r["ht"][...], r["table"][...], 0, 0)[:slots].astype(BF16)
    r["emb"][...] = emb
    pre = dot(emb, r["w_in"][...], 1, 0) + r["b_in"][...]
    r["pre"][...] = pre
    hidden = jnp.maximum(pre, 0.0).astype(BF16)
    r["hid"][...] = hidden
    item_p = dot(hidden, r["w_out"][...], 1, 0)
    for j in range(n_mp):
        r["bs"][j] = item_p[j * sm : (j + 1) * sm]
    r["br"][pl.ds(mp, 1)] = r["bs"][pl.ds(mp, 1)]
    for j in range(1, n_mp):
        md = lax.rem(mp + j, n_mp)
        send(r["bs"].at[md], r["br"].at[mp], r["ss"].at[4], r["rs"].at[4], (dp, md))
    drain(r["br"].at[pl.ds(0, n_mp - 1)], r["rs"].at[4])
    item_own = r["br"][0]
    for j in range(1, n_mp):
        item_own = item_own + r["br"][j]
    r["ag"][pl.ds(g * nz + z, 1)] = item_own.astype(BF16)[None]

    def ag_start(buf, ss, rz):
        own = g * nz + z

        def go(i):
            k = near(nz - 1 - i)
            send(buf.at[own], buf.at[own], r["ss"].at[ss], rz.at[k], (zplus(k) * GRP + g, mp))

        loop(0, nz - 1, go)

    def ag_finish(buf, ss, rs, rz, rx):
        own = g * nz + z

        def pass_on(k, b):
            send(buf.at[b], buf.at[b], r["ss"].at[ss + 1], rx.at[k], to_x)
            send(buf.at[b], buf.at[b], r["ss"].at[ss + 2], r["rs"].at[rs], to_core)

        pass_on(0, own)

        def relay(i):
            k = near(i)
            b = g * nz + zminus(k)
            drain(buf.at[b], rz.at[k])
            pass_on(k, b)

        loop(1, nz, relay)

        def relay_x(i):
            k = near(i)
            b = gx * nz + zminus(k)
            drain(buf.at[b], rx.at[k])
            send(buf.at[b], buf.at[b], r["ss"].at[ss + 3], r["rs"].at[rs + 1], to_core)

        loop(0, nz, relay_x)
        drain(buf.at[pl.ds(0, nz)], r["rs"].at[rs])
        drain(buf.at[pl.ds(0, nz)], r["rs"].at[rs + 1])

    def ag_sent(buf, ss):
        drain(buf.at[pl.ds(0, nz - 1)], r["ss"].at[ss])
        for j in range(1, 4):
            drain(buf.at[pl.ds(0, nz)], r["ss"].at[ss + j])

    ag_start(r["ag"], 5, r["rz"].at[0])

    drain(r["infoz"].at[pl.ds(0, nz - 1)], r["rs"].at[3])
    r["t8"][...] = jnp.zeros_like(r["t8"])
    for s in range(srcs):
        src = mp * srcs + s
        r["t8"][s : s + 1, :] = r["infoz"][lax.div(src, GRP), lax.rem(src, GRP)]
    lines = r["t8"][...]
    cols = lines.T
    at = lax.broadcasted_iota(jnp.int32, (cl, ns), 1).astype(F32)
    for s in range(srcs):
        here = slice(s * cl, (s + 1) * cl)
        r["pick"][here, :] = jnp.where(cols[0:cl, s : s + 1] == at, 1.0, 0.0).astype(BF16)
        r["logq"][here, :] = jnp.log(cols[64 : 64 + cl, s : s + 1])
    ag_finish(r["ag"], 5, 5, r["rz"].at[0], r["rx"].at[0])

    loads["q"].wait()
    items = dot(r["pick"][...], r["ag"][...].reshape(ns, out_w), 1, 0)
    r["items"][...] = items.astype(BF16)
    r["items_t"][...] = items.T.astype(BF16)

    ids = lax.broadcasted_iota(jnp.int32, (nc, QT), 0) + mp * nc

    def score(t):
        where = pl.ds(pl.multiple_of(t * QT, QT), QT)
        sc = dot(r["items"][...], r["q"][where, :], 1, 1) * scale - r["logq"][...]
        top = jnp.max(sc, axis=0, keepdims=True)
        ex = jnp.exp(sc - top)
        r["ex"][t] = ex
        r["st"][0, :, where] = top
        r["st"][1, :, where] = jnp.sum(ex, axis=0, keepdims=True)
        r["st"][2, :, where] = jnp.sum(jnp.where(ids == r["pos"][:, where], sc, 0.0), axis=0, keepdims=True)

    loop(0, nq // QT, score)
    r["sr"][pl.ds(mp, 1)] = r["st"][...][None]
    for j in range(1, n_mp):
        md = lax.rem(mp + j, n_mp)
        send(r["st"], r["sr"].at[mp], r["ss"].at[9], r["rs"].at[7], (dp, md))
    drain(r["sr"].at[pl.ds(0, n_mp - 1)], r["rs"].at[7])
    top = r["sr"][0, 0]
    for j in range(1, n_mp):
        top = jnp.maximum(top, r["sr"][j, 0])
    total = jnp.zeros_like(top)
    at_pos = jnp.zeros_like(top)
    for j in range(n_mp):
        total = total + r["sr"][j, 1] * jnp.exp(r["sr"][j, 0] - top)
        at_pos = at_pos + r["sr"][j, 2]
    lse = top + jnp.log(total)
    r["loss"][...] = lse - at_pos
    r["fac"][...] = jnp.exp(r["st"][0] - lse)

    r["ig"][...] = jnp.zeros_like(r["ig"])

    def prob(t):
        where = pl.ds(pl.multiple_of(t * QT, QT), QT)
        pg = r["ex"][t] * r["fac"][:, where] - jnp.where(ids == r["pos"][:, where], 1.0, 0.0)
        pg = pg.astype(BF16)
        r["pg"][t] = pg
        r["ig"][...] += dot(pg, r["q"][where, :], 1, 0)

    loop(0, nq // QT, prob)

    def rs_start(buf, got, ss, rc):
        def go(j):
            xd = lax.rem(x_hi + j, 2)
            gd = xd * 2 + 1 - core
            send(buf.at[pl.ds(gd * nz, nz)], got.at[xd], r["ss"].at[ss], rc.at[xd], to_core)

        go(1)
        go(0)

    def rs_middle(buf, got, out, gotx, ss, rc, rx):
        drain(got.at[1 - x_hi], rc.at[1 - x_hi])

        def go(i):
            k = near(nz - 1 - i)
            zz = zplus(k)
            out[pl.ds(zz, 1)] = buf[pl.ds(gx * nz + zz, 1)] + got[1 - x_hi, pl.ds(zz, 1)]
            send(out.at[zz], gotx.at[zz], r["ss"].at[ss + 1], rx.at[k], to_x)

        loop(0, nz, go)
        drain(got.at[x_hi], rc.at[x_hi])

    def rs_finish(buf, got, gotx, outz, gotz, ss, rs, rx):
        def block(zz):
            return buf[pl.ds(g * nz + zz, 1)] + got[x_hi, pl.ds(zz, 1)] + gotx[pl.ds(zz, 1)]

        def go(i):
            k = near(nz - 1 - i)
            zz = zplus(k)
            drain(gotx.at[zz], rx.at[k])
            outz[pl.ds(zz, 1)] = block(zz)
            send(outz.at[zz], gotz.at[z], r["ss"].at[ss + 2], r["rs"].at[rs], (zz * GRP + g, mp))

        loop(0, nz - 1, go)
        drain(gotx.at[z], rx.at[0])
        gotz[pl.ds(z, 1)] = block(z)

    def rs_result(gotz, rs):
        drain(gotz.at[pl.ds(0, nz - 1)], r["rs"].at[rs])
        total = gotz[0]
        for i in range(1, nz):
            total = total + gotz[i]
        return total

    def rs_sent(buf, out, outz, ss):
        drain(buf.at[pl.ds(0, 2 * nz)], r["ss"].at[ss])
        drain(out, r["ss"].at[ss + 1])
        drain(outz.at[pl.ds(0, nz - 1)], r["ss"].at[ss + 2])

    ig = r["ig"][...] * scale
    hi = ig.astype(BF16)
    lo = (ig - hi.astype(F32)).astype(BF16)
    part = ns // GRP
    for j in range(GRP):
        pick = r["pick"][:, j * part : (j + 1) * part]
        r["es"][j * nz : (j + 1) * nz] = (dot(pick, hi, 0, 0) + dot(pick, lo, 0, 0)).reshape(nz, sm, out_w)
    rs_start(r["es"], r["er"], 10, r["rc"].at[0])

    def query(t):
        qg = dot(r["items_t"][...], r["pg"][t], 1, 0) * scale
        for j in range(QT // qb):
            b = t * (QT // qb) + j
            r["hs"][lax.rem(b, NY), lax.div(b, NY)] = qg[:, j * qb : (j + 1) * qb]

    loop(0, nq // QT, query)
    r["hr"][pl.ds(y, 1)] = r["hs"][pl.ds(y, 1)]
    for j in range(1, NY):
        yd = lax.rem(y + j, NY)
        send(r["hs"].at[yd], r["hr"].at[y], r["ss"].at[13], r["rs"].at[9], (dp, x_lo * NY + yd))
    rs_middle(r["es"], r["er"], r["ey"], r["ex2"], 10, r["rc"].at[0], r["rx"].at[1])
    rs_finish(r["es"], r["er"], r["ex2"], r["ez"], r["ezr"], 10, 8, r["rx"].at[1])

    drain(r["hr"].at[pl.ds(0, NY - 1)], r["rs"].at[9])
    for j in range(2):
        xd = lax.rem(x_lo + 1 + j, 2)
        q_sum = r["hr"][0, pl.ds(xd, 1)]
        for i in range(1, NY):
            q_sum = q_sum + r["hr"][i, pl.ds(xd, 1)]
        r["h2"][j] = q_sum[0]
        if j == 0:
            send(r["h2"].at[0], r["h3"], r["ss"].at[24], r["rs"].at[16], (dp, xd * NY + y))

    r["igm"][pl.ds(mp, 1)] = rs_result(r["ezr"], 8).astype(BF16)[None]
    for j in range(1, n_mp):
        md = lax.rem(mp + j, n_mp)
        send(r["igm"].at[mp], r["igm"].at[mp], r["ss"].at[14], r["rs"].at[10], (dp, md))
    drain(r["igm"].at[pl.ds(0, n_mp - 1)], r["rs"].at[10])

    item_grad = r["igm"][...].reshape(slots, out_w)
    back = dot(item_grad, r["w_out"][...], 1, 1)
    pre_grad = jnp.where(r["pre"][...] > 0.0, back, 0.0)
    pre_bf = pre_grad.astype(BF16)
    gwi = dot(r["emb"][...], pre_bf, 0, 0)
    gwo = dot(r["hid"][...], item_grad, 0, 0)
    gb = jnp.sum(pre_bf.astype(F32), axis=0, keepdims=True)
    hid_w = gb.shape[1]
    nb = emb_w // n_dp
    r["ga"][:, 0:nb, :] = gwi.reshape(n_dp, nb, hid_w)
    r["ga"][:, nb : nb + 8, :] = jnp.zeros((n_dp, 8, hid_w), F32)
    half = hid_w // 8
    r["ga"][0:half, nb : nb + 8, :] = gwo[:, 0:128].reshape(half, 8, 128)
    r["ga"][half : 2 * half, nb : nb + 8, :] = gwo[:, 128:256].reshape(half, 8, 128)
    r["ga"][2 * half, nb : nb + 1, :] = gb
    rs_start(r["ga"], r["gr"], 15, r["rc"].at[1])
    emb_p = dot(pre_bf, r["w_in"][...], 1, 1)
    for j in range(n_mp):
        r["ks"][j] = emb_p[j * sm : (j + 1) * sm]
    r["kr"][pl.ds(mp, 1)] = r["ks"][pl.ds(mp, 1)]
    rs_middle(r["ga"], r["gr"], r["gy"], r["gx2"], 15, r["rc"].at[1], r["rx"].at[2])
    for j in range(1, n_mp):
        md = lax.rem(mp + j, n_mp)
        send(r["ks"].at[md], r["kr"].at[mp], r["ss"].at[18], r["rs"].at[12], (dp, md))
    rs_finish(r["ga"], r["gr"], r["gx2"], r["gz"], r["gzr"], 15, 11, r["rx"].at[2])

    drain(r["kr"].at[pl.ds(0, n_mp - 1)], r["rs"].at[12])
    emb_own = r["kr"][0]
    for j in range(1, n_mp):
        emb_own = emb_own + r["kr"][j]
    r["eg"][pl.ds(mp, 1)] = emb_own.astype(BF16)[None]
    for j in range(1, n_mp):
        md = lax.rem(mp + j, n_mp)
        send(r["eg"].at[mp], r["eg"].at[mp], r["ss"].at[19], r["rs"].at[13], (dp, md))

    r["gf"][pl.ds(g * nz + z, 1)] = rs_result(r["gzr"], 11).astype(BF16)[None]
    ag_start(r["gf"], 20, r["rz"].at[1])

    def out(name, src):
        copy = pltpu.make_async_copy(src, r[name], r["os"].at[OUTS.index(name)])
        copy.start()
        return copy

    done = [out("o_ht", r["ht"]), out("o_loss", r["loss"])]
    drain(r["h3"], r["rs"].at[16])
    r["qs"][...] = (r["h2"][1] + r["h3"][...]).T
    done.append(out("o_q", r["qs"]))
    drain(r["eg"].at[pl.ds(0, n_mp - 1)], r["rs"].at[13])
    done.append(out("o_eg", r["eg"]))
    for copy in done:
        copy.wait()

    drain(r["r1s"].at[pl.ds(0, GRP - 1)], r["ss"].at[0])
    drain(r["infoz"].at[0, pl.ds(0, GRP - 1)], r["ss"].at[1])
    drain(r["s2"].at[pl.ds(0, nz - 1)], r["ss"].at[2])
    drain(r["infoz"].at[pl.ds(0, nz - 1)], r["ss"].at[3])
    drain(r["bs"].at[pl.ds(0, n_mp - 1)], r["ss"].at[4])
    ag_sent(r["ag"], 5)
    drain(r["sr"].at[pl.ds(0, n_mp - 1)], r["ss"].at[9])
    rs_sent(r["es"], r["ey"], r["ez"], 10)
    drain(r["hs"].at[pl.ds(0, NY - 1)], r["ss"].at[13])
    drain(r["h3"], r["ss"].at[24])
    drain(r["igm"].at[pl.ds(0, n_mp - 1)], r["ss"].at[14])
    rs_sent(r["ga"], r["gy"], r["gz"], 15)
    drain(r["ks"].at[pl.ds(0, n_mp - 1)], r["ss"].at[18])
    drain(r["eg"].at[pl.ds(0, n_mp - 1)], r["ss"].at[19])

    ag_finish(r["gf"], 20, 14, r["rz"].at[1], r["rx"].at[3])
    last = out("o_gf", r["gf"])
    ag_sent(r["gf"], 20)
    last.wait()


def results_kernel(names, *refs):
    r = dict(zip(names, refs))
    n_dp, gr, hid_w = r["gf"].shape
    nb = gr - 8
    emb_w = r["g_wi"].shape[0]
    slots = r["eg"].shape[0] * r["eg"].shape[1]
    half = hid_w // 8
    ht, eg = r["ht"][:, 0:slots], r["eg"][...].reshape(slots, emb_w)
    r["g_table"][...] = dot(ht, eg, 1, 0)
    gf = r["gf"][...].astype(F32)
    r["g_wi"][...] = gf[:, 0:nb, :].reshape(emb_w, hid_w)
    r["g_wo"][:, 0:128] = gf[0:half, nb : nb + 8, :].reshape(hid_w, 128)
    r["g_wo"][:, 128:256] = gf[half : 2 * half, nb : nb + 8, :].reshape(hid_w, 128)
    r["g_b"][...] = gf[2 * half, nb : nb + 1, :]
    r["g_q"][...] = r["qs"][...]
    r["g_loss"][...] = r["loss"][...]


def per_device(queries, item_table, cand_row, cand_owner, cand_count, positive, w_in, b_in, w_out):
    n_dp, n_mp = lax.axis_size("dp"), lax.axis_size("mp")
    nz = n_dp // GRP
    cl = cand_row.shape[0]
    nq, out_w = queries.shape
    rows_dev, emb_w = item_table.shape
    hid_w = w_in.shape[1]
    slots = 2 * n_dp
    sm = slots // n_mp
    nc = n_dp // n_mp * cl
    ns = n_dp * sm
    qb = nq // n_mp
    nt = nq // QT
    gr = emb_w // n_dp + 8
    ins = dict(
        own=cand_owner.reshape(1, cl), row=cand_row[None, :], cnt=cand_count[None, :],
        pos=positive[None, :], b_in=b_in[None, :],
    )
    far = dict(table_in=item_table, w_in_in=w_in, w_out_in=w_out, q_in=queries)
    mids = dict(
        o_loss=((1, nq), F32), o_q=((qb, out_w), F32), o_gf=((n_dp, gr, hid_w), BF16),
        o_ht=((rows_dev, 128), BF16), o_eg=((n_mp, sm, emb_w), BF16),
    )
    outs = dict(
        g_loss=((1, nq), F32), g_q=((qb, out_w), F32), g_wi=((emb_w, hid_w), F32),
        g_b=((1, hid_w), F32), g_wo=((hid_w, out_w), F32), g_table=((rows_dev, emb_w), F32),
    )
    vmem = dict(
        q=((nq, out_w), BF16), table=((rows_dev, emb_w), BF16), w_in=((emb_w, hid_w), BF16),
        w_out=((hid_w, out_w), BF16), loss=((1, nq), F32), qs=((qb, out_w), F32),
        r1s=((GRP, nz, 128), F32), r1r=((GRP, nz, 128), F32), i1=((1, 128), F32),
        infoz=((nz, GRP, 1, 128), F32), s2=((nz, 1, 128), F32), rq=((nz, 1, 128), F32),
        ht=((rows_dev, 128), BF16), emb=((slots, emb_w), BF16), pre=((slots, hid_w), F32),
        hid=((slots, hid_w), BF16), bs=((n_mp, sm, out_w), F32), br=((n_mp, sm, out_w), F32),
        ag=((n_dp, sm, out_w), BF16), t8=((8, 128), F32), pick=((nc, ns), BF16), logq=((nc, 1), F32),
        items=((nc, out_w), BF16), items_t=((out_w, nc), BF16), ex=((nt, nc, QT), F32),
        st=((3, 1, nq), F32), sr=((n_mp, 3, 1, nq), F32), fac=((1, nq), F32),
        pg=((nt, nc, QT), BF16), ig=((nc, out_w), F32),
        es=((n_dp, sm, out_w), F32), er=((2, nz, sm, out_w), F32), ey=((nz, sm, out_w), F32),
        ex2=((nz, sm, out_w), F32), ez=((nz, sm, out_w), F32), ezr=((nz, sm, out_w), F32),
        hs=((NY, 2, out_w, qb), F32), hr=((NY, 2, out_w, qb), F32), h2=((2, out_w, qb), F32), h3=((out_w, qb), F32), igm=((n_mp, sm, out_w), BF16),
        ga=((n_dp, gr, hid_w), F32), gr=((2, nz, gr, hid_w), F32), gy=((nz, gr, hid_w), F32),
        gx2=((nz, gr, hid_w), F32), gz=((nz, gr, hid_w), F32), gzr=((nz, gr, hid_w), F32),
        gf=((n_dp, gr, hid_w), BF16),
        ks=((n_mp, sm, emb_w), F32), kr=((n_mp, sm, emb_w), F32), eg=((n_mp, sm, emb_w), BF16),
    )
    sems = dict(ss=(25,), rs=(17,), rz=(2, nz), rx=(4, nz), rc=(2, 2), ls=(4,), os=(5,))
    names = (*ins, *far, *mids, *vmem, *sems)
    whole = pl.BlockSpec(memory_space=pltpu.VMEM)
    there = pl.BlockSpec(memory_space=pl.ANY)
    loss, qs, gf, ht, eg = pl.pallas_call(
        functools.partial(step_kernel, n_dp, n_mp, names),
        out_shape=[jax.ShapeDtypeStruct(*s) for s in mids.values()],
        in_specs=[whole] * len(ins) + [there] * len(far),
        out_specs=[there] * len(mids),
        scratch_shapes=[pltpu.VMEM(*s) for s in vmem.values()]
        + [pltpu.SemaphoreType.DMA(s) for s in sems.values()],
        compiler_params=pltpu.CompilerParams(
            collective_id=0, has_side_effects=True, vmem_limit_bytes=VMEM_BYTES
        ),
    )(*ins.values(), *far.values())
    loss, g_q, g_wi, g_b, g_wo, g_table = pl.pallas_call(
        functools.partial(results_kernel, ("loss", "qs", "gf", "ht", "eg", *outs)),
        out_shape=[jax.ShapeDtypeStruct(*s) for s in outs.values()],
        in_specs=[whole] * 5,
        out_specs=[whole] * len(outs),
        compiler_params=pltpu.CompilerParams(vmem_limit_bytes=VMEM_BYTES),
    )(loss, qs, gf, ht, eg)
    return loss.reshape(nq), g_q, g_wi, g_b.reshape(hid_w), g_wo, g_table


def solution(mesh):
    placed = (
        P("dp", None),
        P("dp", None),
        P("dp"),
        P("dp", None),
        P("dp"),
        P("dp"),
        P(None, "mp"),
        P("mp"),
        P("mp", None),
    )
    return jax.shard_map(
        per_device,
        mesh=mesh,
        in_specs=placed,
        out_specs=(
            P("dp"),
            P(("dp", "mp"), None),
            P(None, "mp"),
            P("mp"),
            P("mp", None),
            P("dp", None),
        ),
        check_vma=False,
    )
```

```python
import functools
import math

import jax
import jax.numpy as jnp
from jax import lax
from jax.experimental import pallas as pl
from jax.experimental.pallas import tpu as pltpu
from jax.sharding import PartitionSpec as P

MESH = pl.DeviceIdType.MESH
F32 = jnp.float32
BF16 = jnp.bfloat16
GRP = 4
QT = 256
VMEM_BYTES = 64_000_000
TABLE_PARTS = 4
MIDS = ("eg", "ht", "gf", "q", "loss")
OUTS = ("o_loss", "o_q", "o_gf", "o_ht", "o_eg")
FIXED = 32767.0
FAR_ITEMS, FAR_SUMS = 0, 2
NY = 4


def dot(a, b, ca, cb):
    return lax.dot_general(a, b, (((ca,), (cb,)), ((), ())), preferred_element_type=F32)


def drain(ref, sem):
    pltpu.make_async_copy(ref, ref, sem).wait()


def coded(v, tiles):
    rows, width = v.shape[-2], v.shape[-1]
    t = v.reshape(tiles, rows // tiles, width)
    top = jnp.max(jnp.abs(t), axis=1, keepdims=True)
    fixed = t * (FIXED / jnp.maximum(top, 1e-30))
    fixed = jnp.round(fixed).reshape(rows, width).astype(jnp.int32).astype(jnp.int16)
    return fixed, top * (1.0 / FIXED)


def decoded(fixed, scales):
    rows, width = fixed.shape
    tiles = scales.shape[0]
    v = fixed.astype(jnp.int32).astype(F32).reshape(tiles, rows // tiles, width)
    return (v * scales).reshape(rows, width)


def step_kernel(n_dp, n_mp, names, *refs):
    r = dict(zip(names, refs))
    nz = n_dp // GRP
    dp, mp = lax.axis_index("dp"), lax.axis_index("mp")
    z, g = lax.div(dp, GRP), lax.rem(dp, GRP)
    core, x_hi = lax.rem(g, 2), lax.div(g, 2)
    gc = x_hi * 2 + (1 - core)
    gx = lax.rem(g + 2, GRP)
    to_core, to_x = (z * GRP + gc, mp), (z * GRP + gx, mp)
    to_diag = (z * GRP + lax.rem(gc + 2, GRP), mp)
    cl = r["own"].shape[1]
    slots = 2 * n_dp
    sm = slots // n_mp
    srcs = n_dp // n_mp
    nc = srcs * cl
    ns = n_dp * sm
    emb_w = r["table"].shape[1]
    out_w = r["q"].shape[1]
    nq = r["q"].shape[0]
    scale = 1.0 / math.sqrt(out_w)
    qb = nq // n_mp

    def near(i):
        odd = lax.rem(i, 2)
        return odd * lax.div(i + 1, 2) + (1 - odd) * lax.rem(nz - lax.div(i, 2), nz)

    def zplus(k):
        return lax.rem(z + k, nz)

    def zminus(k):
        return lax.rem(z + nz - k, nz)

    def send(src, dst, ssem, rsem, dev):
        pltpu.make_async_remote_copy(
            src_ref=src, dst_ref=dst, send_sem=ssem, recv_sem=rsem, device_id=dev, device_id_type=MESH
        ).start()

    def loop(lo, hi, body):
        def step(i, c):
            body(i)
            return c

        lax.fori_loop(lo, hi, step, 0)

    x_lo, y = lax.div(mp, NY), lax.rem(mp, NY)
    columns = [
        (1 - x_lo) * NY + lax.rem(y + j, NY) if far else x_lo * NY + lax.rem(y + j, NY)
        for far in (True, False) for j in (2, 1, 3, 0) if far or j
    ]
    loads = {}
    for i, name in enumerate(("table", "w_in", "w_out", "q")):
        loads[name] = pltpu.make_async_copy(r[name + "_in"], r[name], r["ls"].at[i])

    barrier = pltpu.get_barrier_semaphore()

    def greet(dev):
        pl.semaphore_signal(barrier, inc=1, device_id=dev, device_id_type=MESH)

    def greet_z(i):
        zd = zplus(near(nz - 1 - i))
        for j in range(GRP):
            greet((zd * GRP + lax.rem(g + j, GRP), mp))

    loop(0, nz - 1, greet_z)
    for j in range(1, GRP):
        greet((z * GRP + lax.rem(g + j, GRP), mp))
    for j in range(1, n_mp):
        greet((dp, lax.rem(mp + j, n_mp)))

    for name in loads:
        loads[name].start()

    r["t8"][...] = jnp.full_like(r["t8"], -1.0)
    r["t8"][0:1, 0:cl] = r["own"][...].astype(F32)
    r["t8"][1:2, 0:cl] = r["row"][...].astype(F32)
    cand = r["t8"][...]
    own_col = cand.T[0:cl, 0:1]
    lane = lax.broadcasted_iota(jnp.int32, (n_dp, 128), 1)
    sub = lax.broadcasted_iota(jnp.int32, (n_dp, 128), 0)
    earlier = (own_col == cand[0:1, :]) & (
        lax.broadcasted_iota(jnp.int32, (cl, 128), 0) < lax.broadcasted_iota(jnp.int32, (cl, 128), 1)
    )
    rank = jnp.sum(jnp.where(earlier, 1.0, 0.0), axis=0, keepdims=True)
    owner = cand[0:1, :].astype(jnp.int32)
    mine = sub == owner
    row1 = cand[1:2, :] + 1.0
    first = jnp.sum(jnp.where(mine & (rank < 0.5), row1, 0.0), axis=1, keepdims=True)
    second = jnp.sum(jnp.where(mine & (rank > 0.5), row1, 0.0), axis=1, keepdims=True)
    asked = jnp.where(lane == 2 * dp, first, jnp.where(lane == 2 * dp + 1, second, 0.0))
    r["r1s"][...] = asked.reshape(n_dp, 1, 128)
    r["rq"][pl.ds(dp, 1)] = r["r1s"][pl.ds(dp, 1)]
    code = (
        ((owner & (GRP - 1)) * nz + lax.shift_right_logical(owner, 2)) * sm + lax.rem(dp, srcs) * 2
    ).astype(F32) + rank
    r["i1"][0:1, :] = code
    r["i1"][0:1, 64 : 64 + cl] = r["cnt"][...].astype(F32)
    r["infoz"][pl.ds(z, 1), pl.ds(g, 1)] = r["i1"][...][None, None]

    pl.semaphore_wait(barrier, n_dp - 1 + n_mp - 1)

    def ask(zd, j):
        to = zd * GRP + lax.rem(g + j, GRP)
        send(r["r1s"].at[to], r["rq"].at[dp], r["ss"].at[0], r["rs"].at[0], (to, mp))

    def ask_z(i):
        for j in range(GRP):
            ask(zplus(near(nz - 1 - i)), j)

    loop(0, nz - 1, ask_z)
    for j in range(1, GRP):
        ask(z, j)
    for j in range(1, GRP):
        gd = lax.rem(g + j, GRP)
        send(r["i1"], r["infoz"].at[z, g], r["ss"].at[1], r["rs"].at[1], (z * GRP + gd, mp))
    drain(r["infoz"].at[0, pl.ds(0, GRP - 1)], r["rs"].at[1])

    def tell(i):
        zd = zplus(near(nz - 1 - i))
        send(r["infoz"].at[z], r["infoz"].at[z], r["ss"].at[3], r["rs"].at[3], (zd * GRP + g, mp))

    loop(0, nz - 1, tell)
    drain(r["rq"].at[pl.ds(0, n_dp - 1)], r["rs"].at[0])

    asked_row = jnp.sum(r["rq"][...], axis=0)
    for name in ("table", "w_in", "w_out"):
        loads[name].wait()
    rows_dev = r["table"].shape[0]
    hits = lax.broadcasted_iota(jnp.int32, (rows_dev, 128), 0).astype(F32) + 1.0 == asked_row
    r["ht"][...] = jnp.where(hits, 1.0, 0.0).astype(BF16)
    emb = dot(r["ht"][...], r["table"][...], 0, 0)[:slots].astype(BF16)
    r["emb"][...] = emb
    pre = dot(emb, r["w_in"][...], 1, 0) + r["b_in"][...]
    r["pre"][...] = pre
    hidden = jnp.maximum(pre, 0.0).astype(BF16)
    r["hid"][...] = hidden
    item_p = dot(hidden, r["w_out"][...], 1, 0)
    for j in range(n_mp):
        r["bs"][j] = item_p[j * sm : (j + 1) * sm]
    r["br"][pl.ds(mp, 1)] = r["bs"][pl.ds(mp, 1)]
    for md in columns:
        send(r["bs"].at[md], r["br"].at[mp], r["ss"].at[4], r["rs"].at[4], (dp, md))
    drain(r["br"].at[pl.ds(0, n_mp - 1)], r["rs"].at[4])
    item_own = r["br"][0]
    for j in range(1, n_mp):
        item_own = item_own + r["br"][j]
    r["ag"][pl.ds(g * nz + z, 1)] = item_own.astype(BF16)[None]

    def ag_start(buf, ss, rz):
        own = g * nz + z

        def go(i):
            k = near(nz - 1 - i)
            send(buf.at[own], buf.at[own], r["ss"].at[ss], rz.at[k], (zplus(k) * GRP + g, mp))

        loop(0, nz - 1, go)

    def ag_finish(buf, ss, rs, rz, rx, far):
        own = g * nz + z

        def pass_on(k, b):
            send(buf.at[b], buf.at[b], r["ss"].at[ss + 1], rx.at[k], to_x)
            send(buf.at[b], buf.at[b], r["ss"].at[ss + 2], r["rs"].at[rs], to_core)

        pass_on(0, own)

        def relay(i):
            k = near(i)
            b = g * nz + zminus(k)
            drain(buf.at[b], rz.at[k])
            pass_on(k, b)
            return b

        def relay_far(i):
            b = relay(i)
            send(buf.at[b], buf.at[b], r["ss"].at[ss + 3], r["rs"].at[rs + 1], to_diag)

        loop(1, nz - far, relay)
        loop(nz - far, nz, relay_far)

        def relay_x(i):
            k = near(i)
            b = gx * nz + zminus(k)
            drain(buf.at[b], rx.at[k])
            send(buf.at[b], buf.at[b], r["ss"].at[ss + 3], r["rs"].at[rs + 1], to_core)

        loop(0, nz - far, relay_x)

        def take_x(i):
            k = near(i)
            drain(buf.at[gx * nz + zminus(k)], rx.at[k])

        loop(nz - far, nz, take_x)
        drain(buf.at[pl.ds(0, nz)], r["rs"].at[rs])
        drain(buf.at[pl.ds(0, nz)], r["rs"].at[rs + 1])

    def ag_sent(buf, ss):
        drain(buf.at[pl.ds(0, nz - 1)], r["ss"].at[ss])
        for j in range(1, 4):
            drain(buf.at[pl.ds(0, nz)], r["ss"].at[ss + j])

    ag_start(r["ag"], 5, r["rz"].at[0])

    drain(r["infoz"].at[pl.ds(0, nz - 1)], r["rs"].at[3])
    r["t8"][...] = jnp.zeros_like(r["t8"])
    for s in range(srcs):
        src = mp * srcs + s
        r["t8"][s : s + 1, :] = r["infoz"][lax.div(src, GRP), lax.rem(src, GRP)]
    lines = r["t8"][...]
    cols = lines.T
    at = lax.broadcasted_iota(jnp.int32, (cl, ns), 1).astype(F32)
    for s in range(srcs):
        here = slice(s * cl, (s + 1) * cl)
        r["pick"][here, :] = jnp.where(cols[0:cl, s : s + 1] == at, 1.0, 0.0).astype(BF16)
        r["logq"][here, :] = jnp.log(cols[64 : 64 + cl, s : s + 1])
    for s in range(srcs):
        r["c2"][s // 2, :, (s % 2) * cl : (s % 2 + 1) * cl] = lines[s : s + 1, 0:cl]
    row_at = lax.broadcasted_iota(jnp.int32, (ns, 2 * cl), 0).astype(F32)
    for s in range(srcs // 2):
        r["pick_t"][:, 2 * s * cl : 2 * (s + 1) * cl] = jnp.where(r["c2"][s] == row_at, 1.0, 0.0).astype(BF16)
    ag_finish(r["ag"], 5, 5, r["rz"].at[0], r["rx"].at[0], FAR_ITEMS)

    loads["q"].wait()
    items = dot(r["pick"][...], r["ag"][...].reshape(ns, out_w), 1, 0)
    r["items"][...] = items.astype(BF16)
    r["items_t"][...] = items.T.astype(BF16)

    ids = lax.broadcasted_iota(jnp.int32, (nc, QT), 0) + mp * nc

    def score(t):
        where = pl.ds(pl.multiple_of(t * QT, QT), QT)
        sc = dot(r["items"][...], r["q"][where, :], 1, 1) * scale - r["logq"][...]
        top = jnp.max(sc, axis=0, keepdims=True)
        ex = jnp.exp(sc - top)
        r["ex"][t] = ex
        r["st"][0, :, where] = top
        r["st"][1, :, where] = jnp.sum(ex, axis=0, keepdims=True)
        r["sp"][0, :, where] = jnp.sum(jnp.where(ids == r["pos"][:, where], sc, 0.0), axis=0, keepdims=True)

    loop(0, nq // QT, score)
    r["sr"][pl.ds(mp, 1)] = r["st"][...][None]
    r["spr"][pl.ds(mp, 1)] = r["sp"][...]
    for md in columns:
        send(r["st"], r["sr"].at[mp], r["ss"].at[9], r["rs"].at[7], (dp, md))
    for md in columns:
        send(r["sp"].at[0], r["spr"].at[mp], r["ss"].at[2], r["rs"].at[2], (dp, md))
    drain(r["sr"].at[pl.ds(0, n_mp - 1)], r["rs"].at[7])
    top = r["sr"][0, 0]
    for j in range(1, n_mp):
        top = jnp.maximum(top, r["sr"][j, 0])
    total = jnp.zeros_like(top)
    for j in range(n_mp):
        total = total + r["sr"][j, 1] * jnp.exp(r["sr"][j, 0] - top)
    lse = top + jnp.log(total)
    r["loss"][...] = lse
    r["fac"][...] = jnp.exp(r["st"][0] - lse)

    r["ig"][...] = jnp.zeros_like(r["ig"])

    def prob(t):
        where = pl.ds(pl.multiple_of(t * QT, QT), QT)
        pg = r["ex"][t] * r["fac"][:, where] - jnp.where(ids == r["pos"][:, where], 1.0, 0.0)
        pg = pg.astype(BF16)
        r["pg"][t] = pg
        r["ig"][...] += dot(pg, r["q"][where, :], 1, 0)

    loop(0, nq // QT, prob)

    def rs_start(buf, got, ss, rc):
        def go(j):
            xd = lax.rem(x_hi + j, 2)
            gd = xd * 2 + 1 - core
            send(buf.at[pl.ds(gd * nz, nz)], got.at[xd], r["ss"].at[ss], rc.at[xd], to_core)

        go(1)
        go(0)

    def rs_middle(buf, got, out, gotx, ss, rc, rx):
        drain(got.at[1 - x_hi], rc.at[1 - x_hi])
        (outq, outs), (gotq, gots) = out, gotx

        def go(i):
            k = near(nz - 1 - i)
            zz = zplus(k)
            outq[zz], outs[zz] = coded(buf[gx * nz + zz] + got[1 - x_hi, zz], outs.shape[1])
            send(outs.at[zz], gots.at[zz], r["ss"].at[ss + 2], r["rxs"].at[rx, k], to_x)
            send(outq.at[zz], gotq.at[zz], r["ss"].at[ss + 1], r["rx"].at[rx, k], to_x)

        loop(0, nz, go)

    def rs_finish(buf, got, gotx, outz, gotz, own, ss, rs, rc, rx):
        drain(got.at[x_hi], rc.at[x_hi])
        (gotq, gots), (outq, outs), (zq, zs) = gotx, outz, gotz

        def block(k, zz):
            drain(gots.at[zz], r["rxs"].at[rx, k])
            drain(gotq.at[zz], r["rx"].at[rx, k])
            return buf[g * nz + zz] + got[x_hi, zz] + decoded(gotq[zz], gots[zz])

        def go(i):
            k = near(nz - 1 - i)
            zz = zplus(k)
            outq[zz], outs[zz] = coded(block(k, zz), outs.shape[1])
            to = (zz * GRP + g, mp)
            send(outs.at[zz], zs.at[z], r["ss"].at[ss + 4], r["rs"].at[rs + 1], to)
            send(outq.at[zz], zq.at[z], r["ss"].at[ss + 3], r["rs"].at[rs], to)

        loop(0, nz - 1, go)
        own[...] = block(0, z)
        zq[pl.ds(z, 1)] = jnp.zeros((1, *zq.shape[1:]), jnp.int16)
        zs[pl.ds(z, 1)] = jnp.zeros((1, *zs.shape[1:]), F32)

    def rs_result(gotz, own, rs):
        zq, zs = gotz
        drain(zs.at[pl.ds(0, nz - 1)], r["rs"].at[rs + 1])
        drain(zq.at[pl.ds(0, nz - 1)], r["rs"].at[rs])
        total = own[...]
        for i in range(nz):
            total = total + decoded(zq[i], zs[i])
        return total

    def rs_sent(buf, out, outz, ss):
        drain(buf.at[pl.ds(0, 2 * nz)], r["ss"].at[ss])
        drain(out[0], r["ss"].at[ss + 1])
        drain(out[1], r["ss"].at[ss + 2])
        drain(outz[0].at[pl.ds(0, nz - 1)], r["ss"].at[ss + 3])
        drain(outz[1].at[pl.ds(0, nz - 1)], r["ss"].at[ss + 4])

    def pair(name):
        return r[name], r[name + "_s"]

    ig = r["ig"][...] * scale
    hi = ig.astype(BF16)
    lo = (ig - hi.astype(F32)).astype(BF16)
    part = ns // GRP

    def expand(gd):
        pick = r["pick_t"][pl.ds(pl.multiple_of(gd * part, part), part), :]
        r["es"][pl.ds(gd * nz, nz)] = (dot(pick, hi, 1, 0) + dot(pick, lo, 1, 0)).reshape(nz, sm, out_w)

    for xd in (1 - x_hi, x_hi):
        gd = xd * 2 + 1 - core
        expand(gd)
        send(r["es"].at[pl.ds(gd * nz, nz)], r["er"].at[xd], r["ss"].at[10], r["rc"].at[0, xd], to_core)
    expand(gx)
    expand(g)
    rs_middle(r["es"], r["er"], pair("ey"), pair("ex2"), 10, r["rc"].at[0], 1)

    def query(t):
        qg = dot(r["items_t"][...], r["pg"][t], 1, 0) * scale
        for j in range(QT // qb):
            b = t * (QT // qb) + j
            yd, xd = lax.rem(b, NY), lax.div(b, NY)
            r["hs"][yd, xd], r["hs_s"][yd, xd] = coded(qg[:, j * qb : (j + 1) * qb], 1)

    loop(0, nq // QT, query)
    r["hr"][pl.ds(y, 1)] = r["hs"][pl.ds(y, 1)]
    r["hr_s"][pl.ds(y, 1)] = r["hs_s"][pl.ds(y, 1)]
    for j in range(1, NY):
        yd = lax.rem(y + j, NY)
        to = (dp, x_lo * NY + yd)
        send(r["hs_s"].at[yd], r["hr_s"].at[y], r["ss"].at[15], r["rs"].at[10], to)
        send(r["hs"].at[yd], r["hr"].at[y], r["ss"].at[16], r["rs"].at[11], to)
    rs_finish(
        r["es"], r["er"], pair("ex2"), pair("ez"), pair("ezr"), r["e_own"], 10, 8, r["rc"].at[0], 1
    )

    r["igm"][pl.ds(mp, 1)] = rs_result(pair("ezr"), r["e_own"], 8).astype(BF16)[None]
    for md in columns:
        send(r["igm"].at[mp], r["igm"].at[mp], r["ss"].at[19], r["rs"].at[14], (dp, md))

    drain(r["hr_s"].at[pl.ds(0, NY - 1)], r["rs"].at[10])
    drain(r["hr"].at[pl.ds(0, NY - 1)], r["rs"].at[11])
    for j in range(2):
        xd = lax.rem(x_lo + 1 + j, 2)
        q_sum = decoded(r["hr"][0, xd], r["hr_s"][0, xd])
        for i in range(1, NY):
            q_sum = q_sum + decoded(r["hr"][i, xd], r["hr_s"][i, xd])
        if j == 0:
            r["h2"][...], r["h2_s"][...] = coded(q_sum, 1)
            to = (dp, (1 - x_lo) * NY + y)
            send(r["h2_s"], r["h3_s"], r["ss"].at[17], r["rs"].at[12], to)
            send(r["h2"], r["h3"], r["ss"].at[18], r["rs"].at[13], to)
        else:
            r["h_own"][...] = q_sum

    drain(r["igm"].at[pl.ds(0, n_mp - 1)], r["rs"].at[14])

    item_grad = r["igm"][...].reshape(slots, out_w)
    back = dot(item_grad, r["w_out"][...], 1, 1)
    pre_grad = jnp.where(r["pre"][...] > 0.0, back, 0.0)
    pre_bf = pre_grad.astype(BF16)
    gwi = dot(r["emb"][...], pre_bf, 0, 0)
    gwo = dot(r["hid"][...], item_grad, 0, 0)
    gb = jnp.sum(pre_bf.astype(F32), axis=0, keepdims=True)
    hid_w = gb.shape[1]
    nb = emb_w // n_dp
    r["ga"][:, 0:nb, :] = gwi.reshape(n_dp, nb, hid_w)
    r["ga"][:, nb : nb + 8, :] = jnp.zeros((n_dp, 8, hid_w), F32)
    half = hid_w // 8
    r["ga"][0:half, nb : nb + 8, :] = gwo[:, 0:128].reshape(half, 8, 128)
    r["ga"][half : 2 * half, nb : nb + 8, :] = gwo[:, 128:256].reshape(half, 8, 128)
    r["ga"][2 * half, nb : nb + 1, :] = gb
    rs_start(r["ga"], r["gr"], 20, r["rc"].at[1])
    emb_p = dot(pre_bf, r["w_in"][...], 1, 1)
    for j in range(n_mp):
        r["ks"][j] = emb_p[j * sm : (j + 1) * sm]
    r["kr"][pl.ds(mp, 1)] = r["ks"][pl.ds(mp, 1)]
    rs_middle(r["ga"], r["gr"], pair("gy"), pair("gx2"), 20, r["rc"].at[1], 2)
    for md in columns:
        send(r["ks"].at[md], r["kr"].at[mp], r["ss"].at[25], r["rs"].at[15], (dp, md))
    rs_finish(
        r["ga"], r["gr"], pair("gx2"), pair("gz"), pair("gzr"), r["g_own"], 20, 16, r["rc"].at[1], 2
    )

    drain(r["kr"].at[pl.ds(0, n_mp - 1)], r["rs"].at[15])
    emb_own = r["kr"][0]
    for j in range(1, n_mp):
        emb_own = emb_own + r["kr"][j]
    r["eg"][pl.ds(mp, 1)] = emb_own.astype(BF16)[None]
    for md in columns:
        send(r["eg"].at[mp], r["eg"].at[mp], r["ss"].at[26], r["rs"].at[18], (dp, md))

    r["gf"][pl.ds(g * nz + z, 1)] = rs_result(pair("gzr"), r["g_own"], 16).astype(BF16)[None]
    ag_start(r["gf"], 27, r["rz"].at[1])

    def out(name, src):
        copy = pltpu.make_async_copy(src, r[name], r["os"].at[OUTS.index(name)])
        copy.start()
        return copy

    drain(r["spr"].at[pl.ds(0, n_mp - 1)], r["rs"].at[2])
    at_pos = r["spr"][0]
    for j in range(1, n_mp):
        at_pos = at_pos + r["spr"][j]
    r["loss"][...] = r["loss"][...] - at_pos
    done = [out("o_ht", r["ht"]), out("o_loss", r["loss"])]
    drain(r["h3_s"], r["rs"].at[12])
    drain(r["h3"], r["rs"].at[13])
    r["qs"][...] = (r["h_own"][...] + decoded(r["h3"][...], r["h3_s"][...])).T
    done.append(out("o_q", r["qs"]))
    drain(r["eg"].at[pl.ds(0, n_mp - 1)], r["rs"].at[18])
    done.append(out("o_eg", r["eg"]))
    for copy in done:
        copy.wait()

    drain(r["r1s"].at[pl.ds(0, n_dp - 1)], r["ss"].at[0])
    drain(r["infoz"].at[0, pl.ds(0, GRP - 1)], r["ss"].at[1])
    drain(r["infoz"].at[pl.ds(0, nz - 1)], r["ss"].at[3])
    drain(r["bs"].at[pl.ds(0, n_mp - 1)], r["ss"].at[4])
    ag_sent(r["ag"], 5)
    drain(r["sr"].at[pl.ds(0, n_mp - 1)], r["ss"].at[9])
    drain(r["spr"].at[pl.ds(0, n_mp - 1)], r["ss"].at[2])
    rs_sent(r["es"], pair("ey"), pair("ez"), 10)
    drain(r["hs_s"].at[pl.ds(0, NY - 1)], r["ss"].at[15])
    drain(r["hs"].at[pl.ds(0, NY - 1)], r["ss"].at[16])
    drain(r["h2_s"], r["ss"].at[17])
    drain(r["h2"], r["ss"].at[18])
    drain(r["igm"].at[pl.ds(0, n_mp - 1)], r["ss"].at[19])
    rs_sent(r["ga"], pair("gy"), pair("gz"), 20)
    drain(r["ks"].at[pl.ds(0, n_mp - 1)], r["ss"].at[25])
    drain(r["eg"].at[pl.ds(0, n_mp - 1)], r["ss"].at[26])

    ag_finish(r["gf"], 27, 19, r["rz"].at[1], r["rx"].at[3], FAR_SUMS)
    last = out("o_gf", r["gf"])
    ag_sent(r["gf"], 27)
    last.wait()


def results_kernel(names, *refs):
    r = dict(zip(names, refs))
    n_dp, gr, hid_w = r["gf"].shape
    nb = gr - 8
    rows_dev, emb_w = r["v_table"].shape
    slots = r["eg"].shape[0] * r["eg"].shape[1]
    half = hid_w // 8
    loads = [pltpu.make_async_copy(r["i_" + n], r[n], r["ls"].at[i]) for i, n in enumerate(MIDS)]
    for copy in loads:
        copy.start()
    stores = []

    def put(name, i, rows=slice(None)):
        copy = pltpu.make_async_copy(r["v_" + name].at[rows], r["g_" + name].at[rows], r["os"].at[i])
        copy.start()
        stores.append(copy)

    loads[0].wait()
    loads[1].wait()
    eg = r["eg"][...].reshape(slots, emb_w)
    step = rows_dev // TABLE_PARTS
    for i in range(TABLE_PARTS):
        rows = pl.ds(i * step, step)
        r["v_table"][rows, :] = dot(r["ht"][rows, 0:slots], eg, 1, 0)
        put("table", i, rows)
    loads[2].wait()
    gf = r["gf"][...].astype(F32)
    r["v_wi"][...] = gf[:, 0:nb, :].reshape(emb_w, hid_w)
    put("wi", TABLE_PARTS)
    r["v_wo"][:, 0:128] = gf[0:half, nb : nb + 8, :].reshape(hid_w, 128)
    r["v_wo"][:, 128:256] = gf[half : 2 * half, nb : nb + 8, :].reshape(hid_w, 128)
    put("wo", TABLE_PARTS + 1)
    r["v_b"][...] = gf[2 * half, nb : nb + 1, :]
    put("b", TABLE_PARTS + 2)
    loads[3].wait()
    r["v_q"][...] = r["q"][...]
    put("q", TABLE_PARTS + 3)
    loads[4].wait()
    r["v_loss"][...] = r["loss"][...]
    put("loss", TABLE_PARTS + 4)
    for copy in stores:
        copy.wait()


def per_device(queries, item_table, cand_row, cand_owner, cand_count, positive, w_in, b_in, w_out):
    n_dp, n_mp = lax.axis_size("dp"), lax.axis_size("mp")
    nz = n_dp // GRP
    cl = cand_row.shape[0]
    nq, out_w = queries.shape
    rows_dev, emb_w = item_table.shape
    hid_w = w_in.shape[1]
    slots = 2 * n_dp
    sm = slots // n_mp
    srcs = n_dp // n_mp
    nc = srcs * cl
    ns = n_dp * sm
    qb = nq // n_mp
    nt = nq // QT
    gr = emb_w // n_dp + 8
    ins = dict(
        own=cand_owner.reshape(1, cl), row=cand_row[None, :], cnt=cand_count[None, :],
        pos=positive[None, :], b_in=b_in[None, :],
    )
    far = dict(table_in=item_table, w_in_in=w_in, w_out_in=w_out, q_in=queries)
    mids = dict(
        o_loss=((1, nq), F32), o_q=((qb, out_w), F32), o_gf=((n_dp, gr, hid_w), BF16),
        o_ht=((rows_dev, 128), BF16), o_eg=((n_mp, sm, emb_w), BF16),
    )
    outs = dict(
        g_loss=((1, nq), F32), g_q=((qb, out_w), F32), g_wi=((emb_w, hid_w), F32),
        g_b=((1, hid_w), F32), g_wo=((hid_w, out_w), F32), g_table=((rows_dev, emb_w), F32),
    )
    vmem = dict(
        q=((nq, out_w), BF16), table=((rows_dev, emb_w), BF16), w_in=((emb_w, hid_w), BF16),
        w_out=((hid_w, out_w), BF16), loss=((1, nq), F32), qs=((qb, out_w), F32),
        r1s=((n_dp, 1, 128), F32), i1=((1, 128), F32),
        infoz=((nz, GRP, 1, 128), F32), rq=((n_dp, 1, 128), F32),
        ht=((rows_dev, 128), BF16), emb=((slots, emb_w), BF16), pre=((slots, hid_w), F32),
        hid=((slots, hid_w), BF16), bs=((n_mp, sm, out_w), F32), br=((n_mp, sm, out_w), F32),
        ag=((n_dp, sm, out_w), BF16), t8=((8, 128), F32), pick=((nc, ns), BF16), pick_t=((ns, nc), BF16), c2=((srcs // 2, 1, 2 * cl), F32), logq=((nc, 1), F32),
        items=((nc, out_w), BF16), items_t=((out_w, nc), BF16), ex=((nt, nc, QT), F32),
        st=((2, 1, nq), F32), sr=((n_mp, 2, 1, nq), F32), sp=((1, 1, nq), F32), spr=((n_mp, 1, nq), F32), fac=((1, nq), F32),
        pg=((nt, nc, QT), BF16), ig=((nc, out_w), F32),
        es=((n_dp, sm, out_w), F32), er=((2, nz, sm, out_w), F32), e_own=((sm, out_w), F32),
        h_own=((out_w, qb), F32), igm=((n_mp, sm, out_w), BF16),
        ga=((n_dp, gr, hid_w), F32), gr=((2, nz, gr, hid_w), F32), g_own=((gr, hid_w), F32),
        gf=((n_dp, gr, hid_w), BF16),
        ks=((n_mp, sm, emb_w), F32), kr=((n_mp, sm, emb_w), F32), eg=((n_mp, sm, emb_w), BF16),
    )
    fixed = dict(
        ey=((nz,), (sm, out_w), 1), ex2=((nz,), (sm, out_w), 1), ez=((nz,), (sm, out_w), 1),
        ezr=((nz,), (sm, out_w), 1), gy=((nz,), (gr, hid_w), 2), gx2=((nz,), (gr, hid_w), 2),
        gz=((nz,), (gr, hid_w), 2), gzr=((nz,), (gr, hid_w), 2), hs=((NY, 2), (out_w, qb), 1),
        hr=((NY, 2), (out_w, qb), 1), h2=((), (out_w, qb), 1), h3=((), (out_w, qb), 1),
    )
    for name, (lead, block, tiles) in fixed.items():
        vmem[name] = ((*lead, *block), jnp.int16)
        vmem[name + "_s"] = ((*lead, tiles, 1, block[1]), F32)
    sems = dict(ss=(31,), rs=(21,), rz=(2, nz), rx=(4, nz), rxs=(4, nz), rc=(2, 2), ls=(4,), os=(5,))
    names = (*ins, *far, *mids, *vmem, *sems)
    whole = pl.BlockSpec(memory_space=pltpu.VMEM)
    there = pl.BlockSpec(memory_space=pl.ANY)
    loss, qs, gf, ht, eg = pl.pallas_call(
        functools.partial(step_kernel, n_dp, n_mp, names),
        out_shape=[jax.ShapeDtypeStruct(*s) for s in mids.values()],
        in_specs=[whole] * len(ins) + [there] * len(far),
        out_specs=[there] * len(mids),
        scratch_shapes=[pltpu.VMEM(*s) for s in vmem.values()]
        + [pltpu.SemaphoreType.DMA(s) for s in sems.values()],
        compiler_params=pltpu.CompilerParams(
            collective_id=0, has_side_effects=True, vmem_limit_bytes=VMEM_BYTES
        ),
    )(*ins.values(), *far.values())
    middle = {n: mids["o_" + n] for n in MIDS}
    held = {"v" + n[1:]: v for n, v in outs.items()}
    names = (*("i_" + n for n in MIDS), *outs, *middle, *held, "ls", "os")
    loss, g_q, g_wi, g_b, g_wo, g_table = pl.pallas_call(
        functools.partial(results_kernel, names),
        out_shape=[jax.ShapeDtypeStruct(*s) for s in outs.values()],
        in_specs=[there] * 5,
        out_specs=[there] * len(outs),
        scratch_shapes=[pltpu.VMEM(*s) for s in (*middle.values(), *held.values())]
        + [pltpu.SemaphoreType.DMA((5,)), pltpu.SemaphoreType.DMA((TABLE_PARTS + 5,))],
        compiler_params=pltpu.CompilerParams(vmem_limit_bytes=VMEM_BYTES),
    )(eg, ht, gf, qs, loss)
    return loss.reshape(nq), g_q, g_wi, g_b.reshape(hid_w), g_wo, g_table


def solution(mesh):
    placed = (
        P("dp", None),
        P("dp", None),
        P("dp"),
        P("dp", None),
        P("dp"),
        P("dp"),
        P(None, "mp"),
        P("mp"),
        P("mp", None),
    )
    return jax.shard_map(
        per_device,
        mesh=mesh,
        in_specs=placed,
        out_specs=(
            P("dp"),
            P(("dp", "mp"), None),
            P(None, "mp"),
            P("mp"),
            P("mp", None),
            P("dp", None),
        ),
        check_vma=False,
    )
```

```python
import functools
import math

import jax
import jax.numpy as jnp
from jax import lax
from jax.experimental import pallas as pl
from jax.experimental.pallas import tpu as pltpu
from jax.sharding import PartitionSpec as P

MESH = pl.DeviceIdType.MESH
F32 = jnp.float32
BF16 = jnp.bfloat16
GRP = 4
QT = 1024
VMEM_BYTES = 64_000_000
TABLE_PARTS = 4
MIDS = ("eg", "ht", "gf", "q", "loss")
OUTS = ("o_loss", "o_q", "o_gf", "o_ht", "o_eg")
FIXED = 32767.0
FAR_ITEMS, FAR_SUMS = 0, 2
NY = 4


def dot(a, b, ca, cb):
    return lax.dot_general(a, b, (((ca,), (cb,)), ((), ())), preferred_element_type=F32)


def drain(ref, sem):
    pltpu.make_async_copy(ref, ref, sem).wait()


def coded(v, tiles):
    rows, width = v.shape[-2], v.shape[-1]
    t = v.reshape(tiles, rows // tiles, width)
    top = jnp.max(jnp.abs(t), axis=1, keepdims=True)
    fixed = t * (FIXED / jnp.maximum(top, 1e-30))
    fixed = jnp.round(fixed).reshape(rows, width).astype(jnp.int32).astype(jnp.int16)
    return fixed, top * (1.0 / FIXED)


def decoded(fixed, scales):
    rows, width = fixed.shape
    tiles = scales.shape[0]
    v = fixed.astype(jnp.int32).astype(F32).reshape(tiles, rows // tiles, width)
    return (v * scales).reshape(rows, width)


def step_kernel(n_dp, n_mp, names, *refs):
    r = dict(zip(names, refs))
    nz = n_dp // GRP
    dp, mp = lax.axis_index("dp"), lax.axis_index("mp")
    z, g = lax.div(dp, GRP), lax.rem(dp, GRP)
    core, x_hi = lax.rem(g, 2), lax.div(g, 2)
    gc = x_hi * 2 + (1 - core)
    gx = lax.rem(g + 2, GRP)
    to_core, to_x = (z * GRP + gc, mp), (z * GRP + gx, mp)
    to_diag = (z * GRP + lax.rem(gc + 2, GRP), mp)
    cl = r["own"].shape[1]
    slots = 2 * n_dp
    sm = slots // n_mp
    srcs = n_dp // n_mp
    nc = srcs * cl
    ns = n_dp * sm
    emb_w = r["table"].shape[1]
    out_w = r["q"].shape[1]
    nq = r["q"].shape[0]
    scale = 1.0 / math.sqrt(out_w)
    qb = nq // n_mp

    def near(i):
        odd = lax.rem(i, 2)
        return odd * lax.div(i + 1, 2) + (1 - odd) * lax.rem(nz - lax.div(i, 2), nz)

    def zplus(k):
        return lax.rem(z + k, nz)

    def zminus(k):
        return lax.rem(z + nz - k, nz)

    def send(src, dst, ssem, rsem, dev):
        pltpu.make_async_remote_copy(
            src_ref=src, dst_ref=dst, send_sem=ssem, recv_sem=rsem, device_id=dev, device_id_type=MESH
        ).start()

    def loop(lo, hi, body):
        def step(i, c):
            body(i)
            return c

        lax.fori_loop(lo, hi, step, 0)

    x_lo, y = lax.div(mp, NY), lax.rem(mp, NY)
    columns = [
        (1 - x_lo) * NY + lax.rem(y + j, NY) if far else x_lo * NY + lax.rem(y + j, NY)
        for far in (True, False) for j in (2, 1, 3, 0) if far or j
    ]
    loads = {}
    for i, name in enumerate(("table", "w_in", "w_out", "q")):
        loads[name] = pltpu.make_async_copy(r[name + "_in"], r[name], r["ls"].at[i])

    barrier = pltpu.get_barrier_semaphore()

    def greet(dev):
        pl.semaphore_signal(barrier, inc=1, device_id=dev, device_id_type=MESH)

    def greet_z(i):
        zd = zplus(near(nz - 1 - i))
        for j in range(GRP):
            greet((zd * GRP + lax.rem(g + j, GRP), mp))

    loop(0, nz - 1, greet_z)
    for j in range(1, GRP):
        greet((z * GRP + lax.rem(g + j, GRP), mp))
    for j in range(1, n_mp):
        greet((dp, lax.rem(mp + j, n_mp)))

    for name in loads:
        loads[name].start()

    r["t8"][...] = jnp.full_like(r["t8"], -1.0)
    r["t8"][0:1, 0:cl] = r["own"][...].astype(F32)
    r["t8"][1:2, 0:cl] = r["row"][...].astype(F32)
    cand = r["t8"][...]
    own_col = cand.T[0:cl, 0:1]
    lane = lax.broadcasted_iota(jnp.int32, (n_dp, 128), 1)
    sub = lax.broadcasted_iota(jnp.int32, (n_dp, 128), 0)
    earlier = (own_col == cand[0:1, :]) & (
        lax.broadcasted_iota(jnp.int32, (cl, 128), 0) < lax.broadcasted_iota(jnp.int32, (cl, 128), 1)
    )
    rank = jnp.sum(jnp.where(earlier, 1.0, 0.0), axis=0, keepdims=True)
    owner = cand[0:1, :].astype(jnp.int32)
    mine = sub == owner
    row1 = cand[1:2, :] + 1.0
    first = jnp.sum(jnp.where(mine & (rank < 0.5), row1, 0.0), axis=1, keepdims=True)
    second = jnp.sum(jnp.where(mine & (rank > 0.5), row1, 0.0), axis=1, keepdims=True)
    asked = jnp.where(lane == 2 * dp, first, jnp.where(lane == 2 * dp + 1, second, 0.0))
    r["r1s"][...] = asked.reshape(n_dp, 1, 128)
    r["rq"][pl.ds(dp, 1)] = r["r1s"][pl.ds(dp, 1)]
    code = (
        ((owner & (GRP - 1)) * nz + lax.shift_right_logical(owner, 2)) * sm + lax.rem(dp, srcs) * 2
    ).astype(F32) + rank
    r["i1"][0:1, :] = code
    r["i1"][0:1, 64 : 64 + cl] = r["cnt"][...].astype(F32)
    r["infoz"][pl.ds(z, 1), pl.ds(g, 1)] = r["i1"][...][None, None]

    pl.semaphore_wait(barrier, n_dp - 1 + n_mp - 1)

    def ask(zd, j):
        to = zd * GRP + lax.rem(g + j, GRP)
        send(r["r1s"].at[to], r["rq"].at[dp], r["ss"].at[0], r["rs"].at[0], (to, mp))

    def ask_z(i):
        for j in range(GRP):
            ask(zplus(near(nz - 1 - i)), j)

    loop(0, nz - 1, ask_z)
    for j in range(1, GRP):
        ask(z, j)
    for j in range(1, GRP):
        gd = lax.rem(g + j, GRP)
        send(r["i1"], r["infoz"].at[z, g], r["ss"].at[1], r["rs"].at[1], (z * GRP + gd, mp))
    drain(r["infoz"].at[0, pl.ds(0, GRP - 1)], r["rs"].at[1])

    def tell(i):
        zd = zplus(near(nz - 1 - i))
        send(r["infoz"].at[z], r["infoz"].at[z], r["ss"].at[3], r["rs"].at[3], (zd * GRP + g, mp))

    loop(0, nz - 1, tell)
    drain(r["rq"].at[pl.ds(0, n_dp - 1)], r["rs"].at[0])

    asked_row = jnp.sum(r["rq"][...], axis=0)
    for name in ("table", "w_in", "w_out"):
        loads[name].wait()
    rows_dev = r["table"].shape[0]
    hits = lax.broadcasted_iota(jnp.int32, (rows_dev, 128), 0).astype(F32) + 1.0 == asked_row
    r["ht"][...] = jnp.where(hits, 1.0, 0.0).astype(BF16)
    emb = dot(r["ht"][...], r["table"][...], 0, 0)[:slots].astype(BF16)
    r["emb"][...] = emb
    pre = dot(emb, r["w_in"][...], 1, 0) + r["b_in"][...]
    r["pre"][...] = pre
    hidden = jnp.maximum(pre, 0.0).astype(BF16)
    r["hid"][...] = hidden
    item_p = dot(hidden, r["w_out"][...], 1, 0)
    for j in range(n_mp):
        r["bs"][j] = item_p[j * sm : (j + 1) * sm]
    r["br"][pl.ds(mp, 1)] = r["bs"][pl.ds(mp, 1)]
    for md in columns:
        send(r["bs"].at[md], r["br"].at[mp], r["ss"].at[4], r["rs"].at[4], (dp, md))
    drain(r["br"].at[pl.ds(0, n_mp - 1)], r["rs"].at[4])
    item_own = r["br"][0]
    for j in range(1, n_mp):
        item_own = item_own + r["br"][j]
    r["ag"][pl.ds(g * nz + z, 1)] = item_own.astype(BF16)[None]

    def ag_start(buf, ss, rz):
        own = g * nz + z

        def go(i):
            k = near(nz - 1 - i)
            send(buf.at[own], buf.at[own], r["ss"].at[ss], rz.at[k], (zplus(k) * GRP + g, mp))

        loop(0, nz - 1, go)

    def ag_finish(buf, ss, rs, rz, rx, far):
        own = g * nz + z

        def pass_on(k, b):
            send(buf.at[b], buf.at[b], r["ss"].at[ss + 1], rx.at[k], to_x)
            send(buf.at[b], buf.at[b], r["ss"].at[ss + 2], r["rs"].at[rs], to_core)

        pass_on(0, own)

        def relay(i):
            k = near(i)
            b = g * nz + zminus(k)
            drain(buf.at[b], rz.at[k])
            pass_on(k, b)
            return b

        def relay_far(i):
            b = relay(i)
            send(buf.at[b], buf.at[b], r["ss"].at[ss + 3], r["rs"].at[rs + 1], to_diag)

        loop(1, nz - far, relay)
        loop(nz - far, nz, relay_far)

        def relay_x(i):
            k = near(i)
            b = gx * nz + zminus(k)
            drain(buf.at[b], rx.at[k])
            send(buf.at[b], buf.at[b], r["ss"].at[ss + 3], r["rs"].at[rs + 1], to_core)

        loop(0, nz - far, relay_x)

        def take_x(i):
            k = near(i)
            drain(buf.at[gx * nz + zminus(k)], rx.at[k])

        loop(nz - far, nz, take_x)
        drain(buf.at[pl.ds(0, nz)], r["rs"].at[rs])
        drain(buf.at[pl.ds(0, nz)], r["rs"].at[rs + 1])

    def ag_sent(buf, ss):
        drain(buf.at[pl.ds(0, nz - 1)], r["ss"].at[ss])
        for j in range(1, 4):
            drain(buf.at[pl.ds(0, nz)], r["ss"].at[ss + j])

    ag_start(r["ag"], 5, r["rz"].at[0])

    drain(r["infoz"].at[pl.ds(0, nz - 1)], r["rs"].at[3])
    r["t8"][...] = jnp.zeros_like(r["t8"])
    for s in range(srcs):
        src = mp * srcs + s
        r["t8"][s : s + 1, :] = r["infoz"][lax.div(src, GRP), lax.rem(src, GRP)]
    lines = r["t8"][...]
    cols = lines.T
    at = lax.broadcasted_iota(jnp.int32, (cl, ns), 1).astype(F32)
    for s in range(srcs):
        here = slice(s * cl, (s + 1) * cl)
        r["pick"][here, :] = jnp.where(cols[0:cl, s : s + 1] == at, 1.0, 0.0).astype(BF16)
        r["logq"][here, :] = jnp.log(cols[64 : 64 + cl, s : s + 1])
    for s in range(srcs):
        r["c2"][s // 2, :, (s % 2) * cl : (s % 2 + 1) * cl] = lines[s : s + 1, 0:cl]
    row_at = lax.broadcasted_iota(jnp.int32, (ns, 2 * cl), 0).astype(F32)
    for s in range(srcs // 2):
        r["pick_t"][:, 2 * s * cl : 2 * (s + 1) * cl] = jnp.where(r["c2"][s] == row_at, 1.0, 0.0).astype(BF16)
    ag_finish(r["ag"], 5, 5, r["rz"].at[0], r["rx"].at[0], FAR_ITEMS)

    loads["q"].wait()
    items = dot(r["pick"][...], r["ag"][...].reshape(ns, out_w), 1, 0)
    r["items"][...] = items.astype(BF16)
    r["items_t"][...] = items.T.astype(BF16)

    ids = lax.broadcasted_iota(jnp.int32, (nc, QT), 0) + mp * nc

    def score(t):
        where = pl.ds(pl.multiple_of(t * QT, QT), QT)
        sc = dot(r["items"][...], r["q"][where, :], 1, 1) * scale - r["logq"][...]
        top = jnp.max(sc, axis=0, keepdims=True)
        ex = jnp.exp(sc - top)
        r["ex"][t] = ex
        r["st"][0, :, where] = top
        r["st"][1, :, where] = jnp.sum(ex, axis=0, keepdims=True)
        r["sp"][0, :, where] = jnp.sum(jnp.where(ids == r["pos"][:, where], sc, 0.0), axis=0, keepdims=True)

    loop(0, nq // QT, score)
    r["sr"][pl.ds(mp, 1)] = r["st"][...][None]
    r["spr"][pl.ds(mp, 1)] = r["sp"][...]
    for md in columns:
        send(r["st"], r["sr"].at[mp], r["ss"].at[9], r["rs"].at[7], (dp, md))
    for md in columns:
        send(r["sp"].at[0], r["spr"].at[mp], r["ss"].at[2], r["rs"].at[2], (dp, md))
    drain(r["sr"].at[pl.ds(0, n_mp - 1)], r["rs"].at[7])
    top = r["sr"][0, 0]
    for j in range(1, n_mp):
        top = jnp.maximum(top, r["sr"][j, 0])
    total = jnp.zeros_like(top)
    for j in range(n_mp):
        total = total + r["sr"][j, 1] * jnp.exp(r["sr"][j, 0] - top)
    lse = top + jnp.log(total)
    r["loss"][...] = lse
    r["fac"][...] = jnp.exp(r["st"][0] - lse)

    r["ig"][...] = jnp.zeros_like(r["ig"])

    def prob(t):
        where = pl.ds(pl.multiple_of(t * QT, QT), QT)
        pg = r["ex"][t] * r["fac"][:, where] - jnp.where(ids == r["pos"][:, where], 1.0, 0.0)
        pg = pg.astype(BF16)
        r["pg"][t] = pg
        r["ig"][...] += dot(pg, r["q"][where, :], 1, 0)

    loop(0, nq // QT, prob)

    def rs_start(buf, got, ss, rc):
        def go(j):
            xd = lax.rem(x_hi + j, 2)
            gd = xd * 2 + 1 - core
            send(buf.at[pl.ds(gd * nz, nz)], got.at[xd], r["ss"].at[ss], rc.at[xd], to_core)

        go(1)
        go(0)

    def rs_middle(buf, got, out, gotx, ss, rc, rx):
        drain(got.at[1 - x_hi], rc.at[1 - x_hi])
        (outq, outs), (gotq, gots) = out, gotx

        def go(i):
            k = near(nz - 1 - i)
            zz = zplus(k)
            outq[zz], outs[zz] = coded(buf[gx * nz + zz] + got[1 - x_hi, zz], outs.shape[1])
            send(outs.at[zz], gots.at[zz], r["ss"].at[ss + 2], r["rxs"].at[rx, k], to_x)
            send(outq.at[zz], gotq.at[zz], r["ss"].at[ss + 1], r["rx"].at[rx, k], to_x)

        loop(0, nz, go)

    def rs_finish(buf, got, gotx, outz, gotz, own, ss, rs, rc, rx):
        drain(got.at[x_hi], rc.at[x_hi])
        (gotq, gots), (outq, outs), (zq, zs) = gotx, outz, gotz

        def block(k, zz):
            drain(gots.at[zz], r["rxs"].at[rx, k])
            drain(gotq.at[zz], r["rx"].at[rx, k])
            return buf[g * nz + zz] + got[x_hi, zz] + decoded(gotq[zz], gots[zz])

        def go(i):
            k = near(nz - 1 - i)
            zz = zplus(k)
            outq[zz], outs[zz] = coded(block(k, zz), outs.shape[1])
            to = (zz * GRP + g, mp)
            send(outs.at[zz], zs.at[z], r["ss"].at[ss + 4], r["rs"].at[rs + 1], to)
            send(outq.at[zz], zq.at[z], r["ss"].at[ss + 3], r["rs"].at[rs], to)

        loop(0, nz - 1, go)
        own[...] = block(0, z)
        zq[pl.ds(z, 1)] = jnp.zeros((1, *zq.shape[1:]), jnp.int16)
        zs[pl.ds(z, 1)] = jnp.zeros((1, *zs.shape[1:]), F32)

    def rs_result(gotz, own, rs):
        zq, zs = gotz
        drain(zs.at[pl.ds(0, nz - 1)], r["rs"].at[rs + 1])
        drain(zq.at[pl.ds(0, nz - 1)], r["rs"].at[rs])
        total = own[...]
        for i in range(nz):
            total = total + decoded(zq[i], zs[i])
        return total

    def rs_sent(buf, out, outz, ss):
        drain(buf.at[pl.ds(0, 2 * nz)], r["ss"].at[ss])
        drain(out[0], r["ss"].at[ss + 1])
        drain(out[1], r["ss"].at[ss + 2])
        drain(outz[0].at[pl.ds(0, nz - 1)], r["ss"].at[ss + 3])
        drain(outz[1].at[pl.ds(0, nz - 1)], r["ss"].at[ss + 4])

    def pair(name):
        return r[name], r[name + "_s"]

    ig = r["ig"][...] * scale
    hi = ig.astype(BF16)
    lo = (ig - hi.astype(F32)).astype(BF16)
    part = ns // GRP

    def expand(gd):
        pick = r["pick_t"][pl.ds(pl.multiple_of(gd * part, part), part), :]
        r["es"][pl.ds(gd * nz, nz)] = (dot(pick, hi, 1, 0) + dot(pick, lo, 1, 0)).reshape(nz, sm, out_w)

    for xd in (1 - x_hi, x_hi):
        gd = xd * 2 + 1 - core
        expand(gd)
        send(r["es"].at[pl.ds(gd * nz, nz)], r["er"].at[xd], r["ss"].at[10], r["rc"].at[0, xd], to_core)
    expand(gx)
    expand(g)
    rs_middle(r["es"], r["er"], pair("ey"), pair("ex2"), 10, r["rc"].at[0], 1)

    def query(t):
        qg = dot(r["items_t"][...], r["pg"][t], 1, 0) * scale
        for j in range(QT // qb):
            b = t * (QT // qb) + j
            yd, xd = lax.rem(b, NY), lax.div(b, NY)
            r["hs"][yd, xd], r["hs_s"][yd, xd] = coded(qg[:, j * qb : (j + 1) * qb], 1)

    loop(0, nq // QT, query)
    r["hr"][pl.ds(y, 1)] = r["hs"][pl.ds(y, 1)]
    r["hr_s"][pl.ds(y, 1)] = r["hs_s"][pl.ds(y, 1)]
    for j in range(1, NY):
        yd = lax.rem(y + j, NY)
        to = (dp, x_lo * NY + yd)
        send(r["hs_s"].at[yd], r["hr_s"].at[y], r["ss"].at[15], r["rs"].at[10], to)
        send(r["hs"].at[yd], r["hr"].at[y], r["ss"].at[16], r["rs"].at[11], to)
    rs_finish(
        r["es"], r["er"], pair("ex2"), pair("ez"), pair("ezr"), r["e_own"], 10, 8, r["rc"].at[0], 1
    )

    r["igm"][pl.ds(mp, 1)] = rs_result(pair("ezr"), r["e_own"], 8).astype(BF16)[None]
    for md in columns:
        send(r["igm"].at[mp], r["igm"].at[mp], r["ss"].at[19], r["rs"].at[14], (dp, md))

    drain(r["hr_s"].at[pl.ds(0, NY - 1)], r["rs"].at[10])
    drain(r["hr"].at[pl.ds(0, NY - 1)], r["rs"].at[11])
    for j in range(2):
        xd = lax.rem(x_lo + 1 + j, 2)
        q_sum = decoded(r["hr"][0, xd], r["hr_s"][0, xd])
        for i in range(1, NY):
            q_sum = q_sum + decoded(r["hr"][i, xd], r["hr_s"][i, xd])
        if j == 0:
            r["h2"][...], r["h2_s"][...] = coded(q_sum, 1)
            to = (dp, (1 - x_lo) * NY + y)
            send(r["h2_s"], r["h3_s"], r["ss"].at[17], r["rs"].at[12], to)
            send(r["h2"], r["h3"], r["ss"].at[18], r["rs"].at[13], to)
        else:
            r["h_own"][...] = q_sum

    drain(r["igm"].at[pl.ds(0, n_mp - 1)], r["rs"].at[14])

    item_grad = r["igm"][...].reshape(slots, out_w)
    back = dot(item_grad, r["w_out"][...], 1, 1)
    pre_grad = jnp.where(r["pre"][...] > 0.0, back, 0.0)
    pre_bf = pre_grad.astype(BF16)
    gwi = dot(r["emb"][...], pre_bf, 0, 0)
    gwo = dot(r["hid"][...], item_grad, 0, 0)
    gb = jnp.sum(pre_bf.astype(F32), axis=0, keepdims=True)
    hid_w = gb.shape[1]
    nb = emb_w // n_dp
    r["ga"][:, 0:nb, :] = gwi.reshape(n_dp, nb, hid_w)
    r["ga"][:, nb : nb + 8, :] = jnp.zeros((n_dp, 8, hid_w), F32)
    half = hid_w // 8
    r["ga"][0:half, nb : nb + 8, :] = gwo[:, 0:128].reshape(half, 8, 128)
    r["ga"][half : 2 * half, nb : nb + 8, :] = gwo[:, 128:256].reshape(half, 8, 128)
    r["ga"][2 * half, nb : nb + 1, :] = gb
    rs_start(r["ga"], r["gr"], 20, r["rc"].at[1])
    emb_p = dot(pre_bf, r["w_in"][...], 1, 1)
    for j in range(n_mp):
        r["ks"][j] = emb_p[j * sm : (j + 1) * sm]
    r["kr"][pl.ds(mp, 1)] = r["ks"][pl.ds(mp, 1)]
    rs_middle(r["ga"], r["gr"], pair("gy"), pair("gx2"), 20, r["rc"].at[1], 2)
    for md in columns:
        send(r["ks"].at[md], r["kr"].at[mp], r["ss"].at[25], r["rs"].at[15], (dp, md))
    rs_finish(
        r["ga"], r["gr"], pair("gx2"), pair("gz"), pair("gzr"), r["g_own"], 20, 16, r["rc"].at[1], 2
    )

    drain(r["kr"].at[pl.ds(0, n_mp - 1)], r["rs"].at[15])
    emb_own = r["kr"][0]
    for j in range(1, n_mp):
        emb_own = emb_own + r["kr"][j]
    r["eg"][pl.ds(mp, 1)] = emb_own.astype(BF16)[None]
    for md in columns:
        send(r["eg"].at[mp], r["eg"].at[mp], r["ss"].at[26], r["rs"].at[18], (dp, md))

    r["gf"][pl.ds(g * nz + z, 1)] = rs_result(pair("gzr"), r["g_own"], 16).astype(BF16)[None]
    ag_start(r["gf"], 27, r["rz"].at[1])

    def out(name, src):
        copy = pltpu.make_async_copy(src, r[name], r["os"].at[OUTS.index(name)])
        copy.start()
        return copy

    drain(r["spr"].at[pl.ds(0, n_mp - 1)], r["rs"].at[2])
    at_pos = r["spr"][0]
    for j in range(1, n_mp):
        at_pos = at_pos + r["spr"][j]
    r["loss"][...] = r["loss"][...] - at_pos
    done = [out("o_ht", r["ht"]), out("o_loss", r["loss"])]
    drain(r["h3_s"], r["rs"].at[12])
    drain(r["h3"], r["rs"].at[13])
    r["qs"][...] = (r["h_own"][...] + decoded(r["h3"][...], r["h3_s"][...])).T
    done.append(out("o_q", r["qs"]))
    drain(r["eg"].at[pl.ds(0, n_mp - 1)], r["rs"].at[18])
    done.append(out("o_eg", r["eg"]))
    for copy in done:
        copy.wait()

    drain(r["r1s"].at[pl.ds(0, n_dp - 1)], r["ss"].at[0])
    drain(r["infoz"].at[0, pl.ds(0, GRP - 1)], r["ss"].at[1])
    drain(r["infoz"].at[pl.ds(0, nz - 1)], r["ss"].at[3])
    drain(r["bs"].at[pl.ds(0, n_mp - 1)], r["ss"].at[4])
    ag_sent(r["ag"], 5)
    drain(r["sr"].at[pl.ds(0, n_mp - 1)], r["ss"].at[9])
    drain(r["spr"].at[pl.ds(0, n_mp - 1)], r["ss"].at[2])
    rs_sent(r["es"], pair("ey"), pair("ez"), 10)
    drain(r["hs_s"].at[pl.ds(0, NY - 1)], r["ss"].at[15])
    drain(r["hs"].at[pl.ds(0, NY - 1)], r["ss"].at[16])
    drain(r["h2_s"], r["ss"].at[17])
    drain(r["h2"], r["ss"].at[18])
    drain(r["igm"].at[pl.ds(0, n_mp - 1)], r["ss"].at[19])
    rs_sent(r["ga"], pair("gy"), pair("gz"), 20)
    drain(r["ks"].at[pl.ds(0, n_mp - 1)], r["ss"].at[25])
    drain(r["eg"].at[pl.ds(0, n_mp - 1)], r["ss"].at[26])

    ag_finish(r["gf"], 27, 19, r["rz"].at[1], r["rx"].at[3], FAR_SUMS)
    last = out("o_gf", r["gf"])
    ag_sent(r["gf"], 27)
    last.wait()


def results_kernel(names, *refs):
    r = dict(zip(names, refs))
    n_dp, gr, hid_w = r["gf"].shape
    nb = gr - 8
    rows_dev, emb_w = r["v_table"].shape
    slots = r["eg"].shape[0] * r["eg"].shape[1]
    half = hid_w // 8
    loads = [pltpu.make_async_copy(r["i_" + n], r[n], r["ls"].at[i]) for i, n in enumerate(MIDS)]
    for copy in loads:
        copy.start()
    stores = []

    def put(name, i, rows=slice(None)):
        copy = pltpu.make_async_copy(r["v_" + name].at[rows], r["g_" + name].at[rows], r["os"].at[i])
        copy.start()
        stores.append(copy)

    loads[0].wait()
    loads[1].wait()
    eg = r["eg"][...].reshape(slots, emb_w)
    step = rows_dev // TABLE_PARTS
    for i in range(TABLE_PARTS):
        rows = pl.ds(i * step, step)
        r["v_table"][rows, :] = dot(r["ht"][rows, 0:slots], eg, 1, 0)
        put("table", i, rows)
    loads[2].wait()
    gf = r["gf"][...].astype(F32)
    r["v_wi"][...] = gf[:, 0:nb, :].reshape(emb_w, hid_w)
    put("wi", TABLE_PARTS)
    r["v_wo"][:, 0:128] = gf[0:half, nb : nb + 8, :].reshape(hid_w, 128)
    r["v_wo"][:, 128:256] = gf[half : 2 * half, nb : nb + 8, :].reshape(hid_w, 128)
    put("wo", TABLE_PARTS + 1)
    r["v_b"][...] = gf[2 * half, nb : nb + 1, :]
    put("b", TABLE_PARTS + 2)
    loads[3].wait()
    r["v_q"][...] = r["q"][...]
    put("q", TABLE_PARTS + 3)
    loads[4].wait()
    r["v_loss"][...] = r["loss"][...]
    put("loss", TABLE_PARTS + 4)
    for copy in stores:
        copy.wait()


def per_device(queries, item_table, cand_row, cand_owner, cand_count, positive, w_in, b_in, w_out):
    n_dp, n_mp = lax.axis_size("dp"), lax.axis_size("mp")
    nz = n_dp // GRP
    cl = cand_row.shape[0]
    nq, out_w = queries.shape
    rows_dev, emb_w = item_table.shape
    hid_w = w_in.shape[1]
    slots = 2 * n_dp
    sm = slots // n_mp
    srcs = n_dp // n_mp
    nc = srcs * cl
    ns = n_dp * sm
    qb = nq // n_mp
    nt = nq // QT
    gr = emb_w // n_dp + 8
    ins = dict(
        own=cand_owner.reshape(1, cl), row=cand_row[None, :], cnt=cand_count[None, :],
        pos=positive[None, :], b_in=b_in[None, :],
    )
    far = dict(table_in=item_table, w_in_in=w_in, w_out_in=w_out, q_in=queries)
    mids = dict(
        o_loss=((1, nq), F32), o_q=((qb, out_w), F32), o_gf=((n_dp, gr, hid_w), BF16),
        o_ht=((rows_dev, 128), BF16), o_eg=((n_mp, sm, emb_w), BF16),
    )
    outs = dict(
        g_loss=((1, nq), F32), g_q=((qb, out_w), F32), g_wi=((emb_w, hid_w), F32),
        g_b=((1, hid_w), F32), g_wo=((hid_w, out_w), F32), g_table=((rows_dev, emb_w), F32),
    )
    vmem = dict(
        q=((nq, out_w), BF16), table=((rows_dev, emb_w), BF16), w_in=((emb_w, hid_w), BF16),
        w_out=((hid_w, out_w), BF16), loss=((1, nq), F32), qs=((qb, out_w), F32),
        r1s=((n_dp, 1, 128), F32), i1=((1, 128), F32),
        infoz=((nz, GRP, 1, 128), F32), rq=((n_dp, 1, 128), F32),
        ht=((rows_dev, 128), BF16), emb=((slots, emb_w), BF16), pre=((slots, hid_w), F32),
        hid=((slots, hid_w), BF16), bs=((n_mp, sm, out_w), F32), br=((n_mp, sm, out_w), F32),
        ag=((n_dp, sm, out_w), BF16), t8=((8, 128), F32), pick=((nc, ns), BF16), pick_t=((ns, nc), BF16), c2=((srcs // 2, 1, 2 * cl), F32), logq=((nc, 1), F32),
        items=((nc, out_w), BF16), items_t=((out_w, nc), BF16), ex=((nt, nc, QT), F32),
        st=((2, 1, nq), F32), sr=((n_mp, 2, 1, nq), F32), sp=((1, 1, nq), F32), spr=((n_mp, 1, nq), F32), fac=((1, nq), F32),
        pg=((nt, nc, QT), BF16), ig=((nc, out_w), F32),
        es=((n_dp, sm, out_w), F32), er=((2, nz, sm, out_w), F32), e_own=((sm, out_w), F32),
        h_own=((out_w, qb), F32), igm=((n_mp, sm, out_w), BF16),
        ga=((n_dp, gr, hid_w), F32), gr=((2, nz, gr, hid_w), F32), g_own=((gr, hid_w), F32),
        gf=((n_dp, gr, hid_w), BF16),
        ks=((n_mp, sm, emb_w), F32), kr=((n_mp, sm, emb_w), F32), eg=((n_mp, sm, emb_w), BF16),
    )
    fixed = dict(
        ey=((nz,), (sm, out_w), 1), ex2=((nz,), (sm, out_w), 1), ez=((nz,), (sm, out_w), 1),
        ezr=((nz,), (sm, out_w), 1), gy=((nz,), (gr, hid_w), 2), gx2=((nz,), (gr, hid_w), 2),
        gz=((nz,), (gr, hid_w), 2), gzr=((nz,), (gr, hid_w), 2), hs=((NY, 2), (out_w, qb), 1),
        hr=((NY, 2), (out_w, qb), 1), h2=((), (out_w, qb), 1), h3=((), (out_w, qb), 1),
    )
    for name, (lead, block, tiles) in fixed.items():
        vmem[name] = ((*lead, *block), jnp.int16)
        vmem[name + "_s"] = ((*lead, tiles, 1, block[1]), F32)
    sems = dict(ss=(31,), rs=(21,), rz=(2, nz), rx=(4, nz), rxs=(4, nz), rc=(2, 2), ls=(4,), os=(5,))
    names = (*ins, *far, *mids, *vmem, *sems)
    whole = pl.BlockSpec(memory_space=pltpu.VMEM)
    there = pl.BlockSpec(memory_space=pl.ANY)
    loss, qs, gf, ht, eg = pl.pallas_call(
        functools.partial(step_kernel, n_dp, n_mp, names),
        out_shape=[jax.ShapeDtypeStruct(*s) for s in mids.values()],
        in_specs=[whole] * len(ins) + [there] * len(far),
        out_specs=[there] * len(mids),
        scratch_shapes=[pltpu.VMEM(*s) for s in vmem.values()]
        + [pltpu.SemaphoreType.DMA(s) for s in sems.values()],
        compiler_params=pltpu.CompilerParams(
            collective_id=0, has_side_effects=True, vmem_limit_bytes=VMEM_BYTES
        ),
    )(*ins.values(), *far.values())
    middle = {n: mids["o_" + n] for n in MIDS}
    held = {"v" + n[1:]: v for n, v in outs.items()}
    names = (*("i_" + n for n in MIDS), *outs, *middle, *held, "ls", "os")
    loss, g_q, g_wi, g_b, g_wo, g_table = pl.pallas_call(
        functools.partial(results_kernel, names),
        out_shape=[jax.ShapeDtypeStruct(*s) for s in outs.values()],
        in_specs=[there] * 5,
        out_specs=[there] * len(outs),
        scratch_shapes=[pltpu.VMEM(*s) for s in (*middle.values(), *held.values())]
        + [pltpu.SemaphoreType.DMA((5,)), pltpu.SemaphoreType.DMA((TABLE_PARTS + 5,))],
        compiler_params=pltpu.CompilerParams(vmem_limit_bytes=VMEM_BYTES),
    )(eg, ht, gf, qs, loss)
    return loss.reshape(nq), g_q, g_wi, g_b.reshape(hid_w), g_wo, g_table


def solution(mesh):
    placed = (
        P("dp", None),
        P("dp", None),
        P("dp"),
        P("dp", None),
        P("dp"),
        P("dp"),
        P(None, "mp"),
        P("mp"),
        P("mp", None),
    )
    return jax.shard_map(
        per_device,
        mesh=mesh,
        in_specs=placed,
        out_specs=(
            P("dp"),
            P(("dp", "mp"), None),
            P(None, "mp"),
            P("mp"),
            P("mp", None),
            P("dp", None),
        ),
        check_vma=False,
    )
```

```python
import functools
import math

import jax
import jax.numpy as jnp
from jax import lax
from jax.experimental import pallas as pl
from jax.experimental.pallas import tpu as pltpu
from jax.sharding import PartitionSpec as P

MESH = pl.DeviceIdType.MESH
F32 = jnp.float32
BF16 = jnp.bfloat16
GRP = 4
QT = 1024
VMEM_BYTES = 64_000_000
TABLE_PARTS = 4
MIDS = ("eg", "ht", "gf", "q", "loss")
OUTS = ("o_loss", "o_q", "o_gf", "o_ht", "o_eg")
FIXED = 32767.0
FAR_ITEMS, FAR_SUMS = 0, 2
NY = 4


def dot(a, b, ca, cb):
    return lax.dot_general(a, b, (((ca,), (cb,)), ((), ())), preferred_element_type=F32)


def drain(ref, sem):
    pltpu.make_async_copy(ref, ref, sem).wait()


def coded(v, tiles):
    rows, width = v.shape[-2], v.shape[-1]
    t = v.reshape(tiles, rows // tiles, width)
    top = jnp.max(jnp.abs(t), axis=1, keepdims=True)
    fixed = t * (FIXED / jnp.maximum(top, 1e-30))
    fixed = jnp.round(fixed).reshape(rows, width).astype(jnp.int32).astype(jnp.int16)
    return fixed, top * (1.0 / FIXED)


def decoded(fixed, scales):
    rows, width = fixed.shape
    tiles = scales.shape[0]
    v = fixed.astype(jnp.int32).astype(F32).reshape(tiles, rows // tiles, width)
    return (v * scales).reshape(rows, width)


def step_kernel(n_dp, n_mp, names, *refs):
    r = dict(zip(names, refs))
    nz = n_dp // GRP
    dp, mp = lax.axis_index("dp"), lax.axis_index("mp")
    z, g = lax.div(dp, GRP), lax.rem(dp, GRP)
    core, x_hi = lax.rem(g, 2), lax.div(g, 2)
    gc = x_hi * 2 + (1 - core)
    gx = lax.rem(g + 2, GRP)
    to_core, to_x = (z * GRP + gc, mp), (z * GRP + gx, mp)
    to_diag = (z * GRP + lax.rem(gc + 2, GRP), mp)
    cl = r["own"].shape[1]
    slots = 2 * n_dp
    sm = slots // n_mp
    srcs = n_dp // n_mp
    nc = srcs * cl
    ns = n_dp * sm
    emb_w = r["table"].shape[1]
    out_w = r["q"].shape[1]
    nq = r["q"].shape[0]
    scale = 1.0 / math.sqrt(out_w)
    qb = nq // n_mp

    def near(i):
        odd = lax.rem(i, 2)
        return odd * lax.div(i + 1, 2) + (1 - odd) * lax.rem(nz - lax.div(i, 2), nz)

    def zplus(k):
        return lax.rem(z + k, nz)

    def zminus(k):
        return lax.rem(z + nz - k, nz)

    def send(src, dst, ssem, rsem, dev):
        pltpu.make_async_remote_copy(
            src_ref=src, dst_ref=dst, send_sem=ssem, recv_sem=rsem, device_id=dev, device_id_type=MESH
        ).start()

    def loop(lo, hi, body):
        def step(i, c):
            body(i)
            return c

        lax.fori_loop(lo, hi, step, 0)

    x_lo, y = lax.div(mp, NY), lax.rem(mp, NY)
    columns = [
        (1 - x_lo) * NY + lax.rem(y + j, NY) if far else x_lo * NY + lax.rem(y + j, NY)
        for far in (True, False) for j in (2, 1, 3, 0) if far or j
    ]
    loads = {}
    for i, name in enumerate(("table", "w_in", "w_out", "q")):
        loads[name] = pltpu.make_async_copy(r[name + "_in"], r[name], r["ls"].at[i])

    barrier = pltpu.get_barrier_semaphore()

    def greet(dev):
        pl.semaphore_signal(barrier, inc=1, device_id=dev, device_id_type=MESH)

    def greet_z(i):
        zd = zplus(near(nz - 1 - i))
        for j in range(GRP):
            greet((zd * GRP + lax.rem(g + j, GRP), mp))

    loop(0, nz - 1, greet_z)
    for j in range(1, GRP):
        greet((z * GRP + lax.rem(g + j, GRP), mp))
    for j in range(1, n_mp):
        greet((dp, lax.rem(mp + j, n_mp)))

    for name in loads:
        loads[name].start()

    r["t8"][...] = jnp.full_like(r["t8"], -1.0)
    r["t8"][0:1, 0:cl] = r["own"][...].astype(F32)
    r["t8"][1:2, 0:cl] = r["row"][...].astype(F32)
    cand = r["t8"][...]
    own_col = cand.T[0:cl, 0:1]
    lane = lax.broadcasted_iota(jnp.int32, (n_dp, 128), 1)
    sub = lax.broadcasted_iota(jnp.int32, (n_dp, 128), 0)
    earlier = (own_col == cand[0:1, :]) & (
        lax.broadcasted_iota(jnp.int32, (cl, 128), 0) < lax.broadcasted_iota(jnp.int32, (cl, 128), 1)
    )
    rank = jnp.sum(jnp.where(earlier, 1.0, 0.0), axis=0, keepdims=True)
    owner = cand[0:1, :].astype(jnp.int32)
    mine = sub == owner
    row1 = cand[1:2, :] + 1.0
    first = jnp.sum(jnp.where(mine & (rank < 0.5), row1, 0.0), axis=1, keepdims=True)
    second = jnp.sum(jnp.where(mine & (rank > 0.5), row1, 0.0), axis=1, keepdims=True)
    asked = jnp.where(lane == 2 * dp, first, jnp.where(lane == 2 * dp + 1, second, 0.0))
    r["r1s"][...] = asked.reshape(n_dp, 1, 128)
    r["rq"][pl.ds(dp, 1)] = r["r1s"][pl.ds(dp, 1)]
    code = (
        ((owner & (GRP - 1)) * nz + lax.shift_right_logical(owner, 2)) * sm + lax.rem(dp, srcs) * 2
    ).astype(F32) + rank
    r["i1"][0:1, :] = code
    r["i1"][0:1, 64 : 64 + cl] = r["cnt"][...].astype(F32)
    r["infoz"][pl.ds(z, 1), pl.ds(g, 1)] = r["i1"][...][None, None]

    pl.semaphore_wait(barrier, n_dp - 1 + n_mp - 1)

    def ask(zd, j):
        to = zd * GRP + lax.rem(g + j, GRP)
        send(r["r1s"].at[to], r["rq"].at[dp], r["ss"].at[0], r["rs"].at[0], (to, mp))

    def ask_z(i):
        for j in range(GRP):
            ask(zplus(near(nz - 1 - i)), j)

    loop(0, nz - 1, ask_z)
    for j in range(1, GRP):
        ask(z, j)
    for j in range(1, GRP):
        gd = lax.rem(g + j, GRP)
        send(r["i1"], r["infoz"].at[z, g], r["ss"].at[1], r["rs"].at[1], (z * GRP + gd, mp))
    drain(r["infoz"].at[0, pl.ds(0, GRP - 1)], r["rs"].at[1])

    def tell(i):
        zd = zplus(near(nz - 1 - i))
        send(r["infoz"].at[z], r["infoz"].at[z], r["ss"].at[3], r["rs"].at[3], (zd * GRP + g, mp))

    loop(0, nz - 1, tell)
    drain(r["rq"].at[pl.ds(0, n_dp - 1)], r["rs"].at[0])

    asked_row = jnp.sum(r["rq"][...], axis=0)
    for name in ("table", "w_in", "w_out"):
        loads[name].wait()
    rows_dev = r["table"].shape[0]
    hits = lax.broadcasted_iota(jnp.int32, (rows_dev, 128), 0).astype(F32) + 1.0 == asked_row
    r["ht"][...] = jnp.where(hits, 1.0, 0.0).astype(BF16)
    emb = dot(r["ht"][...], r["table"][...], 0, 0)[:slots].astype(BF16)
    r["emb"][...] = emb
    pre = dot(emb, r["w_in"][...], 1, 0) + r["b_in"][...]
    r["pre"][...] = pre
    hidden = jnp.maximum(pre, 0.0).astype(BF16)
    r["hid"][...] = hidden
    item_p = dot(hidden, r["w_out"][...], 1, 0)
    for j in range(n_mp):
        r["bs"][j] = item_p[j * sm : (j + 1) * sm]
    r["br"][pl.ds(mp, 1)] = r["bs"][pl.ds(mp, 1)]
    for md in columns:
        send(r["bs"].at[md], r["br"].at[mp], r["ss"].at[4], r["rs"].at[4], (dp, md))
    drain(r["br"].at[pl.ds(0, n_mp - 1)], r["rs"].at[4])
    item_own = r["br"][0]
    for j in range(1, n_mp):
        item_own = item_own + r["br"][j]
    r["ag"][pl.ds(g * nz + z, 1)] = item_own.astype(BF16)[None]

    def ag_start(buf, ss, rz):
        own = g * nz + z

        def go(i):
            k = near(nz - 1 - i)
            send(buf.at[own], buf.at[own], r["ss"].at[ss], rz.at[k], (zplus(k) * GRP + g, mp))

        loop(0, nz - 1, go)

    def ag_finish(buf, ss, rs, rz, rx, far):
        own = g * nz + z

        def pass_on(k, b):
            send(buf.at[b], buf.at[b], r["ss"].at[ss + 1], rx.at[k], to_x)
            send(buf.at[b], buf.at[b], r["ss"].at[ss + 2], r["rs"].at[rs], to_core)

        pass_on(0, own)

        def relay(i):
            k = near(i)
            b = g * nz + zminus(k)
            drain(buf.at[b], rz.at[k])
            pass_on(k, b)
            return b

        def relay_far(i):
            b = relay(i)
            send(buf.at[b], buf.at[b], r["ss"].at[ss + 3], r["rs"].at[rs + 1], to_diag)

        loop(1, nz - far, relay)
        loop(nz - far, nz, relay_far)

        def relay_x(i):
            k = near(i)
            b = gx * nz + zminus(k)
            drain(buf.at[b], rx.at[k])
            send(buf.at[b], buf.at[b], r["ss"].at[ss + 3], r["rs"].at[rs + 1], to_core)

        loop(0, nz - far, relay_x)

        def take_x(i):
            k = near(i)
            drain(buf.at[gx * nz + zminus(k)], rx.at[k])

        loop(nz - far, nz, take_x)
        drain(buf.at[pl.ds(0, nz)], r["rs"].at[rs])
        drain(buf.at[pl.ds(0, nz)], r["rs"].at[rs + 1])

    def ag_sent(buf, ss):
        drain(buf.at[pl.ds(0, nz - 1)], r["ss"].at[ss])
        for j in range(1, 4):
            drain(buf.at[pl.ds(0, nz)], r["ss"].at[ss + j])

    ag_start(r["ag"], 5, r["rz"].at[0])

    drain(r["infoz"].at[pl.ds(0, nz - 1)], r["rs"].at[3])
    r["t8"][...] = jnp.zeros_like(r["t8"])
    for s in range(srcs):
        src = mp * srcs + s
        r["t8"][s : s + 1, :] = r["infoz"][lax.div(src, GRP), lax.rem(src, GRP)]
    lines = r["t8"][...]
    cols = lines.T
    at = lax.broadcasted_iota(jnp.int32, (cl, ns), 1).astype(F32)
    for s in range(srcs):
        here = slice(s * cl, (s + 1) * cl)
        r["pick"][here, :] = jnp.where(cols[0:cl, s : s + 1] == at, 1.0, 0.0).astype(BF16)
        r["logq"][here, :] = jnp.log(cols[64 : 64 + cl, s : s + 1])
    for s in range(srcs):
        r["c2"][s // 2, :, (s % 2) * cl : (s % 2 + 1) * cl] = lines[s : s + 1, 0:cl]
    row_at = lax.broadcasted_iota(jnp.int32, (ns, 2 * cl), 0).astype(F32)
    for s in range(srcs // 2):
        r["pick_t"][:, 2 * s * cl : 2 * (s + 1) * cl] = jnp.where(r["c2"][s] == row_at, 1.0, 0.0).astype(BF16)
    ag_finish(r["ag"], 5, 5, r["rz"].at[0], r["rx"].at[0], FAR_ITEMS)

    loads["q"].wait()
    items = dot(r["pick"][...], r["ag"][...].reshape(ns, out_w), 1, 0)
    r["items"][...] = items.astype(BF16)
    r["items_t"][...] = items.T.astype(BF16)

    ids = lax.broadcasted_iota(jnp.int32, (nc, QT), 0) + mp * nc

    def score(t):
        where = pl.ds(pl.multiple_of(t * QT, QT), QT)
        sc = dot(r["items"][...], r["q"][where, :], 1, 1) * scale - r["logq"][...]
        top = jnp.max(sc, axis=0, keepdims=True)
        ex = jnp.exp(sc - top)
        r["ex"][t] = ex
        r["st"][0, :, where] = top
        r["st"][1, :, where] = jnp.sum(ex, axis=0, keepdims=True)
        r["sp"][0, :, where] = jnp.sum(jnp.where(ids == r["pos"][:, where], sc, 0.0), axis=0, keepdims=True)

    loop(0, nq // QT, score)
    r["sr"][pl.ds(mp, 1)] = r["st"][...][None]
    r["spr"][pl.ds(mp, 1)] = r["sp"][...]
    for md in columns:
        send(r["st"], r["sr"].at[mp], r["ss"].at[9], r["rs"].at[7], (dp, md))
    for md in columns:
        send(r["sp"].at[0], r["spr"].at[mp], r["ss"].at[2], r["rs"].at[2], (dp, md))
    drain(r["sr"].at[pl.ds(0, n_mp - 1)], r["rs"].at[7])
    top = r["sr"][0, 0]
    for j in range(1, n_mp):
        top = jnp.maximum(top, r["sr"][j, 0])
    total = jnp.zeros_like(top)
    for j in range(n_mp):
        total = total + r["sr"][j, 1] * jnp.exp(r["sr"][j, 0] - top)
    lse = top + jnp.log(total)
    r["loss"][...] = lse
    r["fac"][...] = jnp.exp(r["st"][0] - lse)

    r["ig"][...] = jnp.zeros_like(r["ig"])

    def prob(t):
        where = pl.ds(pl.multiple_of(t * QT, QT), QT)
        pg = r["ex"][t] * r["fac"][:, where] - jnp.where(ids == r["pos"][:, where], 1.0, 0.0)
        pg = pg.astype(BF16)
        r["pg"][t] = pg
        r["ig"][...] += dot(pg, r["q"][where, :], 1, 0)

    loop(0, nq // QT, prob)

    def rs_first(buf, got, ss, rb):
        gd = (1 - x_hi) * 2 + 1 - core

        def go(i):
            k = near(nz - 1 - i)
            zz = zplus(k)
            send(buf.at[gd * nz + zz], got.at[1 - x_hi, zz], r["ss"].at[ss], rb.at[k], to_core)

        loop(0, nz, go)

    def rs_second(buf, got, ss, rc):
        gd = x_hi * 2 + 1 - core
        send(buf.at[pl.ds(gd * nz, nz)], got.at[x_hi], r["ss"].at[ss], rc, to_core)

    def rs_middle(buf, got, out, gotx, ss, rb, rx):
        (outq, outs), (gotq, gots) = out, gotx

        def go(i):
            k = near(nz - 1 - i)
            zz = zplus(k)
            drain(got.at[1 - x_hi, zz], rb.at[k])
            outq[zz], outs[zz] = coded(buf[gx * nz + zz] + got[1 - x_hi, zz], outs.shape[1])
            send(outs.at[zz], gots.at[zz], r["ss"].at[ss + 2], r["rxs"].at[rx, k], to_x)
            send(outq.at[zz], gotq.at[zz], r["ss"].at[ss + 1], r["rx"].at[rx, k], to_x)

        loop(0, nz, go)

    def rs_finish(buf, got, gotx, outz, gotz, own, ss, rs, rc, rx):
        drain(got.at[x_hi], rc)
        (gotq, gots), (outq, outs), (zq, zs) = gotx, outz, gotz

        def block(k, zz):
            drain(gots.at[zz], r["rxs"].at[rx, k])
            drain(gotq.at[zz], r["rx"].at[rx, k])
            return buf[g * nz + zz] + got[x_hi, zz] + decoded(gotq[zz], gots[zz])

        def go(i):
            k = near(nz - 1 - i)
            zz = zplus(k)
            outq[zz], outs[zz] = coded(block(k, zz), outs.shape[1])
            to = (zz * GRP + g, mp)
            send(outs.at[zz], zs.at[z], r["ss"].at[ss + 4], r["rs"].at[rs + 1], to)
            send(outq.at[zz], zq.at[z], r["ss"].at[ss + 3], r["rs"].at[rs], to)

        loop(0, nz - 1, go)
        own[...] = block(0, z)
        zq[pl.ds(z, 1)] = jnp.zeros((1, *zq.shape[1:]), jnp.int16)
        zs[pl.ds(z, 1)] = jnp.zeros((1, *zs.shape[1:]), F32)

    def rs_result(gotz, own, rs):
        zq, zs = gotz
        drain(zs.at[pl.ds(0, nz - 1)], r["rs"].at[rs + 1])
        drain(zq.at[pl.ds(0, nz - 1)], r["rs"].at[rs])
        total = own[...]
        for i in range(nz):
            total = total + decoded(zq[i], zs[i])
        return total

    def rs_sent(buf, out, outz, ss):
        drain(buf.at[pl.ds(0, 2 * nz)], r["ss"].at[ss])
        drain(out[0], r["ss"].at[ss + 1])
        drain(out[1], r["ss"].at[ss + 2])
        drain(outz[0].at[pl.ds(0, nz - 1)], r["ss"].at[ss + 3])
        drain(outz[1].at[pl.ds(0, nz - 1)], r["ss"].at[ss + 4])

    def pair(name):
        return r[name], r[name + "_s"]

    ig = r["ig"][...] * scale
    hi = ig.astype(BF16)
    lo = (ig - hi.astype(F32)).astype(BF16)
    part = ns // GRP

    def expand(gd):
        pick = r["pick_t"][pl.ds(pl.multiple_of(gd * part, part), part), :]
        r["es"][pl.ds(gd * nz, nz)] = (dot(pick, hi, 1, 0) + dot(pick, lo, 1, 0)).reshape(nz, sm, out_w)

    expand((1 - x_hi) * 2 + 1 - core)
    rs_first(r["es"], r["er"], 10, r["rb"].at[0])
    expand(gx)
    expand(x_hi * 2 + 1 - core)
    rs_second(r["es"], r["er"], 10, r["rc"].at[0])
    rs_middle(r["es"], r["er"], pair("ey"), pair("ex2"), 10, r["rb"].at[0], 1)
    expand(g)

    def query(t):
        qg = dot(r["items_t"][...], r["pg"][t], 1, 0) * scale
        for j in range(QT // qb):
            b = t * (QT // qb) + j
            yd, xd = lax.rem(b, NY), lax.div(b, NY)
            r["hs"][yd, xd], r["hs_s"][yd, xd] = coded(qg[:, j * qb : (j + 1) * qb], 1)

    loop(0, nq // QT, query)
    r["hr"][pl.ds(y, 1)] = r["hs"][pl.ds(y, 1)]
    r["hr_s"][pl.ds(y, 1)] = r["hs_s"][pl.ds(y, 1)]
    for j in range(1, NY):
        yd = lax.rem(y + j, NY)
        to = (dp, x_lo * NY + yd)
        send(r["hs_s"].at[yd], r["hr_s"].at[y], r["ss"].at[15], r["rs"].at[10], to)
        send(r["hs"].at[yd], r["hr"].at[y], r["ss"].at[16], r["rs"].at[11], to)
    rs_finish(
        r["es"], r["er"], pair("ex2"), pair("ez"), pair("ezr"), r["e_own"], 10, 8, r["rc"].at[0], 1
    )

    r["igm"][pl.ds(mp, 1)] = rs_result(pair("ezr"), r["e_own"], 8).astype(BF16)[None]
    for md in columns:
        send(r["igm"].at[mp], r["igm"].at[mp], r["ss"].at[19], r["rs"].at[14], (dp, md))

    drain(r["hr_s"].at[pl.ds(0, NY - 1)], r["rs"].at[10])
    drain(r["hr"].at[pl.ds(0, NY - 1)], r["rs"].at[11])
    for j in range(2):
        xd = lax.rem(x_lo + 1 + j, 2)
        q_sum = decoded(r["hr"][0, xd], r["hr_s"][0, xd])
        for i in range(1, NY):
            q_sum = q_sum + decoded(r["hr"][i, xd], r["hr_s"][i, xd])
        if j == 0:
            r["h2"][...], r["h2_s"][...] = coded(q_sum, 1)
            to = (dp, (1 - x_lo) * NY + y)
            send(r["h2_s"], r["h3_s"], r["ss"].at[17], r["rs"].at[12], to)
            send(r["h2"], r["h3"], r["ss"].at[18], r["rs"].at[13], to)
        else:
            r["h_own"][...] = q_sum

    drain(r["igm"].at[pl.ds(0, n_mp - 1)], r["rs"].at[14])

    item_grad = r["igm"][...].reshape(slots, out_w)
    back = dot(item_grad, r["w_out"][...], 1, 1)
    pre_grad = jnp.where(r["pre"][...] > 0.0, back, 0.0)
    pre_bf = pre_grad.astype(BF16)
    gwi = dot(r["emb"][...], pre_bf, 0, 0)
    gwo = dot(r["hid"][...], item_grad, 0, 0)
    gb = jnp.sum(pre_bf.astype(F32), axis=0, keepdims=True)
    hid_w = gb.shape[1]
    nb = emb_w // n_dp
    r["ga"][:, 0:nb, :] = gwi.reshape(n_dp, nb, hid_w)
    r["ga"][:, nb : nb + 8, :] = jnp.zeros((n_dp, 8, hid_w), F32)
    half = hid_w // 8
    r["ga"][0:half, nb : nb + 8, :] = gwo[:, 0:128].reshape(half, 8, 128)
    r["ga"][half : 2 * half, nb : nb + 8, :] = gwo[:, 128:256].reshape(half, 8, 128)
    r["ga"][2 * half, nb : nb + 1, :] = gb
    rs_first(r["ga"], r["gr"], 20, r["rb"].at[1])
    rs_second(r["ga"], r["gr"], 20, r["rc"].at[1])
    emb_p = dot(pre_bf, r["w_in"][...], 1, 1)
    for j in range(n_mp):
        r["ks"][j] = emb_p[j * sm : (j + 1) * sm]
    r["kr"][pl.ds(mp, 1)] = r["ks"][pl.ds(mp, 1)]
    rs_middle(r["ga"], r["gr"], pair("gy"), pair("gx2"), 20, r["rb"].at[1], 2)
    for md in columns:
        send(r["ks"].at[md], r["kr"].at[mp], r["ss"].at[25], r["rs"].at[15], (dp, md))
    rs_finish(
        r["ga"], r["gr"], pair("gx2"), pair("gz"), pair("gzr"), r["g_own"], 20, 16, r["rc"].at[1], 2
    )

    drain(r["kr"].at[pl.ds(0, n_mp - 1)], r["rs"].at[15])
    emb_own = r["kr"][0]
    for j in range(1, n_mp):
        emb_own = emb_own + r["kr"][j]
    r["eg"][pl.ds(mp, 1)] = emb_own.astype(BF16)[None]
    for md in columns:
        send(r["eg"].at[mp], r["eg"].at[mp], r["ss"].at[26], r["rs"].at[18], (dp, md))

    r["gf"][pl.ds(g * nz + z, 1)] = rs_result(pair("gzr"), r["g_own"], 16).astype(BF16)[None]
    ag_start(r["gf"], 27, r["rz"].at[1])

    def out(name, src):
        copy = pltpu.make_async_copy(src, r[name], r["os"].at[OUTS.index(name)])
        copy.start()
        return copy

    drain(r["spr"].at[pl.ds(0, n_mp - 1)], r["rs"].at[2])
    at_pos = r["spr"][0]
    for j in range(1, n_mp):
        at_pos = at_pos + r["spr"][j]
    r["loss"][...] = r["loss"][...] - at_pos
    done = [out("o_ht", r["ht"]), out("o_loss", r["loss"])]
    drain(r["h3_s"], r["rs"].at[12])
    drain(r["h3"], r["rs"].at[13])
    r["qs"][...] = (r["h_own"][...] + decoded(r["h3"][...], r["h3_s"][...])).T
    done.append(out("o_q", r["qs"]))
    drain(r["eg"].at[pl.ds(0, n_mp - 1)], r["rs"].at[18])
    done.append(out("o_eg", r["eg"]))
    for copy in done:
        copy.wait()

    drain(r["r1s"].at[pl.ds(0, n_dp - 1)], r["ss"].at[0])
    drain(r["infoz"].at[0, pl.ds(0, GRP - 1)], r["ss"].at[1])
    drain(r["infoz"].at[pl.ds(0, nz - 1)], r["ss"].at[3])
    drain(r["bs"].at[pl.ds(0, n_mp - 1)], r["ss"].at[4])
    ag_sent(r["ag"], 5)
    drain(r["sr"].at[pl.ds(0, n_mp - 1)], r["ss"].at[9])
    drain(r["spr"].at[pl.ds(0, n_mp - 1)], r["ss"].at[2])
    rs_sent(r["es"], pair("ey"), pair("ez"), 10)
    drain(r["hs_s"].at[pl.ds(0, NY - 1)], r["ss"].at[15])
    drain(r["hs"].at[pl.ds(0, NY - 1)], r["ss"].at[16])
    drain(r["h2_s"], r["ss"].at[17])
    drain(r["h2"], r["ss"].at[18])
    drain(r["igm"].at[pl.ds(0, n_mp - 1)], r["ss"].at[19])
    rs_sent(r["ga"], pair("gy"), pair("gz"), 20)
    drain(r["ks"].at[pl.ds(0, n_mp - 1)], r["ss"].at[25])
    drain(r["eg"].at[pl.ds(0, n_mp - 1)], r["ss"].at[26])

    ag_finish(r["gf"], 27, 19, r["rz"].at[1], r["rx"].at[3], FAR_SUMS)
    last = out("o_gf", r["gf"])
    ag_sent(r["gf"], 27)
    last.wait()


def results_kernel(names, *refs):
    r = dict(zip(names, refs))
    n_dp, gr, hid_w = r["gf"].shape
    nb = gr - 8
    rows_dev, emb_w = r["v_table"].shape
    slots = r["eg"].shape[0] * r["eg"].shape[1]
    half = hid_w // 8
    loads = [pltpu.make_async_copy(r["i_" + n], r[n], r["ls"].at[i]) for i, n in enumerate(MIDS)]
    for copy in loads:
        copy.start()
    stores = []

    def put(name, i, rows=slice(None)):
        copy = pltpu.make_async_copy(r["v_" + name].at[rows], r["g_" + name].at[rows], r["os"].at[i])
        copy.start()
        stores.append(copy)

    loads[0].wait()
    loads[1].wait()
    eg = r["eg"][...].reshape(slots, emb_w)
    step = rows_dev // TABLE_PARTS
    for i in range(TABLE_PARTS):
        rows = pl.ds(i * step, step)
        r["v_table"][rows, :] = dot(r["ht"][rows, 0:slots], eg, 1, 0)
        put("table", i, rows)
    loads[2].wait()
    gf = r["gf"][...].astype(F32)
    r["v_wi"][...] = gf[:, 0:nb, :].reshape(emb_w, hid_w)
    put("wi", TABLE_PARTS)
    r["v_wo"][:, 0:128] = gf[0:half, nb : nb + 8, :].reshape(hid_w, 128)
    r["v_wo"][:, 128:256] = gf[half : 2 * half, nb : nb + 8, :].reshape(hid_w, 128)
    put("wo", TABLE_PARTS + 1)
    r["v_b"][...] = gf[2 * half, nb : nb + 1, :]
    put("b", TABLE_PARTS + 2)
    loads[3].wait()
    r["v_q"][...] = r["q"][...]
    put("q", TABLE_PARTS + 3)
    loads[4].wait()
    r["v_loss"][...] = r["loss"][...]
    put("loss", TABLE_PARTS + 4)
    for copy in stores:
        copy.wait()


def per_device(queries, item_table, cand_row, cand_owner, cand_count, positive, w_in, b_in, w_out):
    n_dp, n_mp = lax.axis_size("dp"), lax.axis_size("mp")
    nz = n_dp // GRP
    cl = cand_row.shape[0]
    nq, out_w = queries.shape
    rows_dev, emb_w = item_table.shape
    hid_w = w_in.shape[1]
    slots = 2 * n_dp
    sm = slots // n_mp
    srcs = n_dp // n_mp
    nc = srcs * cl
    ns = n_dp * sm
    qb = nq // n_mp
    nt = nq // QT
    gr = emb_w // n_dp + 8
    ins = dict(
        own=cand_owner.reshape(1, cl), row=cand_row[None, :], cnt=cand_count[None, :],
        pos=positive[None, :], b_in=b_in[None, :],
    )
    far = dict(table_in=item_table, w_in_in=w_in, w_out_in=w_out, q_in=queries)
    mids = dict(
        o_loss=((1, nq), F32), o_q=((qb, out_w), F32), o_gf=((n_dp, gr, hid_w), BF16),
        o_ht=((rows_dev, 128), BF16), o_eg=((n_mp, sm, emb_w), BF16),
    )
    outs = dict(
        g_loss=((1, nq), F32), g_q=((qb, out_w), F32), g_wi=((emb_w, hid_w), F32),
        g_b=((1, hid_w), F32), g_wo=((hid_w, out_w), F32), g_table=((rows_dev, emb_w), F32),
    )
    vmem = dict(
        q=((nq, out_w), BF16), table=((rows_dev, emb_w), BF16), w_in=((emb_w, hid_w), BF16),
        w_out=((hid_w, out_w), BF16), loss=((1, nq), F32), qs=((qb, out_w), F32),
        r1s=((n_dp, 1, 128), F32), i1=((1, 128), F32),
        infoz=((nz, GRP, 1, 128), F32), rq=((n_dp, 1, 128), F32),
        ht=((rows_dev, 128), BF16), emb=((slots, emb_w), BF16), pre=((slots, hid_w), F32),
        hid=((slots, hid_w), BF16), bs=((n_mp, sm, out_w), F32), br=((n_mp, sm, out_w), F32),
        ag=((n_dp, sm, out_w), BF16), t8=((8, 128), F32), pick=((nc, ns), BF16), pick_t=((ns, nc), BF16), c2=((srcs // 2, 1, 2 * cl), F32), logq=((nc, 1), F32),
        items=((nc, out_w), BF16), items_t=((out_w, nc), BF16), ex=((nt, nc, QT), F32),
        st=((2, 1, nq), F32), sr=((n_mp, 2, 1, nq), F32), sp=((1, 1, nq), F32), spr=((n_mp, 1, nq), F32), fac=((1, nq), F32),
        pg=((nt, nc, QT), BF16), ig=((nc, out_w), F32),
        es=((n_dp, sm, out_w), F32), er=((2, nz, sm, out_w), F32), e_own=((sm, out_w), F32),
        h_own=((out_w, qb), F32), igm=((n_mp, sm, out_w), BF16),
        ga=((n_dp, gr, hid_w), F32), gr=((2, nz, gr, hid_w), F32), g_own=((gr, hid_w), F32),
        gf=((n_dp, gr, hid_w), BF16),
        ks=((n_mp, sm, emb_w), F32), kr=((n_mp, sm, emb_w), F32), eg=((n_mp, sm, emb_w), BF16),
    )
    fixed = dict(
        ey=((nz,), (sm, out_w), 1), ex2=((nz,), (sm, out_w), 1), ez=((nz,), (sm, out_w), 1),
        ezr=((nz,), (sm, out_w), 1), gy=((nz,), (gr, hid_w), 2), gx2=((nz,), (gr, hid_w), 2),
        gz=((nz,), (gr, hid_w), 2), gzr=((nz,), (gr, hid_w), 2), hs=((NY, 2), (out_w, qb), 1),
        hr=((NY, 2), (out_w, qb), 1), h2=((), (out_w, qb), 1), h3=((), (out_w, qb), 1),
    )
    for name, (lead, block, tiles) in fixed.items():
        vmem[name] = ((*lead, *block), jnp.int16)
        vmem[name + "_s"] = ((*lead, tiles, 1, block[1]), F32)
    sems = dict(ss=(31,), rs=(21,), rz=(2, nz), rx=(4, nz), rxs=(4, nz), rc=(2,), rb=(2, nz), ls=(4,), os=(5,))
    names = (*ins, *far, *mids, *vmem, *sems)
    whole = pl.BlockSpec(memory_space=pltpu.VMEM)
    there = pl.BlockSpec(memory_space=pl.ANY)
    loss, qs, gf, ht, eg = pl.pallas_call(
        functools.partial(step_kernel, n_dp, n_mp, names),
        out_shape=[jax.ShapeDtypeStruct(*s) for s in mids.values()],
        in_specs=[whole] * len(ins) + [there] * len(far),
        out_specs=[there] * len(mids),
        scratch_shapes=[pltpu.VMEM(*s) for s in vmem.values()]
        + [pltpu.SemaphoreType.DMA(s) for s in sems.values()],
        compiler_params=pltpu.CompilerParams(
            collective_id=0, has_side_effects=True, vmem_limit_bytes=VMEM_BYTES
        ),
    )(*ins.values(), *far.values())
    middle = {n: mids["o_" + n] for n in MIDS}
    held = {"v" + n[1:]: v for n, v in outs.items()}
    names = (*("i_" + n for n in MIDS), *outs, *middle, *held, "ls", "os")
    loss, g_q, g_wi, g_b, g_wo, g_table = pl.pallas_call(
        functools.partial(results_kernel, names),
        out_shape=[jax.ShapeDtypeStruct(*s) for s in outs.values()],
        in_specs=[there] * 5,
        out_specs=[there] * len(outs),
        scratch_shapes=[pltpu.VMEM(*s) for s in (*middle.values(), *held.values())]
        + [pltpu.SemaphoreType.DMA((5,)), pltpu.SemaphoreType.DMA((TABLE_PARTS + 5,))],
        compiler_params=pltpu.CompilerParams(vmem_limit_bytes=VMEM_BYTES),
    )(eg, ht, gf, qs, loss)
    return loss.reshape(nq), g_q, g_wi, g_b.reshape(hid_w), g_wo, g_table


def solution(mesh):
    placed = (
        P("dp", None),
        P("dp", None),
        P("dp"),
        P("dp", None),
        P("dp"),
        P("dp"),
        P(None, "mp"),
        P("mp"),
        P("mp", None),
    )
    return jax.shard_map(
        per_device,
        mesh=mesh,
        in_specs=placed,
        out_specs=(
            P("dp"),
            P(("dp", "mp"), None),
            P(None, "mp"),
            P("mp"),
            P("mp", None),
            P("dp", None),
        ),
        check_vma=False,
    )
```

```python
import functools
import math
import types

import jax
import jax.numpy as jnp
from jax import lax
from jax.experimental import pallas as pl
from jax.experimental.pallas import tpu as pltpu
from jax.sharding import PartitionSpec as P

MESH = pl.DeviceIdType.MESH
F32 = jnp.float32
BF16 = jnp.bfloat16
GRP = 4
QT = 1024
VMEM_BYTES = 64_000_000
TABLE_PARTS = 4
MIDS = ("eg", "ht", "gf", "q", "loss")
OUTS = ("o_loss", "o_q", "o_gf", "o_ht", "o_eg")
FIXED = 32767.0
FAR_ITEMS, FAR_SUMS = 0, 2
NY = 4


def dot(a, b, ca, cb):
    return lax.dot_general(a, b, (((ca,), (cb,)), ((), ())), preferred_element_type=F32)


def drain(ref, sem):
    pltpu.make_async_copy(ref, ref, sem).wait()


def coded(v, tiles):
    rows, width = v.shape[-2], v.shape[-1]
    t = v.reshape(tiles, rows // tiles, width)
    top = jnp.max(jnp.abs(t), axis=1, keepdims=True)
    fixed = t * (FIXED / jnp.maximum(top, 1e-30))
    fixed = jnp.round(fixed).reshape(rows, width).astype(jnp.int32).astype(jnp.int16)
    return fixed, top * (1.0 / FIXED)


def decoded(fixed, scales):
    rows, width = fixed.shape
    tiles = scales.shape[0]
    v = fixed.astype(jnp.int32).astype(F32).reshape(tiles, rows // tiles, width)
    return (v * scales).reshape(rows, width)


def step_kernel(n_dp, n_mp, names, *refs):
    r = types.SimpleNamespace(**dict(zip(names, refs)))
    nz = n_dp // GRP
    dp, mp = lax.axis_index("dp"), lax.axis_index("mp")
    z, g = lax.div(dp, GRP), lax.rem(dp, GRP)
    core, x_hi = lax.rem(g, 2), lax.div(g, 2)
    gc = x_hi * 2 + (1 - core)
    gx = lax.rem(g + 2, GRP)
    to_core, to_x = (z * GRP + gc, mp), (z * GRP + gx, mp)
    to_diag = (z * GRP + lax.rem(gc + 2, GRP), mp)
    cl = r.own.shape[1]
    slots = 2 * n_dp
    sm = slots // n_mp
    srcs = n_dp // n_mp
    nc = srcs * cl
    ns = n_dp * sm
    emb_w = r.table.shape[1]
    out_w = r.q.shape[1]
    nq = r.q.shape[0]
    scale = 1.0 / math.sqrt(out_w)
    qb = nq // n_mp

    def near(i):
        odd = lax.rem(i, 2)
        return odd * lax.div(i + 1, 2) + (1 - odd) * lax.rem(nz - lax.div(i, 2), nz)

    def zplus(k):
        return lax.rem(z + k, nz)

    def zminus(k):
        return lax.rem(z + nz - k, nz)

    def send(src, dst, ssem, rsem, dev):
        pltpu.make_async_remote_copy(
            src_ref=src, dst_ref=dst, send_sem=ssem, recv_sem=rsem, device_id=dev, device_id_type=MESH
        ).start()

    def loop(lo, hi, body):
        def step(i, c):
            body(i)
            return c

        lax.fori_loop(lo, hi, step, 0)

    x_lo, y = lax.div(mp, NY), lax.rem(mp, NY)
    columns = [
        (1 - x_lo) * NY + lax.rem(y + j, NY) if far else x_lo * NY + lax.rem(y + j, NY)
        for far in (True, False) for j in (2, 1, 3, 0) if far or j
    ]
    loads = {}
    for i, name in enumerate(("table", "w_in", "w_out", "q")):
        loads[name] = pltpu.make_async_copy(getattr(r, name + "_in"), getattr(r, name), r.ls.at[i])

    barrier = pltpu.get_barrier_semaphore()

    def greet(dev):
        pl.semaphore_signal(barrier, inc=1, device_id=dev, device_id_type=MESH)

    def greet_z(i):
        zd = zplus(near(nz - 1 - i))
        for j in range(GRP):
            greet((zd * GRP + lax.rem(g + j, GRP), mp))

    loop(0, nz - 1, greet_z)
    for j in range(1, GRP):
        greet((z * GRP + lax.rem(g + j, GRP), mp))
    for j in range(1, n_mp):
        greet((dp, lax.rem(mp + j, n_mp)))

    for name in loads:
        loads[name].start()

    r.t8[...] = jnp.full_like(r.t8, -1.0)
    r.t8[0:1, 0:cl] = r.own[...].astype(F32)
    r.t8[1:2, 0:cl] = r.row[...].astype(F32)
    cand = r.t8[...]
    own_col = cand.T[0:cl, 0:1]
    lane = lax.broadcasted_iota(jnp.int32, (n_dp, 128), 1)
    sub = lax.broadcasted_iota(jnp.int32, (n_dp, 128), 0)
    earlier = (own_col == cand[0:1, :]) & (
        lax.broadcasted_iota(jnp.int32, (cl, 128), 0) < lax.broadcasted_iota(jnp.int32, (cl, 128), 1)
    )
    rank = jnp.sum(jnp.where(earlier, 1.0, 0.0), axis=0, keepdims=True)
    owner = cand[0:1, :].astype(jnp.int32)
    mine = sub == owner
    row1 = cand[1:2, :] + 1.0
    first = jnp.sum(jnp.where(mine & (rank < 0.5), row1, 0.0), axis=1, keepdims=True)
    second = jnp.sum(jnp.where(mine & (rank > 0.5), row1, 0.0), axis=1, keepdims=True)
    asked = jnp.where(lane == 2 * dp, first, jnp.where(lane == 2 * dp + 1, second, 0.0))
    r.r1s[...] = asked.reshape(n_dp, 1, 128)
    r.rq[pl.ds(dp, 1)] = r.r1s[pl.ds(dp, 1)]
    code = (
        ((owner & (GRP - 1)) * nz + lax.shift_right_logical(owner, 2)) * sm + lax.rem(dp, srcs) * 2
    ).astype(F32) + rank
    r.i1[0:1, :] = code
    r.i1[0:1, 64 : 64 + cl] = r.cnt[...].astype(F32)
    r.infoz[pl.ds(z, 1), pl.ds(g, 1)] = r.i1[...][None, None]

    pl.semaphore_wait(barrier, n_dp - 1 + n_mp - 1)

    def ask(zd, j):
        to = zd * GRP + lax.rem(g + j, GRP)
        send(r.r1s.at[to], r.rq.at[dp], r.ss.at[0], r.rs.at[0], (to, mp))

    def ask_z(i):
        for j in range(GRP):
            ask(zplus(near(nz - 1 - i)), j)

    loop(0, nz - 1, ask_z)
    for j in range(1, GRP):
        ask(z, j)
    for j in range(1, GRP):
        gd = lax.rem(g + j, GRP)
        send(r.i1, r.infoz.at[z, g], r.ss.at[1], r.rs.at[1], (z * GRP + gd, mp))
    drain(r.infoz.at[0, pl.ds(0, GRP - 1)], r.rs.at[1])

    def tell(i):
        zd = zplus(near(nz - 1 - i))
        send(r.infoz.at[z], r.infoz.at[z], r.ss.at[3], r.rs.at[3], (zd * GRP + g, mp))

    loop(0, nz - 1, tell)
    drain(r.rq.at[pl.ds(0, n_dp - 1)], r.rs.at[0])

    asked_row = jnp.sum(r.rq[...], axis=0)
    for name in ("table", "w_in", "w_out"):
        loads[name].wait()
    rows_dev = r.table.shape[0]
    hits = lax.broadcasted_iota(jnp.int32, (rows_dev, 128), 0).astype(F32) + 1.0 == asked_row
    r.ht[...] = jnp.where(hits, 1.0, 0.0).astype(BF16)
    emb = dot(r.ht[...], r.table[...], 0, 0)[:slots].astype(BF16)
    r.emb[...] = emb
    pre = dot(emb, r.w_in[...], 1, 0) + r.b_in[...]
    r.pre[...] = pre
    hidden = jnp.maximum(pre, 0.0).astype(BF16)
    r.hid[...] = hidden
    item_p = dot(hidden, r.w_out[...], 1, 0)
    for j in range(n_mp):
        r.bs[j] = item_p[j * sm : (j + 1) * sm]
    r.br[pl.ds(mp, 1)] = r.bs[pl.ds(mp, 1)]
    for md in columns:
        send(r.bs.at[md], r.br.at[mp], r.ss.at[4], r.rs.at[4], (dp, md))
    drain(r.br.at[pl.ds(0, n_mp - 1)], r.rs.at[4])
    item_own = r.br[0]
    for j in range(1, n_mp):
        item_own = item_own + r.br[j]
    r.ag[pl.ds(g * nz + z, 1)] = item_own.astype(BF16)[None]

    def ag_start(buf, ss, rz):
        own = g * nz + z

        def go(i):
            k = near(nz - 1 - i)
            send(buf.at[own], buf.at[own], r.ss.at[ss], rz.at[k], (zplus(k) * GRP + g, mp))

        loop(0, nz - 1, go)

    def ag_finish(buf, ss, rs, rz, rx, far):
        own = g * nz + z

        def pass_on(k, b):
            send(buf.at[b], buf.at[b], r.ss.at[ss + 1], rx.at[k], to_x)
            send(buf.at[b], buf.at[b], r.ss.at[ss + 2], r.rs.at[rs], to_core)

        pass_on(0, own)

        def relay(i):
            k = near(i)
            b = g * nz + zminus(k)
            drain(buf.at[b], rz.at[k])
            pass_on(k, b)
            return b

        def relay_far(i):
            b = relay(i)
            send(buf.at[b], buf.at[b], r.ss.at[ss + 3], r.rs.at[rs + 1], to_diag)

        loop(1, nz - far, relay)
        loop(nz - far, nz, relay_far)

        def relay_x(i):
            k = near(i)
            b = gx * nz + zminus(k)
            drain(buf.at[b], rx.at[k])
            send(buf.at[b], buf.at[b], r.ss.at[ss + 3], r.rs.at[rs + 1], to_core)

        loop(0, nz - far, relay_x)

        def take_x(i):
            k = near(i)
            drain(buf.at[gx * nz + zminus(k)], rx.at[k])

        loop(nz - far, nz, take_x)
        drain(buf.at[pl.ds(0, nz)], r.rs.at[rs])
        drain(buf.at[pl.ds(0, nz)], r.rs.at[rs + 1])

    def ag_sent(buf, ss):
        drain(buf.at[pl.ds(0, nz - 1)], r.ss.at[ss])
        for j in range(1, 4):
            drain(buf.at[pl.ds(0, nz)], r.ss.at[ss + j])

    ag_start(r.ag, 5, r.rz.at[0])

    drain(r.infoz.at[pl.ds(0, nz - 1)], r.rs.at[3])
    r.t8[...] = jnp.zeros_like(r.t8)
    for s in range(srcs):
        src = mp * srcs + s
        r.t8[s : s + 1, :] = r.infoz[lax.div(src, GRP), lax.rem(src, GRP)]
    lines = r.t8[...]
    cols = lines.T
    at = lax.broadcasted_iota(jnp.int32, (cl, ns), 1).astype(F32)
    for s in range(srcs):
        here = slice(s * cl, (s + 1) * cl)
        r.pick[here, :] = jnp.where(cols[0:cl, s : s + 1] == at, 1.0, 0.0).astype(BF16)
        r.logq[here, :] = jnp.log(cols[64 : 64 + cl, s : s + 1])
    for s in range(srcs):
        r.c2[s // 2, :, (s % 2) * cl : (s % 2 + 1) * cl] = lines[s : s + 1, 0:cl]
    row_at = lax.broadcasted_iota(jnp.int32, (ns, 2 * cl), 0).astype(F32)
    for s in range(srcs // 2):
        r.pick_t[:, 2 * s * cl : 2 * (s + 1) * cl] = jnp.where(r.c2[s] == row_at, 1.0, 0.0).astype(BF16)
    ag_finish(r.ag, 5, 5, r.rz.at[0], r.rx.at[0], FAR_ITEMS)

    loads["q"].wait()
    items = dot(r.pick[...], r.ag[...].reshape(ns, out_w), 1, 0)
    r.items[...] = items.astype(BF16)
    r.items_t[...] = items.T.astype(BF16)

    ids = lax.broadcasted_iota(jnp.int32, (nc, QT), 0) + mp * nc

    def score(t):
        where = pl.ds(pl.multiple_of(t * QT, QT), QT)
        sc = dot(r.items[...], r.q[where, :], 1, 1) * scale - r.logq[...]
        top = jnp.max(sc, axis=0, keepdims=True)
        ex = jnp.exp(sc - top)
        r.ex[t] = ex
        r.st[0, :, where] = top
        r.st[1, :, where] = jnp.sum(ex, axis=0, keepdims=True)
        r.sp[0, :, where] = jnp.sum(jnp.where(ids == r.pos[:, where], sc, 0.0), axis=0, keepdims=True)

    loop(0, nq // QT, score)
    r.sr[pl.ds(mp, 1)] = r.st[...][None]
    r.spr[pl.ds(mp, 1)] = r.sp[...]
    for md in columns:
        send(r.st, r.sr.at[mp], r.ss.at[9], r.rs.at[7], (dp, md))
    for md in columns:
        send(r.sp.at[0], r.spr.at[mp], r.ss.at[2], r.rs.at[2], (dp, md))
    drain(r.sr.at[pl.ds(0, n_mp - 1)], r.rs.at[7])
    top = r.sr[0, 0]
    for j in range(1, n_mp):
        top = jnp.maximum(top, r.sr[j, 0])
    total = jnp.zeros_like(top)
    for j in range(n_mp):
        total = total + r.sr[j, 1] * jnp.exp(r.sr[j, 0] - top)
    lse = top + jnp.log(total)
    r.loss[...] = lse
    r.fac[...] = jnp.exp(r.st[0] - lse)

    r.ig[...] = jnp.zeros_like(r.ig)

    def prob(t):
        where = pl.ds(pl.multiple_of(t * QT, QT), QT)
        pg = r.ex[t] * r.fac[:, where] - jnp.where(ids == r.pos[:, where], 1.0, 0.0)
        pg = pg.astype(BF16)
        r.pg[t] = pg
        r.ig[...] += dot(pg, r.q[where, :], 1, 0)

    loop(0, nq // QT, prob)

    def rs_first(buf, got, ss, rb):
        gd = (1 - x_hi) * 2 + 1 - core

        def go(i):
            k = near(nz - 1 - i)
            zz = zplus(k)
            send(buf.at[gd * nz + zz], got.at[1 - x_hi, zz], r.ss.at[ss], rb.at[k], to_core)

        loop(0, nz, go)

    def rs_second(buf, got, ss, rc):
        gd = x_hi * 2 + 1 - core
        send(buf.at[pl.ds(gd * nz, nz)], got.at[x_hi], r.ss.at[ss], rc, to_core)

    def rs_middle(buf, got, out, gotx, ss, rb, rx):
        (outq, outs), (gotq, gots) = out, gotx

        def go(i):
            k = near(nz - 1 - i)
            zz = zplus(k)
            drain(got.at[1 - x_hi, zz], rb.at[k])
            outq[zz], outs[zz] = coded(buf[gx * nz + zz] + got[1 - x_hi, zz], outs.shape[1])
            send(outs.at[zz], gots.at[zz], r.ss.at[ss + 2], r.rxs.at[rx, k], to_x)
            send(outq.at[zz], gotq.at[zz], r.ss.at[ss + 1], r.rx.at[rx, k], to_x)

        loop(0, nz, go)

    def rs_finish(buf, got, gotx, outz, gotz, own, ss, rs, rc, rx):
        drain(got.at[x_hi], rc)
        (gotq, gots), (outq, outs), (zq, zs) = gotx, outz, gotz

        def block(k, zz):
            drain(gots.at[zz], r.rxs.at[rx, k])
            drain(gotq.at[zz], r.rx.at[rx, k])
            return buf[g * nz + zz] + got[x_hi, zz] + decoded(gotq[zz], gots[zz])

        def go(i):
            k = near(nz - 1 - i)
            zz = zplus(k)
            outq[zz], outs[zz] = coded(block(k, zz), outs.shape[1])
            to = (zz * GRP + g, mp)
            send(outs.at[zz], zs.at[z], r.ss.at[ss + 4], r.rs.at[rs + 1], to)
            send(outq.at[zz], zq.at[z], r.ss.at[ss + 3], r.rs.at[rs], to)

        loop(0, nz - 1, go)
        own[...] = block(0, z)
        zq[pl.ds(z, 1)] = jnp.zeros((1, *zq.shape[1:]), jnp.int16)
        zs[pl.ds(z, 1)] = jnp.zeros((1, *zs.shape[1:]), F32)

    def rs_result(gotz, own, rs):
        zq, zs = gotz
        drain(zs.at[pl.ds(0, nz - 1)], r.rs.at[rs + 1])
        drain(zq.at[pl.ds(0, nz - 1)], r.rs.at[rs])
        total = own[...]
        for i in range(nz):
            total = total + decoded(zq[i], zs[i])
        return total

    def rs_sent(buf, out, outz, ss):
        drain(buf.at[pl.ds(0, 2 * nz)], r.ss.at[ss])
        drain(out[0], r.ss.at[ss + 1])
        drain(out[1], r.ss.at[ss + 2])
        drain(outz[0].at[pl.ds(0, nz - 1)], r.ss.at[ss + 3])
        drain(outz[1].at[pl.ds(0, nz - 1)], r.ss.at[ss + 4])

    def pair(name):
        return getattr(r, name), getattr(r, name + "_s")

    ig = r.ig[...] * scale
    hi = ig.astype(BF16)
    lo = (ig - hi.astype(F32)).astype(BF16)
    part = ns // GRP

    def expand(gd):
        pick = r.pick_t[pl.ds(pl.multiple_of(gd * part, part), part), :]
        r.es[pl.ds(gd * nz, nz)] = (dot(pick, hi, 1, 0) + dot(pick, lo, 1, 0)).reshape(nz, sm, out_w)

    expand((1 - x_hi) * 2 + 1 - core)
    rs_first(r.es, r.er, 10, r.rb.at[0])
    expand(gx)
    expand(x_hi * 2 + 1 - core)
    rs_second(r.es, r.er, 10, r.rc.at[0])
    rs_middle(r.es, r.er, pair("ey"), pair("ex2"), 10, r.rb.at[0], 1)
    expand(g)

    def query(t):
        qg = dot(r.items_t[...], r.pg[t], 1, 0) * scale
        for j in range(QT // qb):
            b = t * (QT // qb) + j
            yd, xd = lax.rem(b, NY), lax.div(b, NY)
            r.hs[yd, xd], r.hs_s[yd, xd] = coded(qg[:, j * qb : (j + 1) * qb], 1)

    loop(0, nq // QT, query)
    r.hr[pl.ds(y, 1)] = r.hs[pl.ds(y, 1)]
    r.hr_s[pl.ds(y, 1)] = r.hs_s[pl.ds(y, 1)]
    for j in range(1, NY):
        yd = lax.rem(y + j, NY)
        to = (dp, x_lo * NY + yd)
        send(r.hs_s.at[yd], r.hr_s.at[y], r.ss.at[15], r.rs.at[10], to)
        send(r.hs.at[yd], r.hr.at[y], r.ss.at[16], r.rs.at[11], to)
    rs_finish(
        r.es, r.er, pair("ex2"), pair("ez"), pair("ezr"), r.e_own, 10, 8, r.rc.at[0], 1
    )

    r.igm[pl.ds(mp, 1)] = rs_result(pair("ezr"), r.e_own, 8).astype(BF16)[None]
    for md in columns:
        send(r.igm.at[mp], r.igm.at[mp], r.ss.at[19], r.rs.at[14], (dp, md))

    drain(r.hr_s.at[pl.ds(0, NY - 1)], r.rs.at[10])
    drain(r.hr.at[pl.ds(0, NY - 1)], r.rs.at[11])
    for j in range(2):
        xd = lax.rem(x_lo + 1 + j, 2)
        q_sum = decoded(r.hr[0, xd], r.hr_s[0, xd])
        for i in range(1, NY):
            q_sum = q_sum + decoded(r.hr[i, xd], r.hr_s[i, xd])
        if j == 0:
            r.h2[...], r.h2_s[...] = coded(q_sum, 1)
            to = (dp, (1 - x_lo) * NY + y)
            send(r.h2_s, r.h3_s, r.ss.at[17], r.rs.at[12], to)
            send(r.h2, r.h3, r.ss.at[18], r.rs.at[13], to)
        else:
            r.h_own[...] = q_sum

    drain(r.igm.at[pl.ds(0, n_mp - 1)], r.rs.at[14])

    item_grad = r.igm[...].reshape(slots, out_w)
    back = dot(item_grad, r.w_out[...], 1, 1)
    pre_grad = jnp.where(r.pre[...] > 0.0, back, 0.0)
    pre_bf = pre_grad.astype(BF16)
    gwi = dot(r.emb[...], pre_bf, 0, 0)
    gwo = dot(r.hid[...], item_grad, 0, 0)
    gb = jnp.sum(pre_bf.astype(F32), axis=0, keepdims=True)
    hid_w = gb.shape[1]
    nb = emb_w // n_dp
    r.ga[:, 0:nb, :] = gwi.reshape(n_dp, nb, hid_w)
    r.ga[:, nb : nb + 8, :] = jnp.zeros((n_dp, 8, hid_w), F32)
    half = hid_w // 8
    r.ga[0:half, nb : nb + 8, :] = gwo[:, 0:128].reshape(half, 8, 128)
    r.ga[half : 2 * half, nb : nb + 8, :] = gwo[:, 128:256].reshape(half, 8, 128)
    r.ga[2 * half, nb : nb + 1, :] = gb
    rs_first(r.ga, r.gr, 20, r.rb.at[1])
    rs_second(r.ga, r.gr, 20, r.rc.at[1])
    emb_p = dot(pre_bf, r.w_in[...], 1, 1)
    for j in range(n_mp):
        r.ks[j] = emb_p[j * sm : (j + 1) * sm]
    r.kr[pl.ds(mp, 1)] = r.ks[pl.ds(mp, 1)]
    rs_middle(r.ga, r.gr, pair("gy"), pair("gx2"), 20, r.rb.at[1], 2)
    for md in columns:
        send(r.ks.at[md], r.kr.at[mp], r.ss.at[25], r.rs.at[15], (dp, md))
    rs_finish(
        r.ga, r.gr, pair("gx2"), pair("gz"), pair("gzr"), r.g_own, 20, 16, r.rc.at[1], 2
    )

    drain(r.kr.at[pl.ds(0, n_mp - 1)], r.rs.at[15])
    emb_own = r.kr[0]
    for j in range(1, n_mp):
        emb_own = emb_own + r.kr[j]
    r.eg[pl.ds(mp, 1)] = emb_own.astype(BF16)[None]
    for md in columns:
        send(r.eg.at[mp], r.eg.at[mp], r.ss.at[26], r.rs.at[18], (dp, md))

    r.gf[pl.ds(g * nz + z, 1)] = rs_result(pair("gzr"), r.g_own, 16).astype(BF16)[None]
    ag_start(r.gf, 27, r.rz.at[1])

    def out(name, src):
        copy = pltpu.make_async_copy(src, getattr(r, name), r.os.at[OUTS.index(name)])
        copy.start()
        return copy

    drain(r.spr.at[pl.ds(0, n_mp - 1)], r.rs.at[2])
    at_pos = r.spr[0]
    for j in range(1, n_mp):
        at_pos = at_pos + r.spr[j]
    r.loss[...] = r.loss[...] - at_pos
    done = [out("o_ht", r.ht), out("o_loss", r.loss)]
    drain(r.h3_s, r.rs.at[12])
    drain(r.h3, r.rs.at[13])
    r.qs[...] = (r.h_own[...] + decoded(r.h3[...], r.h3_s[...])).T
    done.append(out("o_q", r.qs))
    drain(r.eg.at[pl.ds(0, n_mp - 1)], r.rs.at[18])
    done.append(out("o_eg", r.eg))
    for copy in done:
        copy.wait()

    drain(r.r1s.at[pl.ds(0, n_dp - 1)], r.ss.at[0])
    drain(r.infoz.at[0, pl.ds(0, GRP - 1)], r.ss.at[1])
    drain(r.infoz.at[pl.ds(0, nz - 1)], r.ss.at[3])
    drain(r.bs.at[pl.ds(0, n_mp - 1)], r.ss.at[4])
    ag_sent(r.ag, 5)
    drain(r.sr.at[pl.ds(0, n_mp - 1)], r.ss.at[9])
    drain(r.spr.at[pl.ds(0, n_mp - 1)], r.ss.at[2])
    rs_sent(r.es, pair("ey"), pair("ez"), 10)
    drain(r.hs_s.at[pl.ds(0, NY - 1)], r.ss.at[15])
    drain(r.hs.at[pl.ds(0, NY - 1)], r.ss.at[16])
    drain(r.h2_s, r.ss.at[17])
    drain(r.h2, r.ss.at[18])
    drain(r.igm.at[pl.ds(0, n_mp - 1)], r.ss.at[19])
    rs_sent(r.ga, pair("gy"), pair("gz"), 20)
    drain(r.ks.at[pl.ds(0, n_mp - 1)], r.ss.at[25])
    drain(r.eg.at[pl.ds(0, n_mp - 1)], r.ss.at[26])

    ag_finish(r.gf, 27, 19, r.rz.at[1], r.rx.at[3], FAR_SUMS)
    last = out("o_gf", r.gf)
    ag_sent(r.gf, 27)
    last.wait()


def results_kernel(names, *refs):
    r = types.SimpleNamespace(**dict(zip(names, refs)))
    n_dp, gr, hid_w = r.gf.shape
    nb = gr - 8
    rows_dev, emb_w = r.v_table.shape
    slots = r.eg.shape[0] * r.eg.shape[1]
    half = hid_w // 8
    loads = [pltpu.make_async_copy(getattr(r, "i_" + n), getattr(r, n), r.ls.at[i]) for i, n in enumerate(MIDS)]
    for copy in loads:
        copy.start()
    stores = []

    def put(name, i, rows=slice(None)):
        copy = pltpu.make_async_copy(getattr(r, "v_" + name).at[rows], getattr(r, "g_" + name).at[rows], r.os.at[i])
        copy.start()
        stores.append(copy)

    loads[0].wait()
    loads[1].wait()
    eg = r.eg[...].reshape(slots, emb_w)
    step = rows_dev // TABLE_PARTS
    for i in range(TABLE_PARTS):
        rows = pl.ds(i * step, step)
        r.v_table[rows, :] = dot(r.ht[rows, 0:slots], eg, 1, 0)
        put("table", i, rows)
    loads[2].wait()
    gf = r.gf[...].astype(F32)
    r.v_wi[...] = gf[:, 0:nb, :].reshape(emb_w, hid_w)
    put("wi", TABLE_PARTS)
    r.v_wo[:, 0:128] = gf[0:half, nb : nb + 8, :].reshape(hid_w, 128)
    r.v_wo[:, 128:256] = gf[half : 2 * half, nb : nb + 8, :].reshape(hid_w, 128)
    put("wo", TABLE_PARTS + 1)
    r.v_b[...] = gf[2 * half, nb : nb + 1, :]
    put("b", TABLE_PARTS + 2)
    loads[3].wait()
    r.v_q[...] = r.q[...]
    put("q", TABLE_PARTS + 3)
    loads[4].wait()
    r.v_loss[...] = r.loss[...]
    put("loss", TABLE_PARTS + 4)
    for copy in stores:
        copy.wait()


def per_device(queries, item_table, cand_row, cand_owner, cand_count, positive, w_in, b_in, w_out):
    n_dp, n_mp = lax.axis_size("dp"), lax.axis_size("mp")
    nz = n_dp // GRP
    cl = cand_row.shape[0]
    nq, out_w = queries.shape
    rows_dev, emb_w = item_table.shape
    hid_w = w_in.shape[1]
    slots = 2 * n_dp
    sm = slots // n_mp
    srcs = n_dp // n_mp
    nc = srcs * cl
    ns = n_dp * sm
    qb = nq // n_mp
    nt = nq // QT
    gr = emb_w // n_dp + 8
    ins = dict(
        own=cand_owner.reshape(1, cl), row=cand_row[None, :], cnt=cand_count[None, :],
        pos=positive[None, :], b_in=b_in[None, :],
    )
    far = dict(table_in=item_table, w_in_in=w_in, w_out_in=w_out, q_in=queries)
    mids = dict(
        o_loss=((1, nq), F32), o_q=((qb, out_w), F32), o_gf=((n_dp, gr, hid_w), BF16),
        o_ht=((rows_dev, 128), BF16), o_eg=((n_mp, sm, emb_w), BF16),
    )
    outs = dict(
        g_loss=((1, nq), F32), g_q=((qb, out_w), F32), g_wi=((emb_w, hid_w), F32),
        g_b=((1, hid_w), F32), g_wo=((hid_w, out_w), F32), g_table=((rows_dev, emb_w), F32),
    )
    vmem = dict(
        q=((nq, out_w), BF16), table=((rows_dev, emb_w), BF16), w_in=((emb_w, hid_w), BF16),
        w_out=((hid_w, out_w), BF16), loss=((1, nq), F32), qs=((qb, out_w), F32),
        r1s=((n_dp, 1, 128), F32), i1=((1, 128), F32),
        infoz=((nz, GRP, 1, 128), F32), rq=((n_dp, 1, 128), F32),
        ht=((rows_dev, 128), BF16), emb=((slots, emb_w), BF16), pre=((slots, hid_w), F32),
        hid=((slots, hid_w), BF16), bs=((n_mp, sm, out_w), F32), br=((n_mp, sm, out_w), F32),
        ag=((n_dp, sm, out_w), BF16), t8=((8, 128), F32), pick=((nc, ns), BF16), pick_t=((ns, nc), BF16), c2=((srcs // 2, 1, 2 * cl), F32), logq=((nc, 1), F32),
        items=((nc, out_w), BF16), items_t=((out_w, nc), BF16), ex=((nt, nc, QT), F32),
        st=((2, 1, nq), F32), sr=((n_mp, 2, 1, nq), F32), sp=((1, 1, nq), F32), spr=((n_mp, 1, nq), F32), fac=((1, nq), F32),
        pg=((nt, nc, QT), BF16), ig=((nc, out_w), F32),
        es=((n_dp, sm, out_w), F32), er=((2, nz, sm, out_w), F32), e_own=((sm, out_w), F32),
        h_own=((out_w, qb), F32), igm=((n_mp, sm, out_w), BF16),
        ga=((n_dp, gr, hid_w), F32), gr=((2, nz, gr, hid_w), F32), g_own=((gr, hid_w), F32),
        gf=((n_dp, gr, hid_w), BF16),
        ks=((n_mp, sm, emb_w), F32), kr=((n_mp, sm, emb_w), F32), eg=((n_mp, sm, emb_w), BF16),
    )
    fixed = dict(
        ey=((nz,), (sm, out_w), 1), ex2=((nz,), (sm, out_w), 1), ez=((nz,), (sm, out_w), 1),
        ezr=((nz,), (sm, out_w), 1), gy=((nz,), (gr, hid_w), 2), gx2=((nz,), (gr, hid_w), 2),
        gz=((nz,), (gr, hid_w), 2), gzr=((nz,), (gr, hid_w), 2), hs=((NY, 2), (out_w, qb), 1),
        hr=((NY, 2), (out_w, qb), 1), h2=((), (out_w, qb), 1), h3=((), (out_w, qb), 1),
    )
    for name, (lead, block, tiles) in fixed.items():
        vmem[name] = ((*lead, *block), jnp.int16)
        vmem[name + "_s"] = ((*lead, tiles, 1, block[1]), F32)
    sems = dict(ss=(31,), rs=(21,), rz=(2, nz), rx=(4, nz), rxs=(4, nz), rc=(2,), rb=(2, nz), ls=(4,), os=(5,))
    names = (*ins, *far, *mids, *vmem, *sems)
    whole = pl.BlockSpec(memory_space=pltpu.VMEM)
    there = pl.BlockSpec(memory_space=pl.ANY)
    loss, qs, gf, ht, eg = pl.pallas_call(
        functools.partial(step_kernel, n_dp, n_mp, names),
        out_shape=[jax.ShapeDtypeStruct(*s) for s in mids.values()],
        in_specs=[whole] * len(ins) + [there] * len(far),
        out_specs=[there] * len(mids),
        scratch_shapes=[pltpu.VMEM(*s) for s in vmem.values()]
        + [pltpu.SemaphoreType.DMA(s) for s in sems.values()],
        compiler_params=pltpu.CompilerParams(
            collective_id=0, has_side_effects=True, vmem_limit_bytes=VMEM_BYTES
        ),
    )(*ins.values(), *far.values())
    middle = {n: mids["o_" + n] for n in MIDS}
    held = {"v" + n[1:]: v for n, v in outs.items()}
    names = (*("i_" + n for n in MIDS), *outs, *middle, *held, "ls", "os")
    loss, g_q, g_wi, g_b, g_wo, g_table = pl.pallas_call(
        functools.partial(results_kernel, names),
        out_shape=[jax.ShapeDtypeStruct(*s) for s in outs.values()],
        in_specs=[there] * 5,
        out_specs=[there] * len(outs),
        scratch_shapes=[pltpu.VMEM(*s) for s in (*middle.values(), *held.values())]
        + [pltpu.SemaphoreType.DMA((5,)), pltpu.SemaphoreType.DMA((TABLE_PARTS + 5,))],
        compiler_params=pltpu.CompilerParams(vmem_limit_bytes=VMEM_BYTES),
    )(eg, ht, gf, qs, loss)
    return loss.reshape(nq), g_q, g_wi, g_b.reshape(hid_w), g_wo, g_table


def solution(mesh):
    placed = (
        P("dp", None),
        P("dp", None),
        P("dp"),
        P("dp", None),
        P("dp"),
        P("dp"),
        P(None, "mp"),
        P("mp"),
        P("mp", None),
    )
    return jax.shard_map(
        per_device,
        mesh=mesh,
        in_specs=placed,
        out_specs=(
            P("dp"),
            P(("dp", "mp"), None),
            P(None, "mp"),
            P("mp"),
            P("mp", None),
            P("dp", None),
        ),
        check_vma=False,
    )
```
